32 devices in a mesh: shard: 2 (over y), ctx: 4 (over x, core), tp: 4 (over z).
Axes of the slice: x: 2, y: 2, z: 4, core: 2. Of those that a mesh axis runs over, the one named last changes fastest.
Arguments:
- video: bfloat16 [2, 16, 16, 16, 1152], P('shard', 'ctx', 'tp'), may hold values from -6 to 6
- cond: bfloat16 [2, 1152], P('shard'), may hold values from -6 to 6
- w_ada: bfloat16 [2, 1152, 6912], P(None, 'shard', 'tp'), may hold values from -0.1875 to 0.1875
- b_ada: bfloat16 [2, 6912], P(None, 'tp'), may hold values from 0.5 to 1.5
- w_qkv: bfloat16 [2, 3, 1152, 1152], P(None, None, 'shard', 'tp'), may hold values from -0.09375 to 0.09375
- b_qv: bfloat16 [2, 2, 1152], P(None, None, 'tp'), may hold values from -3 to 3
- w_out: bfloat16 [2, 1152, 1152], P(None, 'tp', 'shard'), may hold values from -0.75 to 0.75
- b_out: bfloat16 [2, 1152], replicated, may hold values from -3 to 3
- w_up: bfloat16 [2, 1152, 4608], P(None, 'shard', 'tp'), may hold values from -0.09375 to 0.09375
- b_up: bfloat16 [2, 4608], P(None, 'tp'), may hold values from -3 to 3
- w_down: bfloat16 [2, 4608, 1152], P(None, 'tp', 'shard'), may hold values from -0.09375 to 0.09375
- b_down: bfloat16 [2, 1152], replicated, may hold values from -3 to 3
- cotangent: bfloat16 [2, 16, 16, 16, 1152], P('shard', None, 'tp', 'ctx'), may hold values from -6 to 6
Outputs:
- out: bfloat16 [2, 16, 16, 16, 1152], P('shard', None, 'tp', 'ctx')
- grad_video: float32 [2, 16, 16, 16, 1152], P('shard', 'ctx', 'tp')
- grad_cond: float32 [2, 1152], P('shard')
- grad_w_ada: float32 [2, 1152, 6912], P(None, 'shard', 'tp')
- grad_b_ada: float32 [2, 6912], P(None, 'tp')
- grad_w_qkv: float32 [2, 3, 1152, 1152], P(None, None, 'shard', 'tp')
- grad_b_qv: float32 [2, 2, 1152], P(None, None, 'tp')
- grad_w_out: float32 [2, 1152, 1152], P(None, 'tp', 'shard')
- grad_b_out: float32 [2, 1152], replicated
- grad_w_up: float32 [2, 1152, 4608], P(None, 'shard', 'tp')
- grad_b_up: float32 [2, 4608], P(None, 'tp')
- grad_w_down: float32 [2, 4608, 1152], P(None, 'tp', 'shard')
- grad_b_down: float32 [2, 1152], replicated
The draws below stay inside these ranges and needn't reach their ends.
All inputs are finite; a program needn't handle non-finite values.
Results may differ from the reference program's by a relative error of at most 0.025.
Values may be sent and summed in bfloat16 or wider, within the bound.
No kernel may reach another device: no remote copies, remote signals or barrier semaphores. Data moves between devices by JAX's collectives and lax.ppermute only.
A program may use at most 256 MiB of HBM per device.

```python
import math
import jax
import jax.numpy as jnp
from jax import lax

D = 1152
HEADS = 16
HEAD_DIM = 72
FF = 4608
FRAMES = 16
HP = 16
WP = 16
CLIPS = 2


def strengthened(values, stream_key, source, target, parts, factor):
    owner, partner = [(jnp.arange(values.shape[dim]) // (values.shape[dim] // parts)).reshape([-1 if axis == dim else 1 for axis in range(values.ndim)]) for dim in (source, target)]
    chosen = jax.random.permutation(stream_key, parts)[partner]
    strong = (owner == chosen) | (owner == (partner + parts // 2) % parts)
    return jnp.where(strong, factor * values, values)


def steps_of(own_key, shape, cuts, least, high):
    factor_of, own = 1.0, jax.random.fold_in(own_key, 6)
    for position, blocks in cuts:
        steps = jnp.exp(jax.random.uniform(jax.random.fold_in(own, position), (blocks,), jnp.float32, least / len(cuts), high / len(cuts)))
        factor_of = factor_of * jnp.repeat(steps, shape[position] // blocks).reshape([-1 if axis == position else 1 for axis in range(len(shape))])
    return factor_of


def normal_values(rng, shape, scale, reach, cuts=(), kind=jnp.bfloat16):
    level = steps_of(rng, shape, cuts, -0.22, 0.18) if cuts else 1.0
    values = jax.random.normal(rng, shape, jnp.float32) * scale * level
    return jnp.minimum(jnp.maximum(values, -reach), reach).astype(kind)


def gaussian_with(own_key, extent, scale, limit, shards, heavy, held_as=jnp.bfloat16):
    drawn = scale * jax.random.normal(own_key, extent, jnp.float32)
    if shards:
        drawn = drawn * steps_of(own_key, extent, shards, -0.22, 0.18)
    return jnp.clip(strengthened(drawn, jax.random.fold_in(own_key, 3), *heavy), -limit, limit).astype(held_as)


def setup_inputs(seed: int = 0) -> dict:
    streams_of = jax.random.split(jax.random.key(seed), 14)
    video = normal_values(streams_of[0], (CLIPS, FRAMES, HP, WP, D), 1.0, 6.0, ((0, 2), (1, 4), (2, 4)))
    cond = normal_values(streams_of[1], (CLIPS, D), 1.0, 6.0, ((0, 2),))
    w_ada = normal_values(streams_of[2], (2, D, 6 * D), D ** -0.5, 0.1875, ((1, 2), (2, 4)))
    b_ada = jnp.clip(1.0 + 0.1 * jax.random.normal(streams_of[3], (2, 6 * D), jnp.float32), 0.5, 1.5).astype(jnp.bfloat16)
    w_qkv = normal_values(streams_of[4], (2, 3, D, D), (4 * D) ** -0.5, 0.09375, ((2, 2), (3, 4)))
    b_qv = normal_values(streams_of[5], (2, 2, D), 0.5, 3.0, ((2, 4),))
    w_out = normal_values(streams_of[6], (2, D, D), (D // 16) ** -0.5, 0.75, ((1, 4), (2, 2)))
    b_out = normal_values(streams_of[7], (2, D), 0.5, 3.0)
    w_up = normal_values(streams_of[8], (2, D, FF), (4 * D) ** -0.5, 0.09375, ((1, 2), (2, 4)))
    b_up = normal_values(streams_of[9], (2, FF), 0.5, 3.0, ((1, 4),))
    w_down = normal_values(streams_of[10], (2, FF, D), FF ** -0.5, 0.09375, ((1, 4), (2, 2)))
    b_down = normal_values(streams_of[11], (2, D), 0.5, 3.0)
    cotangent = gaussian_with(streams_of[12], (CLIPS, FRAMES, HP, WP, D), 1.0, 6.0, ((0, 2), (2, 4), (3, 4)), (0, 4, 2, 2.0))
    return {"video": video, "cond": cond, "w_ada": w_ada, "b_ada": b_ada, "w_qkv": w_qkv, "b_qv": b_qv, "w_out": w_out, "b_out": b_out, "w_up": w_up, "b_up": b_up, "w_down": w_down, "b_down": b_down, "cotangent": cotangent}


@jax.custom_vjp
def low(v):
    return lax.optimization_barrier(v.astype(jnp.bfloat16)).astype(jnp.float32)

@jax.custom_vjp
def low_back(v):
    return v

def low_keep(v):
    return (low(v), None)

def low_pass(kept, grad):
    return (grad,)

def back_keep(v):
    return (v, None)

def back_low(kept, grad):
    return (low(grad),)
low.defvjp(low_keep, low_pass)
low_back.defvjp(back_keep, back_low)
highest = lax.Precision.HIGHEST

def rounded(value):
    return low_back(low(value))

def matmul(left, right):
    return jnp.dot(left, right, precision=highest, preferred_element_type=jnp.float32)

def layer_norm(values):
    average = lax.optimization_barrier(jnp.mean(values, axis=-1, keepdims=True))
    centered = values - average
    spread = lax.optimization_barrier(jnp.mean(centered * centered, axis=-1, keepdims=True))
    return centered * lax.rsqrt(spread + 1e-06)

def attend_group(query_seq, key_seq, value_seq):
    factor = 1.0 / math.sqrt(HEAD_DIM)
    scores = low_back(jnp.einsum('gqhe,gkhe->ghqk', query_seq, key_seq, precision=highest) * factor)
    weights = low(jax.nn.softmax(scores, axis=-1))
    return jnp.einsum('ghqk,gkhe->gqhe', weights, value_seq, precision=highest)

def attention(query_seq, key_seq, value_seq):
    batch = query_seq.shape[0]
    length = query_seq.shape[1]
    group = math.gcd(batch, max(1, 4096 // length))
    shape = (batch // group, group) + query_seq.shape[1:]
    blocked = jax.checkpoint(attend_group)
    result = lax.map(lambda triple: blocked(triple[0], triple[1], triple[2]), (query_seq.reshape(shape), key_seq.reshape(shape), value_seq.reshape(shape)))
    return result.reshape(query_seq.shape)

def to_sequences(rows, grid, temporal):
    heads = rows.reshape(grid + (HEADS, HEAD_DIM))
    if temporal:
        heads = jnp.transpose(heads, (0, 2, 3, 1, 4, 5))
        return heads.reshape(grid[0] * grid[2] * grid[3], grid[1], HEADS, HEAD_DIM)
    return heads.reshape(grid[0] * grid[1], grid[2] * grid[3], HEADS, HEAD_DIM)

def from_sequences(heads, grid, temporal):
    if temporal:
        heads = heads.reshape(grid[0], grid[2], grid[3], grid[1], HEADS, HEAD_DIM)
        heads = jnp.transpose(heads, (0, 3, 1, 2, 4, 5))
    return heads.reshape(-1, HEADS * HEAD_DIM)

def block(inputs, cond_act, w_ada, b_ada, w_qkv, b_qv, w_out, b_out, w_up, b_up, w_down, b_down, temporal):
    grid = inputs.shape[:4]
    modulation = matmul(cond_act, w_ada) + b_ada
    pieces = modulation.reshape(grid[0], 6, 1, 1, 1, D)
    shift_a, scale_a, gate_a, shift_m, scale_m, gate_m = [pieces[:, number] for number in range(6)]
    hidden = low(layer_norm(inputs) * (1.0 + scale_a) + shift_a).reshape(-1, D)
    query_rows = rounded(matmul(hidden, w_qkv[0]) + b_qv[0])
    key_rows = rounded(matmul(hidden, w_qkv[1]))
    value_rows = rounded(matmul(hidden, w_qkv[2]) + b_qv[1])
    attended = attention(to_sequences(query_rows, grid, temporal), to_sequences(key_rows, grid, temporal), to_sequences(value_rows, grid, temporal))
    attended = rounded(from_sequences(attended, grid, temporal))
    attn_out = low_back(matmul(attended, w_out) + b_out).reshape(inputs.shape)
    after_attn = inputs + gate_a * attn_out
    hidden_two = low(layer_norm(after_attn) * (1.0 + scale_m) + shift_m).reshape(-1, D)
    up_rows = low_back(matmul(hidden_two, w_up) + b_up)
    activated = low(jax.nn.gelu(up_rows, approximate=True))
    mlp_out = low_back(matmul(activated, w_down) + b_down).reshape(inputs.shape)
    return after_attn + gate_m * mlp_out

def reference(video, cond, w_ada, b_ada, w_qkv, b_qv, w_out, b_out, w_up, b_up, w_down, b_down, cotangent):
    params = tuple((array.astype(jnp.float32) for array in (w_ada, b_ada, w_qkv, b_qv, w_out, b_out, w_up, b_up, w_down, b_down)))

    def forward(video_f, cond_f, weights):
        cond_act = low(jax.nn.silu(cond_f))
        first = [weight[0] for weight in weights]
        second = [weight[1] for weight in weights]
        middle = rounded(block(video_f, cond_act, first[0], first[1], first[2], first[3], first[4], first[5], first[6], first[7], first[8], first[9], False))
        return block(middle, cond_act, second[0], second[1], second[2], second[3], second[4], second[5], second[6], second[7], second[8], second[9], True)
    result, pullback = jax.vjp(forward, video.astype(jnp.float32), cond.astype(jnp.float32), params)
    grad_video, grad_cond, grads = pullback(cotangent.astype(jnp.float32))
    return (result.astype(jnp.bfloat16), grad_video, grad_cond, grads[0], grads[1], grads[2], grads[3], grads[4], grads[5], grads[6], grads[7], grads[8], grads[9])
```

```python
from functools import partial
import math

import jax
import jax.numpy as jnp
from jax import lax
from jax.experimental import pallas as pl
from jax.experimental.pallas import tpu as pltpu
from jax.sharding import PartitionSpec as P

HEAD_DIM = 72
bf16 = jnp.bfloat16
f32 = jnp.float32
highest = lax.Precision.HIGHEST


class Place:
    def __init__(self):
        self.ns = lax.axis_size("shard")
        self.nc = lax.axis_size("ctx")
        self.nt = lax.axis_size("tp")
        self.s = lax.axis_index("shard")
        self.c = lax.axis_index("ctx")
        self.t = lax.axis_index("tp")
        self.x = self.c // 2
        self.k = self.c % 2
        self.d = jnp.where(self.k == 0, self.t, self.nt - 1 - self.t)
        self.valid = self.d < 2
        self.first = jnp.where(self.k == 0, 0, self.nt - 1)
        self.second = jnp.where(self.k == 0, 1, self.nt - 2)

    def core(self, v):
        return lax.ppermute(v, "ctx", [(c, c ^ 1) for c in range(self.nc)])

    def swap_x(self, v):
        return lax.ppermute(v, "ctx", [(c, c ^ 2) for c in range(self.nc)])

    def swap_y(self, v):
        return lax.ppermute(v, "shard", [(i, i ^ 1) for i in range(self.ns)])

    def along_z(self, v, pairs):
        def at(c, d):
            return c * self.nt + (d if c % 2 == 0 else self.nt - 1 - d)

        return lax.ppermute(
            v, ("ctx", "tp"), [(at(c, i), at(c, j)) for c in range(self.nc) for i, j in pairs]
        )

    def valid_pairs(self, flip):
        return [
            (c * self.nt + t, (c ^ flip) * self.nt + t)
            for c in range(self.nc)
            for t in range(self.nt)
            if (t if c % 2 == 0 else self.nt - 1 - t) < 2
        ]


def pick(index, options):
    out = options[-1]
    for number in range(len(options) - 2, -1, -1):
        out = jnp.where(index == number, options[number], out)
    return out


def gather_weight(at, own):
    r1 = at.along_z(own, [(0, 1), (1, 2)])
    r2 = at.along_z(own, [(1, 0)])
    r3 = at.along_z(r1, [(1, 2), (2, 3)])
    r4 = at.along_z(r3, [(2, 3)])
    both = jnp.stack([pick(at.d, [own, r1, r3, r4]), pick(at.d, [r2, own, r1, r3])])
    rows = own.shape[0]
    if at.ns != 2:
        return lax.all_gather(both, "shard", axis=1, tiled=True)
    half = rows // 2
    mine = lax.dynamic_slice_in_dim(both, at.x * half, half, axis=1)
    near = at.swap_y(mine)
    far = at.swap_x(near)
    upper = jnp.where(at.x == 0, near, far)
    lower = jnp.where(at.x == 0, far, near)
    other = jnp.concatenate([upper, lower], axis=1)
    return jnp.where(
        at.s == 0,
        jnp.concatenate([both, other], axis=1),
        jnp.concatenate([other, both], axis=1),
    )


def reduce_z(at, blocks):
    m = lax.dynamic_index_in_dim(blocks, jnp.where((at.d == 1) | (at.d == 2), 0, 1), 0, False)
    n = lax.dynamic_index_in_dim(blocks, jnp.where(at.d == 3, 0, 1), 0, False)
    keep = lax.dynamic_index_in_dim(blocks, jnp.where(at.d == 0, 0, 1), 0, False)
    r1 = at.along_z(m, [(1, 0), (0, 1)])
    r2 = at.along_z(m, [(2, 0), (3, 1)])
    r3 = at.along_z(n, [(3, 0), (2, 1)])
    return (keep.astype(f32) + r1.astype(f32)) + (r2.astype(f32) + r3.astype(f32))


def product(left, right):
    return sum(
        jnp.einsum("rd,prn->pdn", l, r, preferred_element_type=f32) for l, r in zip(left, right)
    )


def sum_yzx(at, left, right):
    width = left[0].shape[1]
    rows = width // at.ns
    if at.ns == 2:
        parts = [jnp.where(at.s == 0, l[:, :rows], l[:, rows:]) for l in left]
        others = [jnp.where(at.s == 0, l[:, rows:], l[:, :rows]) for l in left]
        received = at.swap_y(product(others, right).astype(bf16))
        summed = (product(parts, right) + received.astype(f32)).astype(bf16)
    else:
        summed = lax.psum_scatter(
            product(left, right).astype(bf16), "shard", scatter_dimension=1, tiled=True
        )
    final = reduce_z(at, summed).astype(bf16)
    half = rows // 2
    mine = jnp.where(at.valid, final[:half], at.core(final[half:]))
    mine = (mine.astype(f32) + at.swap_x(mine).astype(f32)).astype(bf16)
    theirs = at.core(mine)
    return jnp.concatenate(
        [jnp.where(at.valid, mine, theirs), jnp.where(at.valid, theirs, mine)], axis=0
    ).astype(f32)


def sum_xyz(at, left, right):
    if at.ns != 2:
        return sum_yzx(at, left, right)
    width = left[0].shape[1]
    quarter = width // 4
    cut = [[l[:, i * quarter : (i + 1) * quarter] for i in range(4)] for l in left]

    def term(ds, dx):
        index = 2 * (at.s ^ ds) + (at.x ^ dx)
        return product([pick(index, pieces) for pieces in cut], right)

    sent = jnp.stack([term(1, 1).astype(bf16), term(0, 1).astype(bf16)])
    got = at.swap_x(sent)
    away = (term(1, 0) + got[0].astype(f32)).astype(bf16)
    back = at.swap_y(away)
    summed = (term(0, 0) + got[1].astype(f32) + back.astype(f32)).astype(bf16)
    final = reduce_z(at, summed).astype(bf16)
    far = lax.ppermute(final, ("ctx", "tp"), at.valid_pairs(2))
    both = jnp.stack([final, far])
    both = jnp.where(at.valid, both, lax.ppermute(both, ("ctx", "tp"), at.valid_pairs(1)))
    return jnp.concatenate(
        [jnp.where(at.x == 0, both[0], both[1]), jnp.where(at.x == 0, both[1], both[0])], axis=0
    ).astype(f32)


def heads_of(values, number, head):
    start = number * 4 * HEAD_DIM + head * HEAD_DIM
    return values[:, start : start + HEAD_DIM]


def probs_of(query, key, temporal):
    scores = lax.dot_general(
        query, key, (((1,), (1,)), ((), ())), preferred_element_type=f32
    ) * (1.0 / math.sqrt(HEAD_DIM))
    if temporal:
        rows = lax.broadcasted_iota(jnp.int32, scores.shape, 0) % temporal
        cols = lax.broadcasted_iota(jnp.int32, scores.shape, 1) % temporal
        scores = jnp.where(rows == cols, scores, -jnp.inf)
    weights = jnp.exp(scores - jnp.max(scores, axis=-1, keepdims=True))
    return weights / jnp.sum(weights, axis=-1, keepdims=True)


def attend_kernel(qkv_ref, out_ref, *, temporal):
    values = qkv_ref[0]
    results = [jnp.zeros((values.shape[0], 12 * HEAD_DIM), bf16)]
    for head in range(4):
        probs = probs_of(heads_of(values, 0, head), heads_of(values, 1, head), temporal)
        results.append(
            jnp.dot(
                probs.astype(bf16), heads_of(values, 2, head), preferred_element_type=f32
            ).astype(bf16)
        )
    out_ref[0] = jnp.concatenate(results, axis=1)


def attend_back_kernel(qkv_ref, grad_ref, out_ref, *, temporal):
    factor = 1.0 / math.sqrt(HEAD_DIM)
    values = qkv_ref[0]
    grads = grad_ref[0]
    queries, keys, vals = [], [], []
    for head in range(4):
        query, key, value = (heads_of(values, number, head) for number in range(3))
        grad = heads_of(grads, 3, head)
        probs = probs_of(query, key, temporal)
        vals.append(
            lax.dot_general(
                probs.astype(bf16), grad, (((0,), (0,)), ((), ())), preferred_element_type=f32
            ).astype(bf16)
        )
        grad_probs = lax.dot_general(
            grad, value, (((1,), (1,)), ((), ())), preferred_element_type=f32
        )
        inner = jnp.sum(grad_probs * probs, axis=-1, keepdims=True)
        grad_scores = (probs * (grad_probs - inner)).astype(bf16)
        queries.append(
            (jnp.dot(grad_scores, key, preferred_element_type=f32) * factor).astype(bf16)
        )
        keys.append(
            (
                lax.dot_general(
                    grad_scores, query, (((0,), (0,)), ((), ())), preferred_element_type=f32
                )
                * factor
            ).astype(bf16)
        )
    zeros = jnp.zeros((values.shape[0], 4 * HEAD_DIM), bf16)
    out_ref[0] = jnp.concatenate(queries + keys + vals + [zeros], axis=1)


def call_attention(kernel, arrays, rows, temporal):
    shape = arrays[0].shape
    spec = pl.BlockSpec((1, rows, shape[2]), lambda i, j: (i, j, 0))
    return pl.pallas_call(
        partial(kernel, temporal=temporal),
        out_shape=jax.ShapeDtypeStruct(shape, bf16),
        grid=(shape[0], shape[1] // rows),
        in_specs=[spec] * len(arrays),
        out_specs=spec,
        compiler_params=pltpu.CompilerParams(vmem_limit_bytes=48 * 1024 * 1024),
    )(*arrays)


def normalized(values):
    average = jnp.mean(values, axis=-1, keepdims=True)
    centered = values - average
    inverse = lax.rsqrt(jnp.mean(centered * centered, axis=-1, keepdims=True) + 1e-06)
    return centered * inverse, inverse


def norm_back(grad, normal, inverse, factor):
    dn = grad * (1.0 + factor)
    return (
        dn
        - jnp.mean(dn, axis=-1, keepdims=True)
        - normal * jnp.mean(dn * normal, axis=-1, keepdims=True)
    ) * inverse


def pair_rows(at, values):
    return jnp.concatenate([values, at.core(values)], axis=0)


def pair_sum(at, partial_rows):
    rows = partial_rows.shape[0] // 2
    return partial_rows[:rows] + at.core(partial_rows[rows:].astype(bf16)).astype(f32)


def times(left, weight):
    return jnp.einsum("rd,pdn->prn", left, weight, preferred_element_type=f32)


def times_back(left, weight):
    return jnp.einsum("prn,pdn->rd", left, weight, preferred_element_type=f32)


def forward_block(at, inputs, mod, weights, bias_qkv, bias_up, b_out, b_down, temporal):
    w_attn, w_up, w_down = weights
    shift_a, scale_a, gate_a, shift_m, scale_m, gate_m = mod
    rows = inputs.shape[0]
    hidden = (normalized(inputs)[0] * (1.0 + scale_a) + shift_a).astype(bf16)
    hidden = pair_rows(at, hidden)
    qkv = (times(hidden, w_attn) + bias_qkv[:, None, :]).astype(bf16)
    attended = call_attention(attend_kernel, [qkv], rows, temporal)
    attn_out = pair_sum(at, times_back(attended, w_attn)) + b_out
    after = inputs + gate_a * attn_out
    hidden_two = (normalized(after)[0] * (1.0 + scale_m) + shift_m).astype(bf16)
    hidden_two = pair_rows(at, hidden_two)
    up = times(hidden_two, w_up) + bias_up[:, None, :]
    activated = jax.nn.gelu(up, approximate=True).astype(bf16)
    mlp_out = pair_sum(at, times_back(activated, w_down)) + b_down
    result = after + gate_m * mlp_out
    return result, (inputs, hidden, qkv, attended, attn_out, after, hidden_two, up, mlp_out)


def backward_block(at, grad_y, kept, mod, weights, temporal, orders):
    inputs, hidden, qkv, attended, attn_out, after, hidden_two, up, mlp_out = kept
    w_attn, w_up, w_down = weights
    shift_a, scale_a, gate_a, shift_m, scale_m, gate_m = mod
    rows = inputs.shape[0]
    grad_mlp = (gate_m * grad_y).astype(bf16)
    grad_gate_m = jnp.sum(grad_y * mlp_out, axis=0)
    grad_b_down = jnp.sum(grad_mlp, axis=0, dtype=f32)
    grad_mlp = pair_rows(at, grad_mlp)
    activated, gelu_back = jax.vjp(partial(jax.nn.gelu, approximate=True), up)
    activated = activated.astype(bf16)
    grad_up = gelu_back(times(grad_mlp, w_down))[0].astype(bf16)
    sum_down = orders[0](at, [grad_mlp], [activated])
    grad_b_up = jnp.sum(grad_up, axis=1, dtype=f32)
    grad_hidden_two = pair_sum(at, times_back(grad_up, w_up))
    sum_up = orders[1](at, [hidden_two], [grad_up])
    normal, inverse = normalized(after)
    grad_shift_m = jnp.sum(grad_hidden_two, axis=0)
    grad_scale_m = jnp.sum(grad_hidden_two * normal, axis=0)
    grad_after = grad_y + norm_back(grad_hidden_two, normal, inverse, scale_m)
    grad_attn = (gate_a * grad_after).astype(bf16)
    grad_gate_a = jnp.sum(grad_after * attn_out, axis=0)
    grad_b_out = jnp.sum(grad_attn, axis=0, dtype=f32)
    grad_attn = pair_rows(at, grad_attn)
    grad_attended = times(grad_attn, w_attn).astype(bf16)
    grad_qkv = call_attention(attend_back_kernel, [qkv, grad_attended], rows, temporal)
    grad_b_qkv = jnp.sum(grad_qkv, axis=1, dtype=f32)
    grad_hidden = pair_sum(at, times_back(grad_qkv, w_attn))
    sum_attn = orders[2](at, [hidden, grad_attn], [grad_qkv, attended])
    normal, inverse = normalized(inputs)
    grad_shift_a = jnp.sum(grad_hidden, axis=0)
    grad_scale_a = jnp.sum(grad_hidden * normal, axis=0)
    grad_inputs = grad_after + norm_back(grad_hidden, normal, inverse, scale_a)
    grad_mod = jnp.concatenate(
        [grad_shift_a, grad_scale_a, grad_gate_a, grad_shift_m, grad_scale_m, grad_gate_m]
    )
    width = grad_b_qkv.shape[1] // 4
    grad_bias = jnp.concatenate(
        [grad_b_qkv[:, :width], grad_b_qkv[:, 2 * width : 3 * width], grad_b_up], axis=1
    )
    blocks = jnp.arange(at.nt)[:, None]
    grad_bias = jnp.where(blocks == at.first, grad_bias[0:1], 0.0) + jnp.where(
        blocks == at.second, grad_bias[1:2], 0.0
    )
    clips = jnp.arange(at.ns)[:, None]
    grad_mods = jnp.where(clips == at.s, grad_mod[None], 0.0)
    sums = lax.psum(
        jnp.concatenate([grad_bias.reshape(-1), grad_b_out, grad_b_down, grad_mods.reshape(-1)]),
        ("shard", "ctx", "tp"),
    )
    size = grad_bias.size
    d = grad_b_out.size
    small = (
        lax.dynamic_index_in_dim(sums[:size].reshape(grad_bias.shape), at.t, 0, False),
        sums[size : size + d],
        sums[size + d : size + 2 * d],
        sums[size + 2 * d :].reshape(grad_mods.shape),
    )
    return grad_inputs, (sum_attn, sum_up, sum_down), small


def body(
    video, cond, w_ada, b_ada, w_qkv, b_qv, w_out, b_out, w_up, b_up, w_down, b_down, cotangent
):
    at = Place()
    width = video.shape[-1]
    own_width = w_up.shape[1]
    head_width = w_qkv.shape[3]
    silu_value, silu_back = jax.vjp(jax.nn.silu, cond.astype(f32))
    cond_act = silu_value.astype(bf16)
    cond_all = lax.all_gather(cond_act, "shard", axis=0, tiled=True)
    cond_rows = lax.dynamic_slice_in_dim(cond_all, at.s * own_width, own_width, axis=1)
    mod_part = jnp.einsum("cd,bdn->cbn", cond_rows, w_ada, preferred_element_type=f32)
    mod_part = lax.psum_scatter(mod_part, "shard", scatter_dimension=0, tiled=True)[0]
    mods = lax.all_gather(mod_part + b_ada, "tp", axis=1, tiled=True)
    mods = mods.reshape(2, 6, width)
    biases = jnp.concatenate([b_qv.reshape(2, -1), b_up], axis=1)
    biases = lax.all_gather(biases, "tp", axis=0, tiled=False)
    biases = jnp.stack(
        [
            lax.dynamic_index_in_dim(biases, at.first, 0, False),
            lax.dynamic_index_in_dim(biases, at.second, 0, False),
        ],
        axis=1,
    ).astype(f32)
    zeros = jnp.zeros((2, 2, head_width), f32)
    bias_qkv = jnp.concatenate(
        [biases[:, :, :head_width], zeros, biases[:, :, head_width : 2 * head_width], zeros], axis=2
    )
    bias_up = biases[:, :, 2 * head_width :]

    frames = lax.all_to_all(video, "tp", split_axis=1, concat_axis=2, tiled=True)
    rows = frames.size // width

    weights = []
    for b in range(2):
        attn = jnp.concatenate([w_qkv[b, 0], w_qkv[b, 1], w_qkv[b, 2], w_out[b].T], axis=1)
        weights.append(
            (gather_weight(at, attn), gather_weight(at, w_up[b]), gather_weight(at, w_down[b].T))
        )
    first, second = weights
    inputs = frames.reshape(rows, width).astype(f32)
    middle, kept_one = forward_block(
        at, inputs, mods[0], first, bias_qkv[0], bias_up[0], b_out[0], b_down[0], 0
    )
    moved = lax.all_to_all(
        middle.astype(bf16).reshape(frames.shape), "tp", split_axis=2, concat_axis=1, tiled=True
    )
    moved = lax.all_to_all(moved, "ctx", split_axis=3, concat_axis=1, tiled=True)
    grid = moved.shape
    patches = grid[2] * grid[3]
    result, kept_two = forward_block(
        at,
        moved.reshape(rows, width).astype(f32),
        mods[1],
        second,
        bias_qkv[1],
        bias_up[1],
        b_out[1],
        b_down[1],
        patches,
    )
    grad_moved, sums_two, small_two = backward_block(
        at,
        cotangent.reshape(rows, width).astype(f32),
        kept_two,
        mods[1],
        second,
        patches,
        (sum_yzx, sum_xyz, sum_yzx),
    )
    grad_middle = lax.all_to_all(
        grad_moved.astype(bf16).reshape(grid), "ctx", split_axis=1, concat_axis=3, tiled=True
    )
    grad_middle = lax.all_to_all(grad_middle, "tp", split_axis=1, concat_axis=2, tiled=True)
    grad_frames, sums_one, small_one = backward_block(
        at,
        grad_middle.reshape(rows, width).astype(f32),
        kept_one,
        mods[0],
        first,
        0,
        (sum_xyz, sum_yzx, sum_xyz),
    )
    grad_video = lax.all_to_all(
        grad_frames.astype(bf16).reshape(frames.shape), "tp", split_axis=2, concat_axis=1, tiled=True
    ).astype(f32)

    grad_bias, grad_b_out, grad_b_down, grad_mods = (
        jnp.stack([one, two]) for one, two in zip(small_one, small_two)
    )
    ada_cols = w_ada.shape[2]
    grad_mods = lax.dynamic_slice_in_dim(grad_mods, at.t * ada_cols, ada_cols, axis=2)
    cond_rows = cond_rows.astype(f32)
    grad_w_ada = sum(
        cond_rows[i][None, :, None] * grad_mods[:, i][:, None, :] for i in range(at.ns)
    )
    grad_b_ada = jnp.sum(grad_mods, axis=1)
    grad_act = jnp.einsum(
        "bcn,bdn->cd", grad_mods, w_ada.astype(f32), precision=highest, preferred_element_type=f32
    )
    grad_act = lax.dynamic_update_slice_in_dim(
        jnp.zeros((at.ns, width), f32), grad_act, at.s * own_width, axis=1
    )
    grad_act = lax.psum(grad_act, ("shard", "tp"))
    grad_cond = silu_back(lax.dynamic_slice_in_dim(grad_act, at.s, 1, axis=0))[0]

    attn = [sums[0].reshape(own_width, 4, head_width) for sums in (sums_one, sums_two)]
    return (
        result.astype(bf16).reshape(grid),
        grad_video,
        grad_cond,
        grad_w_ada,
        grad_b_ada,
        jnp.stack([jnp.transpose(a[:, :3], (1, 0, 2)) for a in attn]),
        grad_bias[:, : 2 * head_width].reshape(2, 2, head_width),
        jnp.stack([a[:, 3].T for a in attn]),
        grad_b_out,
        jnp.stack([sums_one[1], sums_two[1]]),
        grad_bias[:, 2 * head_width :],
        jnp.stack([sums_one[2].T, sums_two[2].T]),
        grad_b_down,
    )


def solution(mesh):
    in_specs = (
        P("shard", "ctx", "tp", None, None),
        P("shard", None),
        P(None, "shard", "tp"),
        P(None, "tp"),
        P(None, None, "shard", "tp"),
        P(None, None, "tp"),
        P(None, "tp", "shard"),
        P(),
        P(None, "shard", "tp"),
        P(None, "tp"),
        P(None, "tp", "shard"),
        P(),
        P("shard", None, "tp", "ctx", None),
    )
    out_specs = (
        P("shard", None, "tp", "ctx", None),
        P("shard", "ctx", "tp", None, None),
        P("shard", None),
        P(None, "shard", "tp"),
        P(None, "tp"),
        P(None, None, "shard", "tp"),
        P(None, None, "tp"),
        P(None, "tp", "shard"),
        P(),
        P(None, "shard", "tp"),
        P(None, "tp"),
        P(None, "tp", "shard"),
        P(),
    )
    return jax.shard_map(body, mesh=mesh, in_specs=in_specs, out_specs=out_specs, check_vma=False)
```

```python
from functools import partial
import math

import jax
import jax.numpy as jnp
from jax import lax
from jax.experimental import pallas as pl
from jax.experimental.pallas import tpu as pltpu
from jax.sharding import PartitionSpec as P

HEAD_DIM = 72
bf16 = jnp.bfloat16
f32 = jnp.float32
highest = lax.Precision.HIGHEST


class Place:
    def __init__(self):
        self.ns = lax.axis_size("shard")
        self.nc = lax.axis_size("ctx")
        self.nt = lax.axis_size("tp")
        self.s = lax.axis_index("shard")
        self.c = lax.axis_index("ctx")
        self.t = lax.axis_index("tp")
        self.x = self.c // 2
        self.k = self.c % 2
        self.d = jnp.where(self.k == 0, self.t, self.nt - 1 - self.t)

    def core(self, v):
        return lax.ppermute(v, "ctx", [(c, c ^ 1) for c in range(self.nc)])

    def swap_x(self, v):
        return lax.ppermute(v, "ctx", [(c, c ^ 2) for c in range(self.nc)])

    def swap_y(self, v):
        return lax.ppermute(v, "shard", [(i, i ^ 1) for i in range(self.ns)])

    def along_z(self, v, pairs):
        def at(c, d):
            return c * self.nt + (d if c % 2 == 0 else self.nt - 1 - d)

        return lax.ppermute(
            v, ("ctx", "tp"), [(at(c, i), at(c, j)) for c in range(self.nc) for i, j in pairs]
        )

    def sum_group(self, v, z_only=False):
        if not z_only:
            for step in (1, 2):
                v = v + lax.ppermute(v, "ctx", [(c, c ^ step) for c in range(self.nc)])
        for step in (1, 2):
            v = v + lax.ppermute(v, "tp", [(i, i ^ step) for i in range(self.nt)])
        return v

    def sum_all(self, v, per_clip):
        size = v.size
        v = self.sum_group(jnp.concatenate([v, per_clip]).reshape(1, -1))
        if self.ns != 2:
            return lax.psum(v[0, :size], "shard"), lax.all_gather(
                v[:, size:], "shard", axis=0, tiled=True
            )
        w = self.swap_y(v)
        rows = [jnp.where(self.s == 0, v, w), jnp.where(self.s == 0, w, v)]
        return (v + w)[0, :size], jnp.concatenate(rows, axis=0)[:, size:]

    def by_x(self, near, far):
        return [jnp.where(self.x == 0, near, far), jnp.where(self.x == 0, far, near)]

    def by_k(self, near, far):
        return [jnp.where(self.k == 0, near, far), jnp.where(self.k == 0, far, near)]


def pick(index, options):
    out = options[-1]
    for number in range(len(options) - 2, -1, -1):
        out = jnp.where(index == number, options[number], out)
    return out


def tie(values, *others):
    return lax.optimization_barrier((values, others))[0]


def cuts_of(rows):
    common = rows * 4 // 9 // 32 * 32
    return common, (rows - common) // 2


def gather_z(at, chunk, after):
    if at.ns == 2:
        common, part = cuts_of(chunk.shape[0])
        start = common + at.x * part
        chunk = jnp.concatenate(
            [chunk[:common], lax.dynamic_slice_in_dim(chunk, start, part, axis=0)], axis=0
        )
    routes = ([(0, 1), (1, 0)], [(0, 2), (1, 3)], [(0, 3), (1, 2)])
    got = [
        at.along_z(chunk if wait is None else tie(chunk, *wait), pairs)
        for pairs, wait in zip(routes, after)
    ]
    r1, r2, r3 = got
    source = at.d ^ at.k
    both = jnp.stack([pick(source, [chunk, r1, r2, r3]), pick(source ^ 1, [chunk, r1, r2, r3])])
    return both, [(r,) for r in got]


def gather_yx(at, both, rows):
    common, _ = cuts_of(rows)
    half = common // 2
    mine = jnp.concatenate(
        [lax.dynamic_slice_in_dim(both, at.x * half, half, axis=1), both[:, common:]], axis=1
    )
    near = at.swap_y(mine)
    far = at.swap_x(jnp.concatenate([near, both[:, common:]], axis=1))
    return near, far


def assemble_kernel(place_ref, *refs, sizes):
    out_ref = refs[-1]
    s, x = place_ref[0], place_ref[1]
    width = sum(sizes)

    def copy(source, start, size, offset):
        out_ref[0, pl.ds(pl.multiple_of(offset, 16), size), :] = source[0, start : start + size, :]

    base = 0
    for number, rows in enumerate(sizes):
        both, near, far = refs[3 * number : 3 * number + 3]
        common, part = cuts_of(rows)
        half = common // 2
        own = s * width + base
        other = (1 - s) * width + base
        copy(both, 0, common, own)
        copy(both, common, part, own + common + x * part)
        copy(far, half + part, part, own + common + (1 - x) * part)
        copy(near, 0, half, other + x * half)
        copy(near, half, part, other + common + x * part)
        copy(far, 0, half, other + (1 - x) * half)
        copy(far, half, part, other + common + (1 - x) * part)
        base += rows


def assemble(at, chunks, sizes):
    cols = chunks[0].shape[2]
    return pl.pallas_call(
        partial(assemble_kernel, sizes=sizes),
        out_shape=jax.ShapeDtypeStruct((2, 2 * sum(sizes), cols), bf16),
        grid=(2,),
        in_specs=[pl.BlockSpec(memory_space=pltpu.SMEM)]
        + [pl.BlockSpec((1,) + c.shape[1:], lambda i: (i, 0, 0)) for c in chunks],
        out_specs=pl.BlockSpec((1, 2 * sum(sizes), cols), lambda i: (i, 0, 0)),
        compiler_params=pltpu.CompilerParams(vmem_limit_bytes=40 * 1024 * 1024),
    )(jnp.stack([at.s, at.x]).astype(jnp.int32), *chunks)


def gather_weights(at, pieces, splits, startup):
    after = [None] * 3
    whole = []
    for number, ((piece, prepare), count) in enumerate(zip(pieces, splits)):
        count = count if at.ns == 2 else 1
        if number > 1:
            piece = tie(piece, *[wait[0] for wait in after])
        piece = prepare(piece)
        rows = piece.shape[0] // count
        chunks = []
        for part in range(count):
            both, after = gather_z(at, piece[part * rows : (part + 1) * rows], after)
            if number == 0 and part == 0:
                ready = startup(after)
                after = [wait + tuple(ready) for wait in after]
            if at.ns == 2:
                chunks += [both, *gather_yx(at, both, rows)]
        if at.ns == 2:
            whole.append(assemble(at, chunks, (rows,) * count))
        else:
            whole.append(lax.all_gather(both, "shard", axis=1, tiled=True))
    return whole, ready


def product(left, right):
    return sum(
        jnp.einsum("rd,prn->pdn", l, r, preferred_element_type=f32) for l, r in zip(left, right)
    )


def reduce_z(at, blocks):
    half = blocks.shape[1] // 2
    halves = [blocks[:, :half], blocks[:, half:]]
    got = at.core(jnp.where(at.k == 0, halves[1], halves[0]))
    kept = jnp.where(at.k == 0, halves[0], halves[1])
    everything = jnp.concatenate(at.by_k(kept, got), axis=0)
    return lax.psum_scatter(everything, "tp", scatter_dimension=0, tiled=True)[0]


def sum_flow(at, left, right):
    width = left[0].shape[1]
    if at.ns != 2:
        summed = lax.psum_scatter(
            product(left, right).astype(bf16), "shard", scatter_dimension=1, tiled=True
        )
        (mine,) = yield [(partial(reduce_z, at), summed)]
        mine = (mine.astype(f32) + at.swap_x(mine).astype(f32)).astype(bf16)
        (theirs,) = yield [(at.core, mine)]
        return jnp.concatenate(at.by_k(mine, theirs), axis=0)
    rows = width // 8

    def take(ds, dx, half):
        index = 2 * (at.s ^ ds) + (at.x ^ dx)
        return [
            pick(
                index,
                [l[:, (2 * i + half) * rows : (2 * i + half + 1) * rows] for i in range(4)],
            )
            for l in left
        ]

    def term(one, two):
        return product([jnp.concatenate(pair, axis=1) for pair in zip(take(*one), take(*two))], right)

    away_y = term((1, 0, 0), (1, 1, 0)).astype(bf16)
    away_x = term((0, 1, 1), (1, 1, 1)).astype(bf16)
    from_y, from_x = yield [(at.swap_y, away_y), (at.swap_x, away_x)]
    first = term((0, 0, 0), (0, 1, 0)) + from_y.astype(f32)
    second = term((0, 0, 1), (1, 0, 1)) + from_x.astype(f32)
    from_x, from_y = yield [
        (at.swap_x, first[:, rows:].astype(bf16)),
        (at.swap_y, second[:, rows:].astype(bf16)),
    ]
    first = (first[:, :rows] + from_x.astype(f32)).astype(bf16)
    second = (second[:, :rows] + from_y.astype(f32)).astype(bf16)
    (mine,) = yield [(partial(reduce_z, at), jnp.concatenate([first, second], axis=1))]
    (far,) = yield [(at.swap_x, mine)]
    pair = jnp.stack(at.by_x(mine, far))
    theirs = at.core(pair)
    return jnp.stack(at.by_k(pair, theirs), axis=1).reshape(-1, mine.shape[1])


class Flows:
    def __init__(self, at):
        self.at = at
        self.flows = {}
        self.pending = {}
        self.results = {}

    def start(self, name, left, right, main):
        self.flows[name] = sum_flow(self.at, left, right)
        return self.send(name, next(self.flows[name]), main)

    def send(self, name, messages, main):
        values, main = lax.optimization_barrier(([value for _, value in messages], main))
        self.pending[name] = [how(value) for (how, _), value in zip(messages, values)]
        return main

    def step(self, names, main):
        for name in names.split():
            if name not in self.pending:
                continue
            pending, main = lax.optimization_barrier((self.pending.pop(name), main))
            try:
                main = self.send(name, self.flows[name].send(pending), main)
            except StopIteration as stop:
                self.results[name], main = lax.optimization_barrier((stop.value, main))
        return main

    def finish(self, main):
        while self.pending:
            for name in list(self.pending):
                main = self.step(name, main)
        return main


def layout_kernel(first_ref, second_ref, qkv_ref, out_ref):
    for b, ref in enumerate((first_ref, second_ref)):
        values = ref[...].astype(f32)
        cols = qkv_ref.shape[3]
        for number in range(3):
            qkv_ref[b, number] = values[:, number * cols : (number + 1) * cols]
        out_ref[b] = values[:, 3 * cols :].T


def attention_grads(first, second, head_width):
    rows = first.shape[0]
    return pl.pallas_call(
        layout_kernel,
        out_shape=(
            jax.ShapeDtypeStruct((2, 3, rows, head_width), f32),
            jax.ShapeDtypeStruct((2, head_width, rows), f32),
        ),
        compiler_params=pltpu.CompilerParams(vmem_limit_bytes=40 * 1024 * 1024),
    )(first, second)


def heads_of(values, number, head):
    start = number * 4 * HEAD_DIM + head * HEAD_DIM
    return values[:, start : start + HEAD_DIM]


def probs_of(query, key, temporal):
    scores = lax.dot_general(
        query, key, (((1,), (1,)), ((), ())), preferred_element_type=f32
    ) * (1.0 / math.sqrt(HEAD_DIM))
    if temporal:
        rows = lax.broadcasted_iota(jnp.int32, scores.shape, 0) % temporal
        cols = lax.broadcasted_iota(jnp.int32, scores.shape, 1) % temporal
        scores = jnp.where(rows == cols, scores, -jnp.inf)
    weights = jnp.exp(scores - jnp.max(scores, axis=-1, keepdims=True))
    return weights / jnp.sum(weights, axis=-1, keepdims=True)


def attend_kernel(qkv_ref, out_ref, *, temporal):
    values = qkv_ref[0]
    results = [jnp.zeros((values.shape[0], 12 * HEAD_DIM), bf16)]
    for head in range(4):
        probs = probs_of(heads_of(values, 0, head), heads_of(values, 1, head), temporal)
        results.append(
            jnp.dot(
                probs.astype(bf16), heads_of(values, 2, head), preferred_element_type=f32
            ).astype(bf16)
        )
    out_ref[0] = jnp.concatenate(results, axis=1)


def attend_back_kernel(qkv_ref, grad_ref, out_ref, *, temporal):
    factor = 1.0 / math.sqrt(HEAD_DIM)
    values = qkv_ref[0]
    grads = grad_ref[0]
    queries, keys, vals = [], [], []
    for head in range(4):
        query, key, value = (heads_of(values, number, head) for number in range(3))
        grad = heads_of(grads, 3, head)
        probs = probs_of(query, key, temporal)
        vals.append(
            lax.dot_general(
                probs.astype(bf16), grad, (((0,), (0,)), ((), ())), preferred_element_type=f32
            ).astype(bf16)
        )
        grad_probs = lax.dot_general(
            grad, value, (((1,), (1,)), ((), ())), preferred_element_type=f32
        )
        inner = jnp.sum(grad_probs * probs, axis=-1, keepdims=True)
        grad_scores = (probs * (grad_probs - inner)).astype(bf16)
        queries.append(
            (jnp.dot(grad_scores, key, preferred_element_type=f32) * factor).astype(bf16)
        )
        keys.append(
            (
                lax.dot_general(
                    grad_scores, query, (((0,), (0,)), ((), ())), preferred_element_type=f32
                )
                * factor
            ).astype(bf16)
        )
    zeros = jnp.zeros((values.shape[0], 4 * HEAD_DIM), bf16)
    out_ref[0] = jnp.concatenate(queries + keys + vals + [zeros], axis=1)


def call_attention(kernel, arrays, rows, temporal):
    shape = arrays[0].shape
    spec = pl.BlockSpec((1, rows, shape[2]), lambda i, j: (i, j, 0))
    return pl.pallas_call(
        partial(kernel, temporal=temporal),
        out_shape=jax.ShapeDtypeStruct(shape, bf16),
        grid=(shape[0], shape[1] // rows),
        in_specs=[spec] * len(arrays),
        out_specs=spec,
        compiler_params=pltpu.CompilerParams(vmem_limit_bytes=48 * 1024 * 1024),
    )(*arrays)


def normalized(values):
    average = jnp.mean(values, axis=-1, keepdims=True)
    centered = values - average
    inverse = lax.rsqrt(jnp.mean(centered * centered, axis=-1, keepdims=True) + 1e-06)
    return centered * inverse, inverse


def norm_back(grad, normal, inverse, factor):
    dn = grad * (1.0 + factor)
    return (
        dn
        - jnp.mean(dn, axis=-1, keepdims=True)
        - normal * jnp.mean(dn * normal, axis=-1, keepdims=True)
    ) * inverse


def pair_rows(at, values):
    return jnp.concatenate([values, at.core(values)], axis=0)


def pair_sum(at, partial_rows):
    rows = partial_rows.shape[0] // 2
    return partial_rows[:rows] + at.core(partial_rows[rows:].astype(bf16)).astype(f32)


def times(left, weight):
    return jnp.einsum("rd,pdn->prn", left, weight, preferred_element_type=f32)


def times_back(left, weight):
    return jnp.einsum("prn,pdn->rd", left, weight, preferred_element_type=f32)


def forward_block(at, inputs, mod, weights, bias_qkv, bias_up, b_out, b_down, temporal):
    w_attn, w_up, w_down = weights
    shift_a, scale_a, gate_a, shift_m, scale_m, gate_m = mod
    rows = inputs.shape[0]
    hidden = (normalized(inputs)[0] * (1.0 + scale_a) + shift_a).astype(bf16)
    hidden = pair_rows(at, hidden)
    qkv = (times(hidden, w_attn) + bias_qkv[:, None, :]).astype(bf16)
    attended = call_attention(attend_kernel, [qkv], rows, temporal)
    attn_out = pair_sum(at, times_back(attended, w_attn)) + b_out
    after = inputs + gate_a * attn_out
    hidden_two = (normalized(after)[0] * (1.0 + scale_m) + shift_m).astype(bf16)
    hidden_two = pair_rows(at, hidden_two)
    up = times(hidden_two, w_up) + bias_up[:, None, :]
    activated = jax.nn.gelu(up, approximate=True).astype(bf16)
    mlp_out = pair_sum(at, times_back(activated, w_down)) + b_down
    result = after + gate_m * mlp_out
    return result, (inputs, hidden, qkv, attended, attn_out, after, hidden_two, up, mlp_out)


def backward_block(at, grad_y, kept, mod, weights, temporal, flows, names, steps):
    inputs, hidden, qkv, attended, attn_out, after, hidden_two, up, mlp_out = kept
    w_attn, w_up, w_down = weights
    shift_a, scale_a, gate_a, shift_m, scale_m, gate_m = mod
    rows = inputs.shape[0]
    grad_mlp = (gate_m * grad_y).astype(bf16)
    grad_gate_m = jnp.sum(grad_y * mlp_out, axis=0)
    grad_b_down = jnp.sum(grad_mlp, axis=0, dtype=f32)
    grad_mlp = pair_rows(at, grad_mlp)
    activated, gelu_back = jax.vjp(partial(jax.nn.gelu, approximate=True), up)
    activated = activated.astype(bf16)
    grad_up = gelu_back(times(grad_mlp, w_down))[0].astype(bf16)
    grad_up = flows.step(steps[0], grad_up)
    grad_up = flows.start(names[0], [grad_mlp], [activated], grad_up)
    grad_b_up = jnp.sum(grad_up, axis=1, dtype=f32)
    grad_hidden_two = pair_sum(at, times_back(grad_up, w_up))
    normal, inverse = normalized(after)
    grad_shift_m = jnp.sum(grad_hidden_two, axis=0)
    grad_scale_m = jnp.sum(grad_hidden_two * normal, axis=0)
    grad_after = grad_y + norm_back(grad_hidden_two, normal, inverse, scale_m)
    grad_attn = (gate_a * grad_after).astype(bf16)
    grad_gate_a = jnp.sum(grad_after * attn_out, axis=0)
    grad_b_out = jnp.sum(grad_attn, axis=0, dtype=f32)
    grad_attn = pair_rows(at, grad_attn)
    grad_attn = flows.step(steps[1], grad_attn)
    grad_attn = flows.start(names[1], [hidden_two], [grad_up], grad_attn)
    grad_attended = times(grad_attn, w_attn).astype(bf16)
    grad_attended = flows.step(steps[2], grad_attended)
    grad_qkv = call_attention(attend_back_kernel, [qkv, grad_attended], rows, temporal)
    grad_qkv = flows.step(steps[3], grad_qkv)
    grad_b_qkv = jnp.sum(grad_qkv, axis=1, dtype=f32)
    grad_hidden = times_back(grad_qkv, w_attn)
    grad_hidden = pair_sum(at, grad_hidden)
    normal, inverse = normalized(inputs)
    grad_shift_a = jnp.sum(grad_hidden, axis=0)
    grad_scale_a = jnp.sum(grad_hidden * normal, axis=0)
    grad_inputs = grad_after + norm_back(grad_hidden, normal, inverse, scale_a)
    grad_mod = jnp.concatenate(
        [grad_shift_a, grad_scale_a, grad_gate_a, grad_shift_m, grad_scale_m, grad_gate_m]
    )
    width = grad_b_qkv.shape[1] // 4
    grad_bias = jnp.concatenate(
        [grad_b_qkv[:, :width], grad_b_qkv[:, 2 * width : 3 * width], grad_b_up], axis=1
    )
    last = ([hidden, grad_attn], [grad_qkv, attended])
    return grad_inputs, last, grad_bias, grad_b_out, grad_b_down, grad_mod


def body(
    video, cond, w_ada, b_ada, w_qkv, b_qv, w_out, b_out, w_up, b_up, w_down, b_down, cotangent
):
    at = Place()
    width = video.shape[-1]
    own_width = w_up.shape[1]
    head_width = w_qkv.shape[3]
    silu_value, silu_back = jax.vjp(jax.nn.silu, cond.astype(f32))
    cond_act = silu_value.astype(bf16)
    cond_all = lax.all_gather(cond_act, "shard", axis=0, tiled=True)
    cond_rows = lax.dynamic_slice_in_dim(cond_all, at.s * own_width, own_width, axis=1)
    mod_part = jnp.einsum("cd,bdn->cbn", cond_rows, w_ada, preferred_element_type=f32)
    if at.ns == 2:
        kept = lax.dynamic_index_in_dim(mod_part, at.s, 0, False)
        mod_part = kept + at.swap_y(lax.dynamic_index_in_dim(mod_part, 1 - at.s, 0, False))
    else:
        mod_part = lax.psum_scatter(mod_part, "shard", scatter_dimension=0, tiled=True)[0]
    ada_cols = w_ada.shape[2]
    small = jnp.concatenate(
        [mod_part + b_ada, b_qv.reshape(2, -1).astype(f32), b_up.astype(f32)], axis=1
    )

    def startup(after):
        sent = tie(small, *[wait for waits in after for wait in waits])
        return (lax.all_gather(sent, "tp", axis=0, tiled=False),)

    pieces = []
    for b in range(2):
        pieces += [
            (
                (w_qkv[b], w_out[b]),
                lambda two: jnp.concatenate([*two[0], two[1].T], axis=1),
            ),
            (w_up[b], lambda one: one),
            (w_down[b], lambda one: one.T),
        ]
    weights, (small,) = gather_weights(at, pieces, (2, 1, 1, 1, 1, 2), startup)
    first, second = weights[:3], weights[3:]
    mods = jnp.moveaxis(small[:, :, :ada_cols], 0, 1).reshape(2, 6, width)
    biases = small[:, :, ada_cols:]
    biases = jnp.stack(
        [
            lax.dynamic_index_in_dim(biases, 2 * at.k, 0, False),
            lax.dynamic_index_in_dim(biases, 2 * at.k + 1, 0, False),
        ],
        axis=1,
    )
    zeros = jnp.zeros((2, 2, head_width), f32)
    bias_qkv = jnp.concatenate(
        [biases[:, :, :head_width], zeros, biases[:, :, head_width : 2 * head_width], zeros], axis=2
    )
    bias_up = biases[:, :, 2 * head_width :]

    frames = lax.all_to_all(video, "tp", split_axis=1, concat_axis=2, tiled=True)
    rows = frames.size // width

    inputs = frames.reshape(rows, width).astype(f32)
    middle, kept_one = forward_block(
        at, inputs, mods[0], first, bias_qkv[0], bias_up[0], b_out[0], b_down[0], 0
    )
    moved = lax.all_to_all(
        middle.astype(bf16).reshape(frames.shape), "tp", split_axis=2, concat_axis=1, tiled=True
    )
    moved = lax.all_to_all(moved, "ctx", split_axis=3, concat_axis=1, tiled=True)
    grid = moved.shape
    patches = grid[2] * grid[3]
    result, kept_two = forward_block(
        at,
        moved.reshape(rows, width).astype(f32),
        mods[1],
        second,
        bias_qkv[1],
        bias_up[1],
        b_out[1],
        b_down[1],
        patches,
    )
    flows = Flows(at)
    grad_moved, last, *small_two = backward_block(
        at,
        cotangent.reshape(rows, width).astype(f32),
        kept_two,
        mods[1],
        second,
        patches,
        flows,
        ("d2", "u2"),
        ("", "", "d2", "d2"),
    )
    grad_middle = lax.all_to_all(
        grad_moved.astype(bf16).reshape(grid), "ctx", split_axis=1, concat_axis=3, tiled=True
    )
    grad_middle = flows.step("u2", grad_middle)
    grad_middle = flows.start("a2", *last, grad_middle)
    grad_middle = lax.all_to_all(grad_middle, "tp", split_axis=1, concat_axis=2, tiled=True)
    grad_frames, last, *small_one = backward_block(
        at,
        grad_middle.reshape(rows, width).astype(f32),
        kept_one,
        mods[0],
        first,
        0,
        flows,
        ("d1", "u1"),
        ("u2 a2", "d2", "a2 d2", "d1 u2"),
    )
    grad_frames = flows.start("a1", *last, grad_frames)
    grad_video = lax.all_to_all(
        grad_frames.astype(bf16).reshape(frames.shape), "tp", split_axis=2, concat_axis=1, tiled=True
    ).astype(f32)

    grad_bias, grad_b_out, grad_b_down, grad_mod = (
        jnp.stack([one, two]) for one, two in zip(small_one, small_two)
    )
    blocks = jnp.arange(at.nt)[:, None, None]
    grad_bias = jnp.where(blocks == 2 * at.k, grad_bias[:, 0], 0.0) + jnp.where(
        blocks == 2 * at.k + 1, grad_bias[:, 1], 0.0
    )
    sums, grad_mods = at.sum_all(
        jnp.concatenate([grad_bias.reshape(-1), grad_b_out.reshape(-1), grad_b_down.reshape(-1)]),
        grad_mod.reshape(-1),
    )
    size = grad_bias.size
    grad_bias = lax.dynamic_index_in_dim(sums[:size].reshape(grad_bias.shape), at.t, 0, False)
    grad_b_out, grad_b_down = sums[size:].reshape(2, 2, width)
    grad_mods = jnp.moveaxis(grad_mods.reshape(at.ns, 2, 6 * width), 0, 1)
    flows.finish(())
    sums = flows.results
    grad_mods = lax.dynamic_slice_in_dim(grad_mods, at.t * ada_cols, ada_cols, axis=2)
    cond_rows = cond_rows.astype(f32)
    grad_w_ada = sum(
        cond_rows[i][None, :, None] * grad_mods[:, i][:, None, :] for i in range(at.ns)
    )
    grad_b_ada = jnp.sum(grad_mods, axis=1)
    grad_act = jnp.einsum(
        "bcn,bdn->cd", grad_mods, w_ada.astype(f32), precision=highest, preferred_element_type=f32
    )
    if at.ns == 2:
        grad_act = at.sum_group(grad_act, z_only=True)
        ours = lax.dynamic_slice_in_dim(grad_act, at.s, 1, axis=0)
        theirs = at.swap_y(lax.dynamic_slice_in_dim(grad_act, 1 - at.s, 1, axis=0))
        grad_act = jnp.concatenate(
            [jnp.where(at.s == 0, ours, theirs), jnp.where(at.s == 0, theirs, ours)], axis=1
        )
    else:
        grad_act = lax.psum_scatter(
            lax.dynamic_update_slice_in_dim(
                jnp.zeros((at.ns, width), f32), grad_act, at.s * own_width, axis=1
            ),
            "shard",
            scatter_dimension=0,
            tiled=True,
        )
        grad_act = lax.psum(grad_act, "tp")
    grad_cond = silu_back(grad_act)[0]

    grad_w_qkv, grad_w_out = attention_grads(sums["a1"], sums["a2"], head_width)
    return (
        result.astype(bf16).reshape(grid),
        grad_video,
        grad_cond,
        grad_w_ada,
        grad_b_ada,
        grad_w_qkv,
        grad_bias[:, : 2 * head_width].reshape(2, 2, head_width),
        grad_w_out,
        grad_b_out,
        jnp.stack([sums["u1"], sums["u2"]]).astype(f32),
        grad_bias[:, 2 * head_width :],
        jnp.stack([sums["d1"].T, sums["d2"].T]).astype(f32),
        grad_b_down,
    )


def solution(mesh):
    in_specs = (
        P("shard", "ctx", "tp", None, None),
        P("shard", None),
        P(None, "shard", "tp"),
        P(None, "tp"),
        P(None, None, "shard", "tp"),
        P(None, None, "tp"),
        P(None, "tp", "shard"),
        P(),
        P(None, "shard", "tp"),
        P(None, "tp"),
        P(None, "tp", "shard"),
        P(),
        P("shard", None, "tp", "ctx", None),
    )
    out_specs = (
        P("shard", None, "tp", "ctx", None),
        P("shard", "ctx", "tp", None, None),
        P("shard", None),
        P(None, "shard", "tp"),
        P(None, "tp"),
        P(None, None, "shard", "tp"),
        P(None, None, "tp"),
        P(None, "tp", "shard"),
        P(),
        P(None, "shard", "tp"),
        P(None, "tp"),
        P(None, "tp", "shard"),
        P(),
    )
    return jax.shard_map(body, mesh=mesh, in_specs=in_specs, out_specs=out_specs, check_vma=False)
```

```python
from functools import partial
import math

import jax
import jax.numpy as jnp
from jax import lax
from jax.experimental import pallas as pl
from jax.experimental.pallas import tpu as pltpu
from jax.sharding import PartitionSpec as P

HEAD_DIM = 72
bf16 = jnp.bfloat16
f32 = jnp.float32
highest = lax.Precision.HIGHEST


class Place:
    def __init__(self):
        self.ns = lax.axis_size("shard")
        self.nc = lax.axis_size("ctx")
        self.nt = lax.axis_size("tp")
        self.s = lax.axis_index("shard")
        self.c = lax.axis_index("ctx")
        self.t = lax.axis_index("tp")
        self.x = self.c // 2
        self.k = self.c % 2
        self.d = jnp.where(self.k == 0, self.t, self.nt - 1 - self.t)

    def core(self, v):
        return lax.ppermute(v, "ctx", [(c, c ^ 1) for c in range(self.nc)])

    def swap_x(self, v):
        return lax.ppermute(v, "ctx", [(c, c ^ 2) for c in range(self.nc)])

    def swap_y(self, v):
        return lax.ppermute(v, "shard", [(i, i ^ 1) for i in range(self.ns)])

    def along_z(self, v, pairs):
        def at(c, d):
            return c * self.nt + (d if c % 2 == 0 else self.nt - 1 - d)

        return lax.ppermute(
            v, ("ctx", "tp"), [(at(c, i), at(c, j)) for c in range(self.nc) for i, j in pairs]
        )

    def gather_small(self, v):
        got = [v] + [
            lax.ppermute(v, "tp", [(i, i ^ step) for i in range(self.nt)])
            for step in range(1, self.nt)
        ]
        return jnp.stack([pick(self.t ^ i, got) for i in range(self.nt)])

    def sum_group(self, v, axis, step):
        size = self.nc if axis == "ctx" else self.nt
        return v + lax.ppermute(v, axis, [(i, i ^ step) for i in range(size)])

    def sum_all(self, v, per_clip, between):
        size = v.size
        v = jnp.concatenate([v, per_clip]).reshape(1, -1)
        v = self.sum_group(v, "ctx", 1)
        v = between[0](v)
        v = self.sum_group(v, "ctx", 2)
        v = between[1](v)
        v = self.sum_group(v, "tp", 1)
        v = self.sum_group(v, "tp", 2)
        v = between[2](v)
        if self.ns != 2:
            return lax.psum(v[0, :size], "shard"), lax.all_gather(
                v[:, size:], "shard", axis=0, tiled=True
            )
        w = self.swap_y(v)
        rows = [jnp.where(self.s == 0, v, w), jnp.where(self.s == 0, w, v)]
        return (v + w)[0, :size], jnp.concatenate(rows, axis=0)[:, size:]

    def position(self):
        return jnp.stack([self.s, self.x, self.k]).astype(jnp.int32)

    def by_x(self, near, far):
        return [jnp.where(self.x == 0, near, far), jnp.where(self.x == 0, far, near)]

    def by_k(self, near, far):
        return [jnp.where(self.k == 0, near, far), jnp.where(self.k == 0, far, near)]


def pick(index, options):
    out = options[-1]
    for number in range(len(options) - 2, -1, -1):
        out = jnp.where(index == number, options[number], out)
    return out


def tie(values, *others):
    return lax.optimization_barrier((values, others))[0]


class Chunk:
    def __init__(self, first, common, part):
        self.first = first
        self.common = common
        self.part = part
        self.rows = common + 2 * part

    def sent(self, at, both, b):
        half, part = self.common // 2, self.part // 2
        starts = (self.first + at.k * half, self.first + self.common + at.x * self.part + at.k * part)
        cols = both.shape[2]
        return jnp.concatenate(
            [
                lax.dynamic_slice(both, (b, start, 0), (1, size, cols))[0]
                for start, size in zip(starts, (half, part))
            ],
            axis=0,
        )

    def core_step(self, at, blocks):
        got = at.core(lax.dynamic_slice_in_dim(blocks, 2 - 2 * at.k, 2, axis=0))
        mine = lax.dynamic_slice_in_dim(blocks, 2 * at.k, 2, axis=0)
        half = self.common // 2
        common = jnp.where(at.x == at.k, mine[:, :half], got[:, :half])
        part = jnp.concatenate([mine[:, half:], got[:, half:]], axis=1)
        return (mine, got), jnp.concatenate([common, part], axis=1), part


def assemble_kernel(place_ref, *refs, chunk):
    out_ref, turned_ref = refs[-2:]
    s, x, k = place_ref[0], place_ref[1], place_ref[2]
    width = out_ref.shape[1] // 2

    def copy(source, start, size, offset):
        if size:
            out_ref[0, pl.ds(pl.multiple_of(offset, 16), size), :] = source[
                0, start : start + size, :
            ]

    mine, got, near, far, side = refs[:5]
    half, part = chunk.common // 2, chunk.part // 2
    own, other = s * width, (1 - s) * width

    def parts(source, start, base, plane):
        offset = base + chunk.common + plane * chunk.part
        copy(source, start, part, offset + k * part)
        copy(source, start + part, part, offset + (1 - k) * part)

    copy(mine, 0, half, own + k * half)
    copy(got, 0, half, own + (1 - k) * half)
    copy(mine, half, part, own + chunk.common + x * chunk.part + k * part)
    copy(got, half, part, own + chunk.common + x * chunk.part + (1 - k) * part)
    parts(side, 0, own, 1 - x)
    copy(near, 0, half, other + x * half)
    parts(near, half, other, x)
    copy(far, 0, half, other + (1 - x) * half)
    parts(far, half, other, 1 - x)
    turned_ref[0] = out_ref[0].T


def assemble(at, chunk, arrays):
    cols = arrays[0].shape[2]
    rows = 2 * chunk.rows
    return call(
        partial(assemble_kernel, chunk=chunk),
        [(a, False) for a in arrays],
        [(shape_of(2, rows, cols), False), (shape_of(2, cols, rows), False)],
        scalars=(at.position(),),
    )


class Weights:
    def __init__(self, at, arrays):
        self.at = at
        self.whole = []
        self.count = 2 * len(arrays)
        self.number = 0
        jobs = [(b, array) for b in range(2) for array in arrays]
        if at.ns != 2:
            for b, array in jobs:
                both = lax.all_gather(array[b], "tp", axis=0)
                both = lax.dynamic_slice_in_dim(both, 2 * at.k, 2, axis=0)
                both = lax.all_gather(both, "shard", axis=1, tiled=True)
                self.whole.append((both, jnp.swapaxes(both, 1, 2)))
            return
        rows = arrays[0].shape[1]
        self.plan = Chunk(0, rows // 9 * 5, rows // 9 * 2)
        self.blocks = []
        sent = ()
        for b, array in jobs:
            sent = self.plan.sent(at, tie(array, sent), b)
            self.blocks.append(lax.all_gather(sent, "tp", axis=0))
        self.held, self.near, self.far, self.side = {}, {}, {}, {}

    def step(self, main):
        if self.at.ns != 2 or self.number == self.count + 2:
            return main
        at, number = self.at, self.number
        self.number += 1
        block = self.blocks[number] if number < self.count else ()
        block, near, far, side, main = lax.optimization_barrier(
            (
                block,
                self.near.get(number - 1),
                self.far.get(number - 2),
                self.side.get(number - 1),
                main,
            )
        )
        last = self.count - 1
        if 0 < number <= self.count:
            self.near[number - 1], self.side[number - 1] = near, side
            if number - 1 == last:
                near = jnp.concatenate([near, side], axis=1)
            self.far[number - 1] = at.swap_x(near)
        if number < self.count:
            self.held[number], *messages = self.plan.core_step(at, block)
            messages, main = lax.optimization_barrier((messages, main))
            self.near[number] = at.swap_y(messages[0])
            self.side[number] = messages[1] if number == last else at.swap_x(messages[1])
        if number > 1:
            m = number - 2
            side = self.side[m]
            if m == last:
                edge = self.near[m].shape[1]
                far, side = far[:, :edge], far[:, edge:]
            self.whole.append(assemble(at, self.plan, [*self.held[m], self.near[m], far, side]))
        return main


def scatter_z(everything):
    return lax.psum_scatter(everything, "tp", scatter_dimension=0, tiled=True)[0]


def product(left, right):
    left = jnp.concatenate(left, axis=0)
    right = jnp.concatenate(right, axis=1)
    return jnp.einsum("rd,prn->pdn", left, right, preferred_element_type=f32).astype(bf16)


def term_of(turned, right, starts, rows):
    left = [turned[pl.ds(pl.multiple_of(start, 16), rows), :] for start in starts]
    left = jnp.concatenate(left, axis=0)
    depth = right[0].shape[1]
    return sum(
        jnp.dot(left[:, i * depth : (i + 1) * depth], r[0], preferred_element_type=f32)
        for i, r in enumerate(right)
    )


def starts_of(place_ref, width, pairs, half):
    s, x = place_ref[0], place_ref[1]
    return [
        (4 * jnp.abs(s - ds) + 2 * jnp.abs(x - dx) + half) * (width // 8) for ds, dx in pairs
    ]


def away_kernel(place_ref, *refs, count):
    left, right = refs[:count], refs[count:-3]
    to_y, to_x, turned = refs[-3:]
    rows = left[0].shape[0]
    width = turned.shape[0]

    @pl.when(pl.program_id(0) == 0)
    def _():
        for i, source in enumerate(left):
            turned[:, i * rows : (i + 1) * rows] = source[...].T

    first = starts_of(place_ref, width, ((1, 0), (1, 1)), 0)
    second = starts_of(place_ref, width, ((0, 1), (1, 1)), 1)
    to_y[0] = term_of(turned, right, first, width // 8).astype(bf16)
    to_x[0] = term_of(turned, right, second, width // 8).astype(bf16)


def here_kernel(place_ref, from_y, from_x, turned, *refs):
    right = refs[:-4]
    over_y, over_x, to_x, to_y = refs[-4:]
    width = turned.shape[0]
    rows = width // 8
    first = starts_of(place_ref, width, ((0, 0), (0, 1)), 0)
    second = starts_of(place_ref, width, ((0, 0), (1, 0)), 1)
    one = term_of(turned, right, first, rows) + from_y[0].astype(f32)
    over_y[0] = one[:rows].astype(bf16)
    to_x[0] = one[rows:].astype(bf16)
    two = term_of(turned, right, second, rows) + from_x[0].astype(f32)
    over_x[0] = two[:rows].astype(bf16)
    to_y[0] = two[rows:].astype(bf16)


def join_kernel(place_ref, over_y, over_x, from_x, from_y, kept, given):
    k = place_ref[2]
    for out, flag in ((kept, k == 0), (given, k == 1)):

        @pl.when(flag)
        def _():
            out[0] = (over_y[0].astype(f32) + from_x[0].astype(f32)).astype(bf16)

        @pl.when(jnp.logical_not(flag))
        def _():
            out[0] = (over_x[0].astype(f32) + from_y[0].astype(f32)).astype(bf16)


def per_block(array):
    return pl.BlockSpec((1,) + array.shape[1:], lambda i: (i,) + (0,) * (len(array.shape) - 1))


def entire(array):
    return pl.BlockSpec(array.shape, lambda i: (0,) * len(array.shape))


def call(kernel, inputs, outputs, scratch=(), scalars=()):
    return pl.pallas_call(
        kernel,
        out_shape=tuple(a for a, _ in outputs),
        grid=(2,),
        in_specs=[pl.BlockSpec(memory_space=pltpu.SMEM)] * len(scalars)
        + [entire(a) if whole else per_block(a) for a, whole in inputs],
        out_specs=tuple(entire(a) if whole else per_block(a) for a, whole in outputs),
        scratch_shapes=list(scratch),
        cost_estimate=pl.CostEstimate(flops=0, transcendentals=0, bytes_accessed=0),
        compiler_params=pltpu.CompilerParams(vmem_limit_bytes=48 * 1024 * 1024),
    )(*scalars, *[a for a, _ in inputs])


def shape_of(*dims, kind=bf16):
    return jax.ShapeDtypeStruct(dims, kind)


def products_away(at, left, right):
    rows, width = left[0].shape
    sent = shape_of(2, width // 4, right[0].shape[2])
    return call(
        partial(away_kernel, count=len(left)),
        [(l, True) for l in left] + [(r, False) for r in right],
        [(sent, False), (sent, False), (shape_of(width, rows * len(left)), True)],
        scalars=(at.position(),),
    )


def products_here(at, turned, right, from_y, from_x):
    part = shape_of(2, from_y.shape[1] // 2, from_y.shape[2])
    return call(
        here_kernel,
        [(from_y, False), (from_x, False), (turned, True)] + [(r, False) for r in right],
        [(part, False)] * 4,
        scalars=(at.position(),),
    )


def join_halves(at, *parts):
    return call(
        join_kernel,
        [(part, False) for part in parts],
        [(shape_of(*parts[0].shape), False)] * 2,
        scalars=(at.position(),),
    )


class Sums:
    def __init__(self, at):
        self.at = at
        self.state = {}
        self.done = {}

    def run(self, steps, main, left=None, right=None):
        for step in steps.split():
            kind, name = step.split(":")
            if kind == "p":
                self.state[name] = (None, (list(left), list(right)))
            elif name not in self.state:
                continue
            kept, pending = self.state.pop(name)
            pending, main = lax.optimization_barrier((pending, main))
            if self.at.ns != 2:
                self.done[name] = self.generic(*pending)
                continue
            kept, messages = getattr(self, "step_" + kind)(kept, pending)
            values, main = lax.optimization_barrier(([value for _, value in messages], main))
            if kind == "e":
                self.done[name] = values
            else:
                sent = [value if how is None else how(value) for (how, _), value in zip(messages, values)]
                self.state[name] = (kept, sent)
        return main

    def generic(self, left, right):
        at = self.at
        summed = lax.psum_scatter(
            product(left, right), "shard", scatter_dimension=1, tiled=True
        )
        half = summed.shape[1] // 2
        halves = [summed[:, :half], summed[:, half:]]
        got = at.core(jnp.where(at.k == 0, halves[1], halves[0]))
        kept = jnp.where(at.k == 0, halves[0], halves[1])
        mine = scatter_z(jnp.concatenate(at.by_k(kept, got), axis=0))
        mine = (mine.astype(f32) + at.swap_x(mine).astype(f32)).astype(bf16)
        return jnp.concatenate(at.by_k(mine, at.core(mine)), axis=0)

    def step_p(self, _, pending):
        left, right = pending
        to_y, to_x, turned = products_away(self.at, left, right)
        return (right, turned), [(None, to_y), (None, to_x)]

    def step_1(self, kept, pending):
        to_y, to_x = pending
        return kept, [(self.at.swap_y, to_y), (self.at.swap_x, to_x)]

    def step_2(self, kept, pending):
        right, turned = kept
        over_y, over_x, to_x, to_y = products_here(self.at, turned, right, *pending)
        return (over_y, over_x), [(self.at.swap_x, to_x), (self.at.swap_y, to_y)]

    def step_z(self, kept, pending):
        kept, given = join_halves(self.at, *kept, *pending)
        everything = jnp.concatenate(self.at.by_k(kept, self.at.core(given)), axis=0)
        return None, [(scatter_z, everything)]

    def step_f(self, _, pending):
        (mine,) = pending
        return mine, [(self.at.swap_x, mine)]

    def step_e(self, mine, pending):
        (far,) = pending
        mine = jnp.stack(self.at.by_x(mine, far))
        return None, [(None, mine), (None, self.at.core(mine))]


def rows_in_place(place_ref, mine, theirs, target, b):
    k = place_ref[2]
    rows = mine.shape[1]
    for ref, member in ((mine, k), (theirs, 1 - k)):
        for x in range(2):
            start = pl.multiple_of((2 * x + member) * rows, 8)
            target[b, pl.ds(start, rows), :] = ref[x].astype(f32)


def rows_kernel(place_ref, *refs):
    for b in range(2):
        rows_in_place(place_ref, refs[2 * b], refs[2 * b + 1], refs[4], b)


def turned_kernel(place_ref, *refs):
    qkv_ref, out_ref, target = refs[4:]
    cols = out_ref.shape[1]
    for b in range(2):
        rows_in_place(place_ref, refs[2 * b], refs[2 * b + 1], target, b)
        values = target[b].T
        for number in range(3):
            qkv_ref[b, number] = values[number * cols : (number + 1) * cols]
        out_ref[b] = values[3 * cols :]


def simple_call(kernel, inputs, outputs, scratch=(), scalars=()):
    return pl.pallas_call(
        kernel,
        out_shape=tuple(outputs),
        in_specs=[pl.BlockSpec(memory_space=pltpu.SMEM)] * len(scalars)
        + [pl.BlockSpec(memory_space=pltpu.VMEM)] * len(inputs),
        out_specs=tuple(pl.BlockSpec(memory_space=pltpu.VMEM) for _ in outputs),
        scratch_shapes=list(scratch),
        cost_estimate=pl.CostEstimate(flops=0, transcendentals=0, bytes_accessed=0),
        compiler_params=pltpu.CompilerParams(vmem_limit_bytes=48 * 1024 * 1024),
    )(*scalars, *inputs)


def rows_grads(at, first, second):
    if at.ns != 2:
        return jnp.stack([first, second]).astype(f32)
    _, rows, cols = first[0].shape
    shape = shape_of(2, 4 * rows, cols, kind=f32)
    return simple_call(rows_kernel, [*first, *second], [shape], scalars=(at.position(),))[0]


def attention_grads(at, first, second, head_width):
    if at.ns != 2:
        both = jnp.swapaxes(jnp.stack([first, second]).astype(f32), 1, 2)
        qkv = both[:, : 3 * head_width].reshape(2, 3, head_width, -1)
        return jnp.swapaxes(qkv, 2, 3), both[:, 3 * head_width :]
    _, rows, cols = first[0].shape
    qkv, out = simple_call(
        turned_kernel,
        [*first, *second],
        [
            shape_of(2, 3, head_width, 4 * rows, kind=f32),
            shape_of(2, head_width, 4 * rows, kind=f32),
        ],
        scratch=[pltpu.VMEM((2, 4 * rows, cols), f32)],
        scalars=(at.position(),),
    )
    return jnp.swapaxes(qkv, 2, 3), out


def prepare_kernel(qkv_ref, out_ref, target):
    for b in range(2):
        rows = [qkv_ref[b, number].T for number in range(3)] + [out_ref[b].T]
        target[b] = jnp.concatenate(rows, axis=1)


def attention_weights(w_qkv, w_out):
    _, _, rows, cols = w_qkv.shape
    return simple_call(
        prepare_kernel, [jnp.swapaxes(w_qkv, 2, 3), w_out], [shape_of(2, rows, 4 * cols)]
    )[0]


def heads_of(values, number, head):
    start = number * 4 * HEAD_DIM + head * HEAD_DIM
    return values[:, start : start + HEAD_DIM]


def probs_of(query, key, temporal):
    scores = lax.dot_general(
        query, key, (((1,), (1,)), ((), ())), preferred_element_type=f32
    ) * (1.0 / math.sqrt(HEAD_DIM))
    if temporal:
        rows = lax.broadcasted_iota(jnp.int32, scores.shape, 0) % temporal
        cols = lax.broadcasted_iota(jnp.int32, scores.shape, 1) % temporal
        scores = jnp.where(rows == cols, scores, -jnp.inf)
    weights = jnp.exp(scores - jnp.max(scores, axis=-1, keepdims=True))
    return weights / jnp.sum(weights, axis=-1, keepdims=True)


def attend_kernel(qkv_ref, out_ref, *, temporal):
    values = qkv_ref[0]
    results = [jnp.zeros((values.shape[0], 12 * HEAD_DIM), bf16)]
    for head in range(4):
        probs = probs_of(heads_of(values, 0, head), heads_of(values, 1, head), temporal)
        results.append(
            jnp.dot(
                probs.astype(bf16), heads_of(values, 2, head), preferred_element_type=f32
            ).astype(bf16)
        )
    out_ref[0] = jnp.concatenate(results, axis=1)


def attend_back_kernel(qkv_ref, grad_ref, out_ref, *, temporal):
    factor = 1.0 / math.sqrt(HEAD_DIM)
    values = qkv_ref[0]
    grads = grad_ref[0]
    queries, keys, vals = [], [], []
    for head in range(4):
        query, key, value = (heads_of(values, number, head) for number in range(3))
        grad = heads_of(grads, 3, head)
        probs = probs_of(query, key, temporal)
        vals.append(
            lax.dot_general(
                probs.astype(bf16), grad, (((0,), (0,)), ((), ())), preferred_element_type=f32
            ).astype(bf16)
        )
        grad_probs = lax.dot_general(
            grad, value, (((1,), (1,)), ((), ())), preferred_element_type=f32
        )
        inner = jnp.sum(grad_probs * probs, axis=-1, keepdims=True)
        grad_scores = (probs * (grad_probs - inner)).astype(bf16)
        queries.append(
            (jnp.dot(grad_scores, key, preferred_element_type=f32) * factor).astype(bf16)
        )
        keys.append(
            (
                lax.dot_general(
                    grad_scores, query, (((0,), (0,)), ((), ())), preferred_element_type=f32
                )
                * factor
            ).astype(bf16)
        )
    zeros = jnp.zeros((values.shape[0], 4 * HEAD_DIM), bf16)
    out_ref[0] = jnp.concatenate(queries + keys + vals + [zeros], axis=1)


def call_attention(kernel, arrays, rows, temporal):
    shape = arrays[0].shape
    spec = pl.BlockSpec((1, rows, shape[2]), lambda i, j: (i, j, 0))
    return pl.pallas_call(
        partial(kernel, temporal=temporal),
        out_shape=shape_of(*shape),
        grid=(shape[0], shape[1] // rows),
        in_specs=[spec] * len(arrays),
        out_specs=spec,
        cost_estimate=pl.CostEstimate(flops=0, transcendentals=0, bytes_accessed=0),
        compiler_params=pltpu.CompilerParams(vmem_limit_bytes=48 * 1024 * 1024),
    )(*arrays)


SLOPE = math.sqrt(2.0 / math.pi)


def gelu(u):
    return 0.5 * u * (1.0 + jnp.tanh(SLOPE * (u + 0.044715 * (u * u * u))))


def gelu_slope(u):
    t = jnp.tanh(SLOPE * (u + 0.044715 * (u * u * u)))
    inner = SLOPE * (1.0 + 3.0 * 0.044715 * (u * u))
    return 0.5 * (1.0 + t) + 0.5 * u * (1.0 - t * t) * inner


def times_of(own, other, weight):
    left = jnp.concatenate([own[...], other[...]], axis=0)
    return jnp.dot(left, weight[0], preferred_element_type=f32)


def qkv_kernel(own, other, weight, bias, out):
    out[0] = (times_of(own, other, weight) + bias[0]).astype(bf16)


def plain_kernel(own, other, weight, out):
    out[0] = times_of(own, other, weight).astype(bf16)


def up_kernel(own, other, weight, bias, up, activated):
    values = times_of(own, other, weight) + bias[0]
    up[0] = values
    activated[0] = gelu(values).astype(bf16)


def up_back_kernel(own, other, weight, up, out, sums):
    values = (gelu_slope(up[0]) * times_of(own, other, weight)).astype(bf16)
    out[0] = values
    sums[0] = jnp.sum(values.astype(f32), axis=0, keepdims=True)


def back_kernel(left, weight, own, other, total):
    term = jnp.dot(left[0], weight[0], preferred_element_type=f32)
    rows = own.shape[0]

    @pl.when(pl.program_id(0) == 0)
    def _():
        total[...] = term

    @pl.when(pl.program_id(0) == 1)
    def _():
        own[...] = total[:rows] + term[:rows]
        other[...] = (total[rows:] + term[rows:]).astype(bf16)


def times(kernel, pair, weight, extra=(), outputs=()):
    rows = 2 * pair[0].shape[0]
    cols = weight.shape[2]
    return call(
        kernel,
        [(pair[0], True), (pair[1], True), (weight, False)] + [(e, False) for e in extra],
        [(shape_of(2, rows if tall else 1, cols, kind=kind), False) for tall, kind in outputs],
    )


def times_back(at, left, weight):
    rows, width = left.shape[1] // 2, weight.shape[2]
    own, other = call(
        back_kernel,
        [(left, False), (weight, False)],
        [(shape_of(rows, width, kind=f32), True), (shape_of(rows, width), True)],
        scratch=[pltpu.VMEM((2 * rows, width), f32)],
    )
    return own, at.core(other)


def normalized(values):
    average = jnp.mean(values, axis=-1, keepdims=True)
    centered = values - average
    inverse = lax.rsqrt(jnp.mean(centered * centered, axis=-1, keepdims=True) + 1e-06)
    return centered * inverse, inverse


def norm_back(grad, normal, inverse, factor):
    dn = grad * (1.0 + factor)
    return (
        dn
        - jnp.mean(dn, axis=-1, keepdims=True)
        - normal * jnp.mean(dn * normal, axis=-1, keepdims=True)
    ) * inverse


def token_sum(values):
    return jnp.sum(values, axis=0, keepdims=True)


def mod_of(mod, number):
    return mod[number : number + 1, :]


def enter_kernel(inputs, mod, hidden):
    normal, _ = normalized(inputs[...].astype(f32))
    hidden[...] = (normal * (1.0 + mod_of(mod, 1)) + mod_of(mod, 0)).astype(bf16)


def middle_kernel(own, got, inputs, mod, bias, attn, after, hidden):
    attn_out = own[...] + got[...].astype(f32) + bias[...]
    attn[...] = attn_out
    values = inputs[...].astype(f32) + mod_of(mod, 2) * attn_out
    after[...] = values
    normal, _ = normalized(values)
    hidden[...] = (normal * (1.0 + mod_of(mod, 4)) + mod_of(mod, 3)).astype(bf16)


def leave_kernel(own, got, after, mod, bias, mlp, result):
    mlp_out = own[...] + got[...].astype(f32) + bias[...]
    mlp[...] = mlp_out
    result[...] = (after[...] + mod_of(mod, 5) * mlp_out).astype(bf16)


def enter_back_kernel(grad_y, mlp, mod, grad_mlp, sums):
    grad = grad_y[...].astype(f32)
    values = (mod_of(mod, 5) * grad).astype(bf16)
    grad_mlp[...] = values
    sums[0:1] = token_sum(grad * mlp[...])
    sums[1:2] = token_sum(values.astype(f32))


def middle_back_kernel(own, got, after, grad_y, attn, mod, grad_after, grad_attn, sums):
    grad = own[...] + got[...].astype(f32)
    normal, inverse = normalized(after[...])
    sums[0:1] = token_sum(grad)
    sums[1:2] = token_sum(grad * normal)
    total = grad_y[...].astype(f32) + norm_back(grad, normal, inverse, mod_of(mod, 4))
    grad_after[...] = total
    values = (mod_of(mod, 2) * total).astype(bf16)
    grad_attn[...] = values
    sums[2:3] = token_sum(total * attn[...])
    sums[3:4] = token_sum(values.astype(f32))


def leave_back_kernel(own, got, inputs, grad_after, mod, grad_inputs, sums):
    grad = own[...] + got[...].astype(f32)
    normal, inverse = normalized(inputs[...].astype(f32))
    sums[0:1] = token_sum(grad)
    sums[1:2] = token_sum(grad * normal)
    grad_inputs[...] = (
        grad_after[...] + norm_back(grad, normal, inverse, mod_of(mod, 1))
    ).astype(bf16)


def forward_block(
    at, inputs, mod, weights, first, bias_qkv, bias_up, b_out, b_down, temporal, steps
):
    rows, width = inputs.shape
    for _ in range(steps[0]):
        inputs = weights.step(inputs)
    wide = shape_of(rows, width, kind=f32)
    low = shape_of(rows, width)
    (hidden,) = simple_call(enter_kernel, [inputs, mod], [low])
    hidden = (hidden, at.core(hidden))
    for _ in range(steps[1]):
        hidden = weights.step(hidden)
    w_attn, w_attn_t = weights.whole[first]
    (qkv,) = times(qkv_kernel, hidden, w_attn, [bias_qkv], [(True, bf16)])
    attended = call_attention(attend_kernel, [qkv], rows, temporal)
    own, got = times_back(at, attended, w_attn_t)
    attn, after, hidden_two = simple_call(
        middle_kernel, [own, got, inputs, mod, b_out], [wide, wide, low]
    )
    hidden_two = (hidden_two, at.core(hidden_two))
    for _ in range(steps[2]):
        hidden_two = weights.step(hidden_two)
    w_up = weights.whole[first + 1][0]
    up, activated = times(up_kernel, hidden_two, w_up, [bias_up], [(True, f32), (True, bf16)])
    for _ in range(steps[3]):
        activated = weights.step(activated)
    w_down_t = weights.whole[first + 2][1]
    own, got = times_back(at, activated, w_down_t)
    mlp, result = simple_call(leave_kernel, [own, got, after, mod, b_down], [wide, low])
    return result, (inputs, hidden, qkv, attended, attn, after, hidden_two, up, activated, mlp)


def backward_block(at, grad_y, kept, mod, weights, temporal, sums, plan):
    inputs, hidden, qkv, attended, attn, after, hidden_two, up, activated, mlp = kept
    (w_attn, w_attn_t), (_, w_up_t), (w_down, _) = weights
    rows, width = inputs.shape
    wide = shape_of(rows, width, kind=f32)
    low = shape_of(rows, width)
    grad_mlp, sums_m = simple_call(
        enter_back_kernel, [grad_y, mlp, mod], [low, shape_of(2, width, kind=f32)]
    )
    grad_mlp = (grad_mlp, at.core(grad_mlp))
    grad_mlp = sums.run(plan[0], grad_mlp, grad_mlp, [activated])
    grad_up, grad_b_up = times(
        up_back_kernel, grad_mlp, w_down, [up], [(True, bf16), (False, f32)]
    )
    grad_up = sums.run(plan[1], grad_up, hidden_two, [grad_up])
    own, got = times_back(at, grad_up, w_up_t)
    grad_after, grad_attn, sums_a = simple_call(
        middle_back_kernel,
        [own, got, after, grad_y, attn, mod],
        [wide, low, shape_of(4, width, kind=f32)],
    )
    grad_attn = (grad_attn, at.core(grad_attn))
    grad_attn = sums.run(plan[2], grad_attn)
    (grad_attended,) = times(plain_kernel, grad_attn, w_attn, [], [(True, bf16)])
    grad_attended = sums.run(plan[3], grad_attended)
    grad_qkv = call_attention(attend_back_kernel, [qkv, grad_attended], rows, temporal)
    last = (hidden + grad_attn, [grad_qkv, attended])
    own, got = times_back(at, grad_qkv, w_attn_t)
    own = sums.run(plan[4], own, *last)
    grad_inputs, sums_i = simple_call(
        leave_back_kernel,
        [own, got, inputs, grad_after, mod],
        [low, shape_of(2, width, kind=f32)],
    )
    grad_mod = jnp.concatenate(
        [sums_i[0], sums_i[1], sums_a[2], sums_a[0], sums_a[1], sums_m[0]]
    )
    grad_b_qkv = jnp.sum(grad_qkv, axis=1, dtype=f32)
    cols = grad_b_qkv.shape[1] // 4
    grad_bias = jnp.concatenate(
        [grad_b_qkv[:, :cols], grad_b_qkv[:, 2 * cols : 3 * cols], grad_b_up[:, 0]], axis=1
    )
    return grad_inputs, last, grad_bias, sums_a[3], sums_m[1], grad_mod


def body(
    video, cond, w_ada, b_ada, w_qkv, b_qv, w_out, b_out, w_up, b_up, w_down, b_down, cotangent
):
    at = Place()
    width = video.shape[-1]
    own_width = w_up.shape[1]
    head_width = w_qkv.shape[3]
    silu_value, silu_back = jax.vjp(jax.nn.silu, cond.astype(f32))
    cond_act = silu_value.astype(bf16)
    if at.ns == 2:
        other = at.swap_y(cond_act)
        cond_all = jnp.concatenate(
            [jnp.where(at.s == 0, cond_act, other), jnp.where(at.s == 0, other, cond_act)], axis=0
        )
    else:
        cond_all = lax.all_gather(cond_act, "shard", axis=0, tiled=True)
    cond_rows = lax.dynamic_slice_in_dim(cond_all, at.s * own_width, own_width, axis=1)
    mod_part = jnp.einsum("cd,bdn->cbn", cond_rows, w_ada, preferred_element_type=f32)
    if at.ns == 2:
        kept = lax.dynamic_index_in_dim(mod_part, at.s, 0, False)
        mod_part = kept + at.swap_y(lax.dynamic_index_in_dim(mod_part, 1 - at.s, 0, False))
    else:
        mod_part = lax.psum_scatter(mod_part, "shard", scatter_dimension=0, tiled=True)[0]
    ada_cols = w_ada.shape[2]
    small = jnp.concatenate(
        [mod_part + b_ada, b_qv.reshape(2, -1).astype(f32), b_up.astype(f32)], axis=1
    )

    small = at.gather_small(small)
    arrays = (attention_weights(w_qkv, w_out), w_up, jnp.swapaxes(w_down, 1, 2))
    frames = lax.all_to_all(video, "tp", split_axis=1, concat_axis=2, tiled=True)
    rows = frames.size // width
    arrays, frames = lax.optimization_barrier((arrays, frames))
    weights = Weights(at, arrays)
    small, frames = weights.step((small, frames))
    mods = jnp.moveaxis(small[:, :, :ada_cols], 0, 1).reshape(2, 6, width)
    biases = small[:, :, ada_cols:]
    biases = jnp.stack(
        [
            lax.dynamic_index_in_dim(biases, 2 * at.k, 0, False),
            lax.dynamic_index_in_dim(biases, 2 * at.k + 1, 0, False),
        ],
        axis=1,
    )
    zeros = jnp.zeros((2, 2, head_width), f32)
    bias_qkv = jnp.concatenate(
        [biases[:, :, :head_width], zeros, biases[:, :, head_width : 2 * head_width], zeros], axis=2
    )[:, :, None]
    bias_up = biases[:, :, None, 2 * head_width :]
    b_out_row, b_down_row = (v.astype(f32)[:, None] for v in (b_out, b_down))

    frames = weights.step(frames)
    inputs = frames.reshape(rows, width)
    middle, kept_one = forward_block(
        at,
        inputs,
        mods[0],
        weights,
        0,
        bias_qkv[0],
        bias_up[0],
        b_out_row[0],
        b_down_row[0],
        0,
        (0, 1, 1, 1),
    )
    moved = lax.all_to_all(
        middle.reshape(frames.shape), "tp", split_axis=2, concat_axis=1, tiled=True
    )
    middle = weights.step(middle)
    moved, middle = lax.optimization_barrier((moved, middle))
    moved = lax.all_to_all(moved, "ctx", split_axis=3, concat_axis=1, tiled=True)
    grid = moved.shape
    patches = grid[2] * grid[3]
    result, kept_two = forward_block(
        at,
        moved.reshape(rows, width),
        mods[1],
        weights,
        3,
        bias_qkv[1],
        bias_up[1],
        b_out_row[1],
        b_down_row[1],
        patches,
        (1, 0, 0, 1),
    )
    first, second = weights.whole[:3], weights.whole[3:]
    sums = Sums(at)
    grad_moved, last, *small_two = backward_block(
        at,
        cotangent.reshape(rows, width),
        kept_two,
        mods[1],
        second,
        patches,
        sums,
        ("p:d2 1:d2", "p:u2", "2:d2", "z:d2 1:u2", "p:a2 2:u2"),
    )
    grad_middle = lax.all_to_all(
        grad_moved.reshape(grid), "ctx", split_axis=1, concat_axis=3, tiled=True
    )
    grad_moved = sums.run("z:u2", grad_moved)
    grad_middle, grad_moved = lax.optimization_barrier((grad_middle, grad_moved))
    grad_moved = sums.run("f:d2 1:a2", grad_moved)
    grad_middle, grad_moved = lax.optimization_barrier((grad_middle, grad_moved))
    grad_middle = lax.all_to_all(grad_middle, "tp", split_axis=1, concat_axis=2, tiled=True)
    grad_middle = sums.run("2:a2", grad_middle)
    grad_frames, last, *small_one = backward_block(
        at,
        grad_middle.reshape(rows, width),
        kept_one,
        mods[0],
        first,
        0,
        sums,
        (
            "p:d1",
            "p:u1 z:a2 f:u2 1:d1",
            "2:d1 e:d2",
            "z:d1 f:a2 1:u1 e:u2",
            "p:a1 2:u1",
        ),
    )
    grad_video = lax.all_to_all(
        grad_frames.reshape(frames.shape), "tp", split_axis=2, concat_axis=1, tiled=True
    ).astype(f32)

    grad_bias, grad_b_out, grad_b_down, grad_mod = (
        jnp.stack([one, two]) for one, two in zip(small_one, small_two)
    )
    blocks = jnp.arange(at.nt)[:, None, None]
    grad_bias = jnp.where(blocks == 2 * at.k, grad_bias[:, 0], 0.0) + jnp.where(
        blocks == 2 * at.k + 1, grad_bias[:, 1], 0.0
    )
    small = jnp.concatenate(
        [grad_bias.reshape(-1), grad_b_out.reshape(-1), grad_b_down.reshape(-1)]
    )
    order = ("z:u1 f:d1 1:a1 e:a2", "2:a1 e:d1", "z:a1 f:u1", "e:u1", "f:a1", "e:a1")
    small, grad_mods = at.sum_all(
        small, grad_mod.reshape(-1), [partial(sums.run, text) for text in order[:3]]
    )
    size = grad_bias.size
    grad_bias = lax.dynamic_index_in_dim(small[:size].reshape(grad_bias.shape), at.t, 0, False)
    grad_b_out, grad_b_down = small[size:].reshape(2, 2, width)
    grad_mods = jnp.moveaxis(grad_mods.reshape(at.ns, 2, 6 * width), 0, 1)
    for name in order[3:]:
        sums.run(name, ())
    sums = sums.done
    grad_mods = lax.dynamic_slice_in_dim(grad_mods, at.t * ada_cols, ada_cols, axis=2)
    cond_rows = cond_rows.astype(f32)
    grad_w_ada = sum(
        cond_rows[i][None, :, None] * grad_mods[:, i][:, None, :] for i in range(at.ns)
    )
    grad_b_ada = jnp.sum(grad_mods, axis=1)
    grad_act = jnp.einsum(
        "bcn,bdn->cd", grad_mods, w_ada.astype(f32), precision=highest, preferred_element_type=f32
    )
    if at.ns == 2:
        grad_act = at.sum_group(at.sum_group(grad_act, "tp", 1), "tp", 2)
        ours = lax.dynamic_slice_in_dim(grad_act, at.s, 1, axis=0)
        theirs = at.swap_y(lax.dynamic_slice_in_dim(grad_act, 1 - at.s, 1, axis=0))
        grad_act = jnp.concatenate(
            [jnp.where(at.s == 0, ours, theirs), jnp.where(at.s == 0, theirs, ours)], axis=1
        )
    else:
        grad_act = lax.psum_scatter(
            lax.dynamic_update_slice_in_dim(
                jnp.zeros((at.ns, width), f32), grad_act, at.s * own_width, axis=1
            ),
            "shard",
            scatter_dimension=0,
            tiled=True,
        )
        grad_act = lax.psum(grad_act, "tp")
    grad_cond = silu_back(grad_act)[0]

    grad_w_qkv, grad_w_out = attention_grads(at, sums["a1"], sums["a2"], head_width)
    return (
        result.reshape(grid),
        grad_video,
        grad_cond,
        grad_w_ada,
        grad_b_ada,
        grad_w_qkv,
        grad_bias[:, : 2 * head_width].reshape(2, 2, head_width),
        grad_w_out,
        grad_b_out,
        rows_grads(at, sums["u1"], sums["u2"]),
        grad_bias[:, 2 * head_width :],
        jnp.swapaxes(rows_grads(at, sums["d1"], sums["d2"]), 1, 2),
        grad_b_down,
    )


def solution(mesh):
    in_specs = (
        P("shard", "ctx", "tp", None, None),
        P("shard", None),
        P(None, "shard", "tp"),
        P(None, "tp"),
        P(None, None, "shard", "tp"),
        P(None, None, "tp"),
        P(None, "tp", "shard"),
        P(),
        P(None, "shard", "tp"),
        P(None, "tp"),
        P(None, "tp", "shard"),
        P(),
        P("shard", None, "tp", "ctx", None),
    )
    out_specs = (
        P("shard", None, "tp", "ctx", None),
        P("shard", "ctx", "tp", None, None),
        P("shard", None),
        P(None, "shard", "tp"),
        P(None, "tp"),
        P(None, None, "shard", "tp"),
        P(None, None, "tp"),
        P(None, "tp", "shard"),
        P(),
        P(None, "shard", "tp"),
        P(None, "tp"),
        P(None, "tp", "shard"),
        P(),
    )
    return jax.shard_map(body, mesh=mesh, in_specs=in_specs, out_specs=out_specs, check_vma=False)
```

```python
from functools import partial
import math

import jax
import jax.numpy as jnp
from jax import lax
from jax.experimental import pallas as pl
from jax.experimental.pallas import tpu as pltpu
from jax.sharding import PartitionSpec as P

HEAD_DIM = 72
bf16 = jnp.bfloat16
f32 = jnp.float32
highest = lax.Precision.HIGHEST


class Place:
    def __init__(self):
        self.ns = lax.axis_size("shard")
        self.nc = lax.axis_size("ctx")
        self.nt = lax.axis_size("tp")
        self.s = lax.axis_index("shard")
        self.c = lax.axis_index("ctx")
        self.t = lax.axis_index("tp")
        self.x = self.c // 2
        self.k = self.c % 2
        self.d = jnp.where(self.k == 0, self.t, self.nt - 1 - self.t)

    def core(self, v):
        return lax.ppermute(v, "ctx", [(c, c ^ 1) for c in range(self.nc)])

    def swap_x(self, v):
        return lax.ppermute(v, "ctx", [(c, c ^ 2) for c in range(self.nc)])

    def swap_y(self, v):
        return lax.ppermute(v, "shard", [(i, i ^ 1) for i in range(self.ns)])

    def along_z(self, v, pairs):
        def at(c, d):
            return c * self.nt + (d if c % 2 == 0 else self.nt - 1 - d)

        return lax.ppermute(
            v, ("ctx", "tp"), [(at(c, i), at(c, j)) for c in range(self.nc) for i, j in pairs]
        )

    def gather_small(self, v):
        got = [v] + [
            lax.ppermute(v, "tp", [(i, i ^ step) for i in range(self.nt)])
            for step in range(1, self.nt)
        ]
        return jnp.stack([pick(self.t ^ i, got) for i in range(self.nt)])

    def sum_group(self, v, axis, step):
        size = self.nc if axis == "ctx" else self.nt
        return v + lax.ppermute(v, axis, [(i, i ^ step) for i in range(size)])

    def sum_all(self, v, per_clip, run):
        size = v.size
        v = jnp.concatenate([v, per_clip]).reshape(1, -1)
        v = run("C0", self.sum_group(v, "ctx", 1))
        v = run("C1", self.sum_group(v, "ctx", 2))
        v = run("C2", self.sum_group(v, "tp", 1))
        v = run("C3", self.sum_group(v, "tp", 2))
        if self.ns != 2:
            return lax.psum(v[0, :size], "shard"), lax.all_gather(
                v[:, size:], "shard", axis=0, tiled=True
            )
        v, w = run("C4", (v, self.swap_y(v)))
        rows = [jnp.where(self.s == 0, v, w), jnp.where(self.s == 0, w, v)]
        return (v + w)[0, :size], jnp.concatenate(rows, axis=0)[:, size:]

    def position(self):
        return jnp.stack([self.s, self.x, self.k]).astype(jnp.int32)

    def by_x(self, near, far):
        return [jnp.where(self.x == 0, near, far), jnp.where(self.x == 0, far, near)]

    def by_k(self, near, far):
        return [jnp.where(self.k == 0, near, far), jnp.where(self.k == 0, far, near)]


def pick(index, options):
    out = options[-1]
    for number in range(len(options) - 2, -1, -1):
        out = jnp.where(index == number, options[number], out)
    return out


def tie(values, *others):
    return lax.optimization_barrier((values, others))[0]


class Chunk:
    def __init__(self, first, common, part):
        self.first = first
        self.common = common
        self.part = part
        self.rows = common + 2 * part

    def sent(self, at, both, b):
        half, part = self.common // 2, self.part // 2
        starts = (self.first + at.k * half, self.first + self.common + at.x * self.part + at.k * part)
        cols = both.shape[2]
        return jnp.concatenate(
            [
                lax.dynamic_slice(both, (b, start, 0), (1, size, cols))[0]
                for start, size in zip(starts, (half, part))
                if size
            ],
            axis=0,
        )

    def core_step(self, at, blocks):
        got = at.core(lax.dynamic_slice_in_dim(blocks, 2 - 2 * at.k, 2, axis=0))
        mine = lax.dynamic_slice_in_dim(blocks, 2 * at.k, 2, axis=0)
        half = self.common // 2
        common = jnp.where(at.x == at.k, mine[:, :half], got[:, :half])
        if not self.part:
            return (mine, got), common
        part = jnp.concatenate([mine[:, half:], got[:, half:]], axis=1)
        return (mine, got), jnp.concatenate([common, part], axis=1), part


def assemble_kernel(place_ref, *refs, chunk):
    out_ref, turned_ref = refs[-2:]
    s, x, k = place_ref[0], place_ref[1], place_ref[2]
    width = out_ref.shape[1] // 2

    def copy(source, start, size, offset):
        if size:
            out_ref[0, pl.ds(pl.multiple_of(offset, 16), size), :] = source[
                0, start : start + size, :
            ]

    mine, got, near, far = refs[:4]
    side = refs[4] if chunk.part else None
    half, part = chunk.common // 2, chunk.part // 2
    own, other = s * width, (1 - s) * width

    def parts(source, start, base, plane):
        offset = base + chunk.common + plane * chunk.part
        copy(source, start, part, offset + k * part)
        copy(source, start + part, part, offset + (1 - k) * part)

    copy(mine, 0, half, own + k * half)
    copy(got, 0, half, own + (1 - k) * half)
    copy(mine, half, part, own + chunk.common + x * chunk.part + k * part)
    copy(got, half, part, own + chunk.common + x * chunk.part + (1 - k) * part)
    parts(side, 0, own, 1 - x)
    copy(near, 0, half, other + x * half)
    parts(near, half, other, x)
    copy(far, 0, half, other + (1 - x) * half)
    parts(far, half, other, 1 - x)
    turned_ref[0] = out_ref[0].T


def assemble(at, chunk, arrays):
    cols = arrays[0].shape[2]
    rows = 2 * chunk.rows
    return call(
        partial(assemble_kernel, chunk=chunk),
        [(a, False) for a in arrays],
        [(shape_of(2, rows, cols), False), (shape_of(2, cols, rows), False)],
        scalars=(at.position(),),
    )


class Weights:
    def __init__(self, at, arrays):
        self.at = at
        self.whole = []
        self.count = 2 * len(arrays)
        self.number = 0
        jobs = [(b, array) for b in range(2) for array in arrays]
        if at.ns != 2:
            for b, array in jobs:
                both = lax.all_gather(array[b], "tp", axis=0)
                both = lax.dynamic_slice_in_dim(both, 2 * at.k, 2, axis=0)
                both = lax.all_gather(both, "shard", axis=1, tiled=True)
                self.whole.append((both, jnp.swapaxes(both, 1, 2)))
            return
        rows = arrays[0].shape[1]
        self.plans = [
            Chunk(0, rows - 2 * part, part)
            for part in (rows // 36 * units for units in (14, 10, 8, 8, 6, 0))
        ]
        self.blocks = []
        sent = ()
        for plan, (b, array) in zip(self.plans, jobs):
            sent = plan.sent(at, tie(array, sent), b)
            self.blocks.append(lax.all_gather(sent, "tp", axis=0))
        self.held, self.near, self.far, self.side = {}, {}, {}, {}

    def step(self, main):
        if self.at.ns != 2 or self.number == self.count + 2:
            return main
        at, number = self.at, self.number
        self.number += 1
        block = self.blocks[number] if number < self.count else ()
        block, near, far, side, main = lax.optimization_barrier(
            (
                block,
                self.near.get(number - 1),
                self.far.get(number - 2),
                self.side.get(number - 1),
                main,
            )
        )
        if 0 < number <= self.count:
            self.near[number - 1], self.side[number - 1] = near, side
            self.far[number - 1] = at.swap_x(near)
        if number < self.count:
            self.held[number], *messages = self.plans[number].core_step(at, block)
            messages, main = lax.optimization_barrier((messages, main))
            self.near[number] = at.swap_y(messages[0])
            self.side[number] = at.swap_x(messages[-1]) if self.plans[number].part else ()
        if number > 1:
            m = number - 2
            sides = [self.side[m]] if self.plans[m].part else []
            arrays = [*self.held[m], self.near[m], far, *sides]
            self.whole.append(assemble(at, self.plans[m], arrays))
        return main


def scatter_z(everything):
    return lax.psum_scatter(everything, "tp", scatter_dimension=0, tiled=True)[0]


def product(left, right):
    left = jnp.concatenate(left, axis=0)
    right = jnp.concatenate(right, axis=1)
    return jnp.einsum("rd,prn->pdn", left, right, preferred_element_type=f32).astype(bf16)


def term_of(turned, right, starts, rows):
    left = [turned[pl.ds(pl.multiple_of(start, 16), rows), :] for start in starts]
    left = jnp.concatenate(left, axis=0)
    depth = right[0].shape[1]
    return sum(
        jnp.dot(left[:, i * depth : (i + 1) * depth], r[0], preferred_element_type=f32)
        for i, r in enumerate(right)
    )


def starts_of(place_ref, width, pairs, half):
    s, x = place_ref[0], place_ref[1]
    return [
        (4 * jnp.abs(s - ds) + 2 * jnp.abs(x - dx) + half) * (width // 8) for ds, dx in pairs
    ]


def away_kernel(place_ref, *refs, count):
    left, right = refs[:count], refs[count:-3]
    to_y, to_x, turned = refs[-3:]
    rows = left[0].shape[0]
    width = turned.shape[0]

    @pl.when(pl.program_id(0) == 0)
    def _():
        for i, source in enumerate(left):
            turned[:, i * rows : (i + 1) * rows] = source[...].T

    first = starts_of(place_ref, width, ((1, 0), (1, 1)), 0)
    second = starts_of(place_ref, width, ((0, 1), (1, 1)), 1)
    to_y[0] = term_of(turned, right, first, width // 8).astype(bf16)
    to_x[0] = term_of(turned, right, second, width // 8).astype(bf16)


def here_kernel(place_ref, from_y, from_x, turned, *refs):
    right = refs[:-4]
    over_y, over_x, to_x, to_y = refs[-4:]
    width = turned.shape[0]
    rows = width // 8
    first = starts_of(place_ref, width, ((0, 0), (0, 1)), 0)
    second = starts_of(place_ref, width, ((0, 0), (1, 0)), 1)
    one = term_of(turned, right, first, rows) + from_y[0].astype(f32)
    over_y[0] = one[:rows].astype(bf16)
    to_x[0] = one[rows:].astype(bf16)
    two = term_of(turned, right, second, rows) + from_x[0].astype(f32)
    over_x[0] = two[:rows].astype(bf16)
    to_y[0] = two[rows:].astype(bf16)


def join_kernel(place_ref, over_y, over_x, from_x, from_y, kept, given):
    k = place_ref[2]
    for out, flag in ((kept, k == 0), (given, k == 1)):

        @pl.when(flag)
        def _():
            out[0] = (over_y[0].astype(f32) + from_x[0].astype(f32)).astype(bf16)

        @pl.when(jnp.logical_not(flag))
        def _():
            out[0] = (over_x[0].astype(f32) + from_y[0].astype(f32)).astype(bf16)


def per_block(array):
    return pl.BlockSpec((1,) + array.shape[1:], lambda i: (i,) + (0,) * (len(array.shape) - 1))


def entire(array):
    return pl.BlockSpec(array.shape, lambda i: (0,) * len(array.shape))


def call(kernel, inputs, outputs, scratch=(), scalars=()):
    return pl.pallas_call(
        kernel,
        out_shape=tuple(a for a, _ in outputs),
        grid=(2,),
        in_specs=[pl.BlockSpec(memory_space=pltpu.SMEM)] * len(scalars)
        + [entire(a) if whole else per_block(a) for a, whole in inputs],
        out_specs=tuple(entire(a) if whole else per_block(a) for a, whole in outputs),
        scratch_shapes=list(scratch),
        cost_estimate=pl.CostEstimate(flops=0, transcendentals=0, bytes_accessed=0),
        compiler_params=pltpu.CompilerParams(vmem_limit_bytes=48 * 1024 * 1024),
    )(*scalars, *[a for a, _ in inputs])


def shape_of(*dims, kind=bf16):
    return jax.ShapeDtypeStruct(dims, kind)


def products_away(at, left, right):
    rows, width = left[0].shape
    sent = shape_of(2, width // 4, right[0].shape[2])
    return call(
        partial(away_kernel, count=len(left)),
        [(l, True) for l in left] + [(r, False) for r in right],
        [(sent, False), (sent, False), (shape_of(width, rows * len(left)), True)],
        scalars=(at.position(),),
    )


def products_here(at, turned, right, from_y, from_x):
    part = shape_of(2, from_y.shape[1] // 2, from_y.shape[2])
    return call(
        here_kernel,
        [(from_y, False), (from_x, False), (turned, True)] + [(r, False) for r in right],
        [(part, False)] * 4,
        scalars=(at.position(),),
    )


def join_halves(at, *parts):
    return call(
        join_kernel,
        [(part, False) for part in parts],
        [(shape_of(*parts[0].shape), False)] * 2,
        scalars=(at.position(),),
    )


PLAN = {
    "A0": ("pD", "1D"),
    "A1": ("pU",),
    "A2": ("2D", "1U"),
    "A3": (),
    "A4": ("pA",),
    "A5": (),
    "A6": ("2U", "1A", "zD"),
    "A7": (),
    "B0": ("pd", "2A", "1d", "zU", "fD"),
    "B1": ("pu",),
    "B2": (),
    "B3": (),
    "B4": ("2d", "1u", "zA", "fU"),
    "C0": (),
    "C1": ("eD", "pa", "fA", "2u", "1a", "zd", "eU"),
    "C2": (),
    "C3": (),
    "C4": ("2a", "zu", "fd"),
    "C5": ("za",),
    "C6": (),
    "C7": ("fu", "ed", "fa", "eA", "ea", "eu"),
}


class Sums:
    def __init__(self, at):
        self.at = at
        self.state = {}
        self.done = {}

    def offer(self, name, left, right):
        self.state[name] = (None, (list(left), list(right)))

    def run(self, place, main):
        for step in PLAN[place]:
            kind, name = step
            if name not in self.state:
                continue
            kept, pending = self.state.pop(name)
            pending, main = lax.optimization_barrier((pending, main))
            if kind == "w":
                self.state[name] = (kept, pending)
                continue
            if self.at.ns != 2:
                self.done[name] = self.generic(*pending)
                continue
            kept, messages = getattr(self, "step_" + kind)(kept, pending)
            values, main = lax.optimization_barrier(([value for _, value in messages], main))
            if kind == "e":
                self.done[name] = values
            else:
                sent = [value if how is None else how(value) for (how, _), value in zip(messages, values)]
                self.state[name] = (kept, sent)
        return main

    def generic(self, left, right):
        at = self.at
        summed = lax.psum_scatter(
            product(left, right), "shard", scatter_dimension=1, tiled=True
        )
        half = summed.shape[1] // 2
        halves = [summed[:, :half], summed[:, half:]]
        got = at.core(jnp.where(at.k == 0, halves[1], halves[0]))
        kept = jnp.where(at.k == 0, halves[0], halves[1])
        mine = scatter_z(jnp.concatenate(at.by_k(kept, got), axis=0))
        mine = (mine.astype(f32) + at.swap_x(mine).astype(f32)).astype(bf16)
        return jnp.concatenate(at.by_k(mine, at.core(mine)), axis=0)

    def step_p(self, _, pending):
        left, right = pending
        to_y, to_x, turned = products_away(self.at, left, right)
        return (right, turned), [(None, to_y), (None, to_x)]

    def step_1(self, kept, pending):
        to_y, to_x = pending
        return kept, [(self.at.swap_y, to_y), (self.at.swap_x, to_x)]

    def step_2(self, kept, pending):
        right, turned = kept
        over_y, over_x, to_x, to_y = products_here(self.at, turned, right, *pending)
        return (over_y, over_x), [(self.at.swap_x, to_x), (self.at.swap_y, to_y)]

    def step_z(self, kept, pending):
        kept, given = join_halves(self.at, *kept, *pending)
        everything = jnp.concatenate(self.at.by_k(kept, self.at.core(given)), axis=0)
        return None, [(scatter_z, everything)]

    def step_f(self, _, pending):
        (mine,) = pending
        return mine, [(self.at.swap_x, mine)]

    def step_e(self, mine, pending):
        (far,) = pending
        mine = jnp.stack(self.at.by_x(mine, far))
        return None, [(None, mine), (None, self.at.core(mine))]


def rows_in_place(place_ref, mine, theirs, target, b):
    k = place_ref[2]
    rows = mine.shape[1]
    for ref, member in ((mine, k), (theirs, 1 - k)):
        for x in range(2):
            start = pl.multiple_of((2 * x + member) * rows, 8)
            target[b, pl.ds(start, rows), :] = ref[x].astype(f32)


def rows_kernel(place_ref, *refs):
    for b in range(2):
        rows_in_place(place_ref, refs[2 * b], refs[2 * b + 1], refs[4], b)


def turned_kernel(place_ref, *refs):
    qkv_ref, out_ref, target = refs[4:]
    cols = out_ref.shape[1]
    for b in range(2):
        rows_in_place(place_ref, refs[2 * b], refs[2 * b + 1], target, b)
        values = target[b].T
        for number in range(3):
            qkv_ref[b, number] = values[number * cols : (number + 1) * cols]
        out_ref[b] = values[3 * cols :]


def simple_call(kernel, inputs, outputs, scratch=(), scalars=()):
    return pl.pallas_call(
        kernel,
        out_shape=tuple(outputs),
        in_specs=[pl.BlockSpec(memory_space=pltpu.SMEM)] * len(scalars)
        + [pl.BlockSpec(memory_space=pltpu.VMEM)] * len(inputs),
        out_specs=tuple(pl.BlockSpec(memory_space=pltpu.VMEM) for _ in outputs),
        scratch_shapes=list(scratch),
        cost_estimate=pl.CostEstimate(flops=0, transcendentals=0, bytes_accessed=0),
        compiler_params=pltpu.CompilerParams(vmem_limit_bytes=48 * 1024 * 1024),
    )(*scalars, *inputs)


def rows_grads(at, first, second):
    if at.ns != 2:
        return jnp.stack([first, second]).astype(f32)
    _, rows, cols = first[0].shape
    shape = shape_of(2, 4 * rows, cols, kind=f32)
    return simple_call(rows_kernel, [*first, *second], [shape], scalars=(at.position(),))[0]


def attention_grads(at, first, second, head_width):
    if at.ns != 2:
        both = jnp.swapaxes(jnp.stack([first, second]).astype(f32), 1, 2)
        qkv = both[:, : 3 * head_width].reshape(2, 3, head_width, -1)
        return jnp.swapaxes(qkv, 2, 3), both[:, 3 * head_width :]
    _, rows, cols = first[0].shape
    qkv, out = simple_call(
        turned_kernel,
        [*first, *second],
        [
            shape_of(2, 3, head_width, 4 * rows, kind=f32),
            shape_of(2, head_width, 4 * rows, kind=f32),
        ],
        scratch=[pltpu.VMEM((2, 4 * rows, cols), f32)],
        scalars=(at.position(),),
    )
    return jnp.swapaxes(qkv, 2, 3), out


def prepare_kernel(qkv_ref, out_ref, target):
    for b in range(2):
        rows = [qkv_ref[b, number].T for number in range(3)] + [out_ref[b].T]
        target[b] = jnp.concatenate(rows, axis=1)


def attention_weights(w_qkv, w_out):
    _, _, rows, cols = w_qkv.shape
    return simple_call(
        prepare_kernel, [jnp.swapaxes(w_qkv, 2, 3), w_out], [shape_of(2, rows, 4 * cols)]
    )[0]


def heads_of(values, number, head):
    start = number * 4 * HEAD_DIM + head * HEAD_DIM
    return values[:, start : start + HEAD_DIM]


def probs_of(query, key, temporal):
    scores = lax.dot_general(
        query, key, (((1,), (1,)), ((), ())), preferred_element_type=f32
    ) * (1.0 / math.sqrt(HEAD_DIM))
    if temporal:
        rows = lax.broadcasted_iota(jnp.int32, scores.shape, 0) % temporal
        cols = lax.broadcasted_iota(jnp.int32, scores.shape, 1) % temporal
        scores = jnp.where(rows == cols, scores, -jnp.inf)
    weights = jnp.exp(scores - jnp.max(scores, axis=-1, keepdims=True))
    return weights / jnp.sum(weights, axis=-1, keepdims=True)


def attend_kernel(qkv_ref, out_ref, *, temporal):
    values = qkv_ref[0]
    results = [jnp.zeros((values.shape[0], 12 * HEAD_DIM), bf16)]
    for head in range(4):
        probs = probs_of(heads_of(values, 0, head), heads_of(values, 1, head), temporal)
        results.append(
            jnp.dot(
                probs.astype(bf16), heads_of(values, 2, head), preferred_element_type=f32
            ).astype(bf16)
        )
    out_ref[0] = jnp.concatenate(results, axis=1)


def attend_back_kernel(qkv_ref, grad_ref, out_ref, *, temporal):
    factor = 1.0 / math.sqrt(HEAD_DIM)
    values = qkv_ref[0]
    grads = grad_ref[0]
    queries, keys, vals = [], [], []
    for head in range(4):
        query, key, value = (heads_of(values, number, head) for number in range(3))
        grad = heads_of(grads, 3, head)
        probs = probs_of(query, key, temporal)
        vals.append(
            lax.dot_general(
                probs.astype(bf16), grad, (((0,), (0,)), ((), ())), preferred_element_type=f32
            ).astype(bf16)
        )
        grad_probs = lax.dot_general(
            grad, value, (((1,), (1,)), ((), ())), preferred_element_type=f32
        )
        inner = jnp.sum(grad_probs * probs, axis=-1, keepdims=True)
        grad_scores = (probs * (grad_probs - inner)).astype(bf16)
        queries.append(
            (jnp.dot(grad_scores, key, preferred_element_type=f32) * factor).astype(bf16)
        )
        keys.append(
            (
                lax.dot_general(
                    grad_scores, query, (((0,), (0,)), ((), ())), preferred_element_type=f32
                )
                * factor
            ).astype(bf16)
        )
    zeros = jnp.zeros((values.shape[0], 4 * HEAD_DIM), bf16)
    out_ref[0] = jnp.concatenate(queries + keys + vals + [zeros], axis=1)


def call_attention(kernel, arrays, rows, temporal):
    shape = arrays[0].shape
    spec = pl.BlockSpec((1, rows, shape[2]), lambda i, j: (i, j, 0))
    return pl.pallas_call(
        partial(kernel, temporal=temporal),
        out_shape=shape_of(*shape),
        grid=(shape[0], shape[1] // rows),
        in_specs=[spec] * len(arrays),
        out_specs=spec,
        cost_estimate=pl.CostEstimate(flops=0, transcendentals=0, bytes_accessed=0),
        compiler_params=pltpu.CompilerParams(vmem_limit_bytes=48 * 1024 * 1024),
    )(*arrays)


SLOPE = math.sqrt(2.0 / math.pi)


def gelu(u):
    return 0.5 * u * (1.0 + jnp.tanh(SLOPE * (u + 0.044715 * (u * u * u))))


def gelu_slope(u):
    t = jnp.tanh(SLOPE * (u + 0.044715 * (u * u * u)))
    inner = SLOPE * (1.0 + 3.0 * 0.044715 * (u * u))
    return 0.5 * (1.0 + t) + 0.5 * u * (1.0 - t * t) * inner


def times_of(own, other, weight):
    left = jnp.concatenate([own[...], other[...]], axis=0)
    return jnp.dot(left, weight[0], preferred_element_type=f32)


def qkv_kernel(own, other, weight, bias, out):
    out[0] = (times_of(own, other, weight) + bias[0]).astype(bf16)


def plain_kernel(own, other, weight, out):
    out[0] = times_of(own, other, weight).astype(bf16)


def up_kernel(own, other, weight, bias, up, activated):
    values = times_of(own, other, weight) + bias[0]
    up[0] = values
    activated[0] = gelu(values).astype(bf16)


def up_back_kernel(own, other, weight, up, out, sums):
    values = (gelu_slope(up[0]) * times_of(own, other, weight)).astype(bf16)
    out[0] = values
    sums[0] = jnp.sum(values.astype(f32), axis=0, keepdims=True)


def back_kernel(left, weight, own, other, total):
    term = jnp.dot(left[0], weight[0], preferred_element_type=f32)
    rows = own.shape[0]

    @pl.when(pl.program_id(0) == 0)
    def _():
        total[...] = term

    @pl.when(pl.program_id(0) == 1)
    def _():
        own[...] = total[:rows] + term[:rows]
        other[...] = (total[rows:] + term[rows:]).astype(bf16)


def times(kernel, pair, weight, extra=(), outputs=()):
    rows = 2 * pair[0].shape[0]
    cols = weight.shape[2]
    return call(
        kernel,
        [(pair[0], True), (pair[1], True), (weight, False)] + [(e, False) for e in extra],
        [(shape_of(2, rows if tall else 1, cols, kind=kind), False) for tall, kind in outputs],
    )


def times_back(at, left, weight):
    rows, width = left.shape[1] // 2, weight.shape[2]
    own, other = call(
        back_kernel,
        [(left, False), (weight, False)],
        [(shape_of(rows, width, kind=f32), True), (shape_of(rows, width), True)],
        scratch=[pltpu.VMEM((2 * rows, width), f32)],
    )
    return own, at.core(other)


def normalized(values):
    average = jnp.mean(values, axis=-1, keepdims=True)
    centered = values - average
    inverse = lax.rsqrt(jnp.mean(centered * centered, axis=-1, keepdims=True) + 1e-06)
    return centered * inverse, inverse


def norm_back(grad, normal, inverse, factor):
    dn = grad * (1.0 + factor)
    return (
        dn
        - jnp.mean(dn, axis=-1, keepdims=True)
        - normal * jnp.mean(dn * normal, axis=-1, keepdims=True)
    ) * inverse


def token_sum(values):
    return jnp.sum(values, axis=0, keepdims=True)


def mod_of(mod, number):
    return mod[number : number + 1, :]


def enter_kernel(inputs, mod, hidden):
    normal, _ = normalized(inputs[...].astype(f32))
    hidden[...] = (normal * (1.0 + mod_of(mod, 1)) + mod_of(mod, 0)).astype(bf16)


def middle_kernel(own, got, inputs, mod, bias, attn, after, hidden):
    attn_out = own[...] + got[...].astype(f32) + bias[...]
    attn[...] = attn_out
    values = inputs[...].astype(f32) + mod_of(mod, 2) * attn_out
    after[...] = values
    normal, _ = normalized(values)
    hidden[...] = (normal * (1.0 + mod_of(mod, 4)) + mod_of(mod, 3)).astype(bf16)


def leave_kernel(own, got, after, mod, bias, mlp, result):
    mlp_out = own[...] + got[...].astype(f32) + bias[...]
    mlp[...] = mlp_out
    result[...] = (after[...] + mod_of(mod, 5) * mlp_out).astype(bf16)


def enter_back_kernel(grad_y, mlp, mod, grad_mlp, sums):
    grad = grad_y[...].astype(f32)
    values = (mod_of(mod, 5) * grad).astype(bf16)
    grad_mlp[...] = values
    sums[0:1] = token_sum(grad * mlp[...])
    sums[1:2] = token_sum(values.astype(f32))


def middle_back_kernel(own, got, after, grad_y, attn, mod, grad_after, grad_attn, sums):
    grad = own[...] + got[...].astype(f32)
    normal, inverse = normalized(after[...])
    sums[0:1] = token_sum(grad)
    sums[1:2] = token_sum(grad * normal)
    total = grad_y[...].astype(f32) + norm_back(grad, normal, inverse, mod_of(mod, 4))
    grad_after[...] = total
    values = (mod_of(mod, 2) * total).astype(bf16)
    grad_attn[...] = values
    sums[2:3] = token_sum(total * attn[...])
    sums[3:4] = token_sum(values.astype(f32))


def leave_back_kernel(own, got, inputs, grad_after, mod, grad_inputs, sums):
    grad = own[...] + got[...].astype(f32)
    normal, inverse = normalized(inputs[...].astype(f32))
    sums[0:1] = token_sum(grad)
    sums[1:2] = token_sum(grad * normal)
    grad_inputs[...] = (
        grad_after[...] + norm_back(grad, normal, inverse, mod_of(mod, 1))
    ).astype(bf16)


def forward_block(
    at, inputs, mod, weights, first, bias_qkv, bias_up, b_out, b_down, temporal, steps
):
    rows, width = inputs.shape
    for _ in range(steps[0]):
        inputs = weights.step(inputs)
    wide = shape_of(rows, width, kind=f32)
    low = shape_of(rows, width)
    (hidden,) = simple_call(enter_kernel, [inputs, mod], [low])
    hidden = (hidden, at.core(hidden))
    for _ in range(steps[1]):
        hidden = weights.step(hidden)
    w_attn, w_attn_t = weights.whole[first]
    (qkv,) = times(qkv_kernel, hidden, w_attn, [bias_qkv], [(True, bf16)])
    attended = call_attention(attend_kernel, [qkv], rows, temporal)
    own, got = times_back(at, attended, w_attn_t)
    attn, after, hidden_two = simple_call(
        middle_kernel, [own, got, inputs, mod, b_out], [wide, wide, low]
    )
    hidden_two = (hidden_two, at.core(hidden_two))
    for _ in range(steps[2]):
        hidden_two = weights.step(hidden_two)
    w_up = weights.whole[first + 1][0]
    up, activated = times(up_kernel, hidden_two, w_up, [bias_up], [(True, f32), (True, bf16)])
    for _ in range(steps[3]):
        activated = weights.step(activated)
    w_down_t = weights.whole[first + 2][1]
    own, got = times_back(at, activated, w_down_t)
    mlp, result = simple_call(leave_kernel, [own, got, after, mod, b_down], [wide, low])
    return result, (inputs, hidden, qkv, attended, attn, after, hidden_two, up, activated, mlp)


def backward_block(at, grad_y, kept, mod, weights, temporal, sums, names, place):
    inputs, hidden, qkv, attended, attn, after, hidden_two, up, activated, mlp = kept
    (w_attn, w_attn_t), (_, w_up_t), (w_down, _) = weights
    rows, width = inputs.shape
    wide = shape_of(rows, width, kind=f32)
    low = shape_of(rows, width)
    grad_mlp, sums_m = simple_call(
        enter_back_kernel, [grad_y, mlp, mod], [low, shape_of(2, width, kind=f32)]
    )
    grad_mlp = (grad_mlp, at.core(grad_mlp))
    sums.offer(names[0], grad_mlp, [activated])
    grad_mlp = sums.run(place + "0", grad_mlp)
    grad_up, grad_b_up = times(
        up_back_kernel, grad_mlp, w_down, [up], [(True, bf16), (False, f32)]
    )
    sums.offer(names[1], hidden_two, [grad_up])
    grad_up = sums.run(place + "1", grad_up)
    own, got = times_back(at, grad_up, w_up_t)
    grad_after, grad_attn, sums_a = simple_call(
        middle_back_kernel,
        [own, got, after, grad_y, attn, mod],
        [wide, low, shape_of(4, width, kind=f32)],
    )
    grad_attn = (grad_attn, at.core(grad_attn))
    grad_attn = sums.run(place + "2", grad_attn)
    (grad_attended,) = times(plain_kernel, grad_attn, w_attn, [], [(True, bf16)])
    grad_attended = sums.run(place + "3", grad_attended)
    grad_qkv = call_attention(attend_back_kernel, [qkv, grad_attended], rows, temporal)
    sums.offer(names[2], hidden + grad_attn, [grad_qkv, attended])
    own, got = times_back(at, grad_qkv, w_attn_t)
    own = sums.run(place + "4", own)
    grad_inputs, sums_i = simple_call(
        leave_back_kernel,
        [own, got, inputs, grad_after, mod],
        [low, shape_of(2, width, kind=f32)],
    )
    grad_mod = jnp.concatenate(
        [sums_i[0], sums_i[1], sums_a[2], sums_a[0], sums_a[1], sums_m[0]]
    )
    grad_b_qkv = jnp.sum(grad_qkv, axis=1, dtype=f32)
    cols = grad_b_qkv.shape[1] // 4
    grad_bias = jnp.concatenate(
        [grad_b_qkv[:, :cols], grad_b_qkv[:, 2 * cols : 3 * cols], grad_b_up[:, 0]], axis=1
    )
    return grad_inputs, grad_bias, sums_a[3], sums_m[1], grad_mod


def body(
    video, cond, w_ada, b_ada, w_qkv, b_qv, w_out, b_out, w_up, b_up, w_down, b_down, cotangent
):
    at = Place()
    width = video.shape[-1]
    own_width = w_up.shape[1]
    head_width = w_qkv.shape[3]
    silu_value, silu_back = jax.vjp(jax.nn.silu, cond.astype(f32))
    cond_act = silu_value.astype(bf16)
    if at.ns == 2:
        other = at.swap_y(cond_act)
        cond_all = jnp.concatenate(
            [jnp.where(at.s == 0, cond_act, other), jnp.where(at.s == 0, other, cond_act)], axis=0
        )
    else:
        cond_all = lax.all_gather(cond_act, "shard", axis=0, tiled=True)
    cond_rows = lax.dynamic_slice_in_dim(cond_all, at.s * own_width, own_width, axis=1)
    mod_part = jnp.einsum("cd,bdn->cbn", cond_rows, w_ada, preferred_element_type=f32)
    if at.ns == 2:
        kept = lax.dynamic_index_in_dim(mod_part, at.s, 0, False)
        mod_part = kept + at.swap_y(lax.dynamic_index_in_dim(mod_part, 1 - at.s, 0, False))
    else:
        mod_part = lax.psum_scatter(mod_part, "shard", scatter_dimension=0, tiled=True)[0]
    ada_cols = w_ada.shape[2]
    small = jnp.concatenate(
        [mod_part + b_ada, b_qv.reshape(2, -1).astype(f32), b_up.astype(f32)], axis=1
    )

    small = at.gather_small(small)
    arrays = (attention_weights(w_qkv, w_out), w_up, jnp.swapaxes(w_down, 1, 2))
    frames = lax.all_to_all(video, "tp", split_axis=1, concat_axis=2, tiled=True)
    rows = frames.size // width
    weights = Weights(at, arrays)
    small, frames = weights.step((small, frames))
    mods = jnp.moveaxis(small[:, :, :ada_cols], 0, 1).reshape(2, 6, width)
    biases = small[:, :, ada_cols:]
    biases = jnp.stack(
        [
            lax.dynamic_index_in_dim(biases, 2 * at.k, 0, False),
            lax.dynamic_index_in_dim(biases, 2 * at.k + 1, 0, False),
        ],
        axis=1,
    )
    zeros = jnp.zeros((2, 2, head_width), f32)
    bias_qkv = jnp.concatenate(
        [biases[:, :, :head_width], zeros, biases[:, :, head_width : 2 * head_width], zeros], axis=2
    )[:, :, None]
    bias_up = biases[:, :, None, 2 * head_width :]
    b_out_row, b_down_row = (v.astype(f32)[:, None] for v in (b_out, b_down))

    frames = weights.step(frames)
    inputs = frames.reshape(rows, width)
    middle, kept_one = forward_block(
        at,
        inputs,
        mods[0],
        weights,
        0,
        bias_qkv[0],
        bias_up[0],
        b_out_row[0],
        b_down_row[0],
        0,
        (0, 1, 1, 1),
    )
    moved = lax.all_to_all(
        middle.reshape(frames.shape), "tp", split_axis=2, concat_axis=1, tiled=True
    )
    middle = weights.step(middle)
    moved, middle = lax.optimization_barrier((moved, middle))
    moved = lax.all_to_all(moved, "ctx", split_axis=3, concat_axis=1, tiled=True)
    grid = moved.shape
    patches = grid[2] * grid[3]
    result, kept_two = forward_block(
        at,
        moved.reshape(rows, width),
        mods[1],
        weights,
        3,
        bias_qkv[1],
        bias_up[1],
        b_out_row[1],
        b_down_row[1],
        patches,
        (1, 0, 0, 1),
    )
    first, second = weights.whole[:3], weights.whole[3:]
    sums = Sums(at)
    grad_moved, *small_two = backward_block(
        at, cotangent.reshape(rows, width), kept_two, mods[1], second, patches, sums, "DUA", "A"
    )
    grad_moved = sums.run("A5", grad_moved)
    grad_middle = lax.all_to_all(
        grad_moved.reshape(grid), "ctx", split_axis=1, concat_axis=3, tiled=True
    )
    grad_middle = sums.run("A6", grad_middle)
    grad_middle = lax.all_to_all(grad_middle, "tp", split_axis=1, concat_axis=2, tiled=True)
    grad_middle = sums.run("A7", grad_middle)
    grad_frames, *small_one = backward_block(
        at, grad_middle.reshape(rows, width), kept_one, mods[0], first, 0, sums, "dua", "B"
    )
    grad_video = lax.all_to_all(
        grad_frames.reshape(frames.shape), "tp", split_axis=2, concat_axis=1, tiled=True
    ).astype(f32)

    grad_bias, grad_b_out, grad_b_down, grad_mod = (
        jnp.stack([one, two]) for one, two in zip(small_one, small_two)
    )
    blocks = jnp.arange(at.nt)[:, None, None]
    grad_bias = jnp.where(blocks == 2 * at.k, grad_bias[:, 0], 0.0) + jnp.where(
        blocks == 2 * at.k + 1, grad_bias[:, 1], 0.0
    )
    small = jnp.concatenate(
        [grad_bias.reshape(-1), grad_b_out.reshape(-1), grad_b_down.reshape(-1)]
    )
    small, grad_mods = at.sum_all(
        small,
        grad_mod.reshape(-1),
        sums.run,
    )
    size = grad_bias.size
    grad_bias = lax.dynamic_index_in_dim(small[:size].reshape(grad_bias.shape), at.t, 0, False)
    grad_b_out, grad_b_down = small[size:].reshape(2, 2, width)
    grad_mods = jnp.moveaxis(grad_mods.reshape(at.ns, 2, 6 * width), 0, 1)
    grad_mods = lax.dynamic_slice_in_dim(grad_mods, at.t * ada_cols, ada_cols, axis=2)
    cond_rows = cond_rows.astype(f32)
    grad_w_ada = sum(
        cond_rows[i][None, :, None] * grad_mods[:, i][:, None, :] for i in range(at.ns)
    )
    grad_b_ada = jnp.sum(grad_mods, axis=1)
    grad_act = jnp.einsum(
        "bcn,bdn->cd", grad_mods, w_ada.astype(f32), precision=highest, preferred_element_type=f32
    )
    if at.ns == 2:
        grad_act = at.sum_group(at.sum_group(grad_act, "tp", 1), "tp", 2)
        grad_act = sums.run("C5", grad_act)
        ours = lax.dynamic_slice_in_dim(grad_act, at.s, 1, axis=0)
        theirs = at.swap_y(lax.dynamic_slice_in_dim(grad_act, 1 - at.s, 1, axis=0))
        grad_act = jnp.concatenate(
            [jnp.where(at.s == 0, ours, theirs), jnp.where(at.s == 0, theirs, ours)], axis=1
        )
    else:
        grad_act = lax.psum_scatter(
            lax.dynamic_update_slice_in_dim(
                jnp.zeros((at.ns, width), f32), grad_act, at.s * own_width, axis=1
            ),
            "shard",
            scatter_dimension=0,
            tiled=True,
        )
        grad_act = lax.psum(grad_act, "tp")
    grad_act, grad_video = sums.run("C6", (grad_act, grad_video))
    sums.run("C7", ())
    sums = sums.done
    grad_cond = silu_back(grad_act)[0]

    grad_w_qkv, grad_w_out = attention_grads(at, sums["a"], sums["A"], head_width)
    return (
        result.reshape(grid),
        grad_video,
        grad_cond,
        grad_w_ada,
        grad_b_ada,
        grad_w_qkv,
        grad_bias[:, : 2 * head_width].reshape(2, 2, head_width),
        grad_w_out,
        grad_b_out,
        rows_grads(at, sums["u"], sums["U"]),
        grad_bias[:, 2 * head_width :],
        jnp.swapaxes(rows_grads(at, sums["d"], sums["D"]), 1, 2),
        grad_b_down,
    )


def solution(mesh):
    in_specs = (
        P("shard", "ctx", "tp", None, None),
        P("shard", None),
        P(None, "shard", "tp"),
        P(None, "tp"),
        P(None, None, "shard", "tp"),
        P(None, None, "tp"),
        P(None, "tp", "shard"),
        P(),
        P(None, "shard", "tp"),
        P(None, "tp"),
        P(None, "tp", "shard"),
        P(),
        P("shard", None, "tp", "ctx", None),
    )
    out_specs = (
        P("shard", None, "tp", "ctx", None),
        P("shard", "ctx", "tp", None, None),
        P("shard", None),
        P(None, "shard", "tp"),
        P(None, "tp"),
        P(None, None, "shard", "tp"),
        P(None, None, "tp"),
        P(None, "tp", "shard"),
        P(),
        P(None, "shard", "tp"),
        P(None, "tp"),
        P(None, "tp", "shard"),
        P(),
    )
    return jax.shard_map(body, mesh=mesh, in_specs=in_specs, out_specs=out_specs, check_vma=False)
```

```python
from functools import partial
import math

import jax
import jax.numpy as jnp
from jax import lax
from jax.experimental import pallas as pl
from jax.experimental.pallas import tpu as pltpu
from jax.sharding import PartitionSpec as P

HEAD_DIM = 72
bf16 = jnp.bfloat16
f32 = jnp.float32
highest = lax.Precision.HIGHEST


class Place:
    def __init__(self):
        self.ns = lax.axis_size("shard")
        self.nc = lax.axis_size("ctx")
        self.nt = lax.axis_size("tp")
        self.s = lax.axis_index("shard")
        self.c = lax.axis_index("ctx")
        self.t = lax.axis_index("tp")
        self.x = self.c // 2
        self.k = self.c % 2
        self.d = jnp.where(self.k == 0, self.t, self.nt - 1 - self.t)

    def core(self, v):
        return lax.ppermute(v, "ctx", [(c, c ^ 1) for c in range(self.nc)])

    def swap_x(self, v):
        return lax.ppermute(v, "ctx", [(c, c ^ 2) for c in range(self.nc)])

    def swap_y(self, v):
        return lax.ppermute(v, "shard", [(i, i ^ 1) for i in range(self.ns)])

    def along_z(self, v, pairs):
        def at(c, d):
            return c * self.nt + (d if c % 2 == 0 else self.nt - 1 - d)

        return lax.ppermute(
            v, ("ctx", "tp"), [(at(c, i), at(c, j)) for c in range(self.nc) for i, j in pairs]
        )

    def gather_small(self, v):
        got = [v] + [
            lax.ppermute(v, "tp", [(i, i ^ step) for i in range(self.nt)])
            for step in range(1, self.nt)
        ]
        return jnp.stack([pick(self.t ^ i, got) for i in range(self.nt)])

    def sum_group(self, v, axis, step):
        size = self.nc if axis == "ctx" else self.nt
        return v + lax.ppermute(v, axis, [(i, i ^ step) for i in range(size)])

    def sum_all(self, v, per_clip, run):
        size = v.size
        v = jnp.concatenate([v, per_clip]).reshape(1, -1)
        v = run("C0", self.sum_group(v, "ctx", 1))
        v = run("C1", self.sum_group(v, "ctx", 2))
        v = run("C2", self.sum_group(v, "tp", 1))
        v = run("C3", self.sum_group(v, "tp", 2))
        if self.ns != 2:
            return lax.psum(v[0, :size], "shard"), lax.all_gather(
                v[:, size:], "shard", axis=0, tiled=True
            )
        v, w = run("C4", (v, self.swap_y(v)))
        rows = [jnp.where(self.s == 0, v, w), jnp.where(self.s == 0, w, v)]
        return (v + w)[0, :size], jnp.concatenate(rows, axis=0)[:, size:]

    def position(self):
        return jnp.stack([self.s, self.x, self.k]).astype(jnp.int32)

    def by_x(self, near, far):
        return [jnp.where(self.x == 0, near, far), jnp.where(self.x == 0, far, near)]

    def by_k(self, near, far):
        return [jnp.where(self.k == 0, near, far), jnp.where(self.k == 0, far, near)]


def pick(index, options):
    out = options[-1]
    for number in range(len(options) - 2, -1, -1):
        out = jnp.where(index == number, options[number], out)
    return out


def tie(values, *others):
    return lax.optimization_barrier((values, others))[0]


class Chunk:
    def __init__(self, first, common, part):
        self.first = first
        self.common = common
        self.part = part
        self.rows = common + 2 * part

    def sent(self, at, both, b):
        half, part = self.common // 2, self.part // 2
        starts = (self.first + at.k * half, self.first + self.common + at.x * self.part + at.k * part)
        cols = both.shape[2]
        return jnp.concatenate(
            [
                lax.dynamic_slice(both, (b, start, 0), (1, size, cols))[0]
                for start, size in zip(starts, (half, part))
                if size
            ],
            axis=0,
        )

    def core_step(self, at, blocks):
        got = at.core(lax.dynamic_slice_in_dim(blocks, 2 - 2 * at.k, 2, axis=0))
        mine = lax.dynamic_slice_in_dim(blocks, 2 * at.k, 2, axis=0)
        half = self.common // 2
        common = jnp.where(at.x == at.k, mine[:, :half], got[:, :half])
        if not self.part:
            return (mine, got), common
        part = jnp.concatenate([mine[:, half:], got[:, half:]], axis=1)
        return (mine, got), jnp.concatenate([common, part], axis=1), part


def assemble_kernel(place_ref, *refs, chunk):
    out_ref, turned_ref = refs[-2:]
    s, x, k = place_ref[0], place_ref[1], place_ref[2]
    width = out_ref.shape[1] // 2

    def copy(source, start, size, offset):
        if size:
            out_ref[0, pl.ds(pl.multiple_of(offset, 16), size), :] = source[
                0, start : start + size, :
            ]

    mine, got, near, far = refs[:4]
    side = refs[4] if chunk.part else None
    half, part = chunk.common // 2, chunk.part // 2
    own, other = s * width, (1 - s) * width

    def parts(source, start, base, plane):
        offset = base + chunk.common + plane * chunk.part
        copy(source, start, part, offset + k * part)
        copy(source, start + part, part, offset + (1 - k) * part)

    copy(mine, 0, half, own + k * half)
    copy(got, 0, half, own + (1 - k) * half)
    copy(mine, half, part, own + chunk.common + x * chunk.part + k * part)
    copy(got, half, part, own + chunk.common + x * chunk.part + (1 - k) * part)
    parts(side, 0, own, 1 - x)
    copy(near, 0, half, other + x * half)
    parts(near, half, other, x)
    copy(far, 0, half, other + (1 - x) * half)
    parts(far, half, other, 1 - x)
    turned_ref[0] = out_ref[0].T


def assemble(at, chunk, arrays):
    cols = arrays[0].shape[2]
    rows = 2 * chunk.rows
    return call(
        partial(assemble_kernel, chunk=chunk),
        [(a, False) for a in arrays],
        [(shape_of(2, rows, cols), False), (shape_of(2, cols, rows), False)],
        scalars=(at.position(),),
    )


class Weights:
    def __init__(self, at, arrays):
        self.at = at
        self.whole = []
        self.count = 2 * len(arrays)
        self.number = 0
        jobs = [(b, array) for b in range(2) for array in arrays]
        if at.ns != 2:
            for b, array in jobs:
                both = lax.all_gather(array[b], "tp", axis=0)
                both = lax.dynamic_slice_in_dim(both, 2 * at.k, 2, axis=0)
                both = lax.all_gather(both, "shard", axis=1, tiled=True)
                self.whole.append((both, jnp.swapaxes(both, 1, 2)))
            return
        rows = arrays[0].shape[1]
        self.plans = [
            Chunk(0, rows - 2 * part, part)
            for part in (rows // 36 * units for units in (14, 10, 8, 8, 6, 0))
        ]
        self.blocks = []
        sent = ()
        for plan, (b, array) in zip(self.plans, jobs):
            sent = plan.sent(at, tie(array, sent), b)
            self.blocks.append(lax.all_gather(sent, "tp", axis=0))
        self.held, self.near, self.far, self.side = {}, {}, {}, {}

    def step(self, main):
        if self.at.ns != 2 or self.number == self.count + 2:
            return main
        at, number = self.at, self.number
        self.number += 1
        block = self.blocks[number] if number < self.count else ()
        block, near, far, side, main = lax.optimization_barrier(
            (
                block,
                self.near.get(number - 1),
                self.far.get(number - 2),
                self.side.get(number - 1),
                main,
            )
        )
        if 0 < number <= self.count:
            self.near[number - 1], self.side[number - 1] = near, side
            self.far[number - 1] = at.swap_x(near)
        if number < self.count:
            self.held[number], *messages = self.plans[number].core_step(at, block)
            messages, main = lax.optimization_barrier((messages, main))
            self.near[number] = at.swap_y(messages[0])
            self.side[number] = at.swap_x(messages[-1]) if self.plans[number].part else ()
        if number > 1:
            m = number - 2
            sides = [self.side[m]] if self.plans[m].part else []
            arrays = [*self.held[m], self.near[m], far, *sides]
            self.whole.append(assemble(at, self.plans[m], arrays))
        return main


def scatter_z(everything):
    return lax.psum_scatter(everything, "tp", scatter_dimension=0, tiled=True)[0]


def product(left, right):
    left = jnp.concatenate(left, axis=0)
    right = jnp.concatenate(right, axis=1)
    return jnp.einsum("rd,prn->pdn", left, right, preferred_element_type=f32).astype(bf16)


def term_of(turned, right, starts, rows):
    left = [turned[pl.ds(pl.multiple_of(start, 16), rows), :] for start in starts]
    left = jnp.concatenate(left, axis=0)
    depth = right[0].shape[1]
    return sum(
        jnp.dot(left[:, i * depth : (i + 1) * depth], r[0], preferred_element_type=f32)
        for i, r in enumerate(right)
    )


def starts_of(place_ref, width, pairs, half):
    s, x = place_ref[0], place_ref[1]
    return [
        (4 * jnp.abs(s - ds) + 2 * jnp.abs(x - dx) + half) * (width // 8) for ds, dx in pairs
    ]


def away_kernel(place_ref, *refs, count):
    left, right = refs[:count], refs[count:-3]
    to_y, to_x, turned = refs[-3:]
    rows = left[0].shape[0]
    width = turned.shape[0]

    @pl.when(pl.program_id(0) == 0)
    def _():
        for i, source in enumerate(left):
            turned[:, i * rows : (i + 1) * rows] = source[...].T

    first = starts_of(place_ref, width, ((1, 0), (1, 1)), 0)
    second = starts_of(place_ref, width, ((0, 1), (1, 1)), 1)
    to_y[0] = term_of(turned, right, first, width // 8).astype(bf16)
    to_x[0] = term_of(turned, right, second, width // 8).astype(bf16)


def here_kernel(place_ref, from_y, from_x, turned, *refs):
    right = refs[:-4]
    over_y, over_x, to_x, to_y = refs[-4:]
    width = turned.shape[0]
    rows = width // 8
    first = starts_of(place_ref, width, ((0, 0), (0, 1)), 0)
    second = starts_of(place_ref, width, ((0, 0), (1, 0)), 1)
    one = term_of(turned, right, first, rows) + from_y[0].astype(f32)
    over_y[0] = one[:rows].astype(bf16)
    to_x[0] = one[rows:].astype(bf16)
    two = term_of(turned, right, second, rows) + from_x[0].astype(f32)
    over_x[0] = two[:rows].astype(bf16)
    to_y[0] = two[rows:].astype(bf16)


def join_kernel(place_ref, over_y, over_x, from_x, from_y, kept, given):
    k = place_ref[2]
    for out, flag in ((kept, k == 0), (given, k == 1)):

        @pl.when(flag)
        def _():
            out[0] = (over_y[0].astype(f32) + from_x[0].astype(f32)).astype(bf16)

        @pl.when(jnp.logical_not(flag))
        def _():
            out[0] = (over_x[0].astype(f32) + from_y[0].astype(f32)).astype(bf16)


def per_block(array):
    return pl.BlockSpec((1,) + array.shape[1:], lambda i: (i,) + (0,) * (len(array.shape) - 1))


def entire(array):
    return pl.BlockSpec(array.shape, lambda i: (0,) * len(array.shape))


def call(kernel, inputs, outputs, scratch=(), scalars=()):
    return pl.pallas_call(
        kernel,
        out_shape=tuple(a for a, _ in outputs),
        grid=(2,),
        in_specs=[pl.BlockSpec(memory_space=pltpu.SMEM)] * len(scalars)
        + [entire(a) if whole else per_block(a) for a, whole in inputs],
        out_specs=tuple(entire(a) if whole else per_block(a) for a, whole in outputs),
        scratch_shapes=list(scratch),
        cost_estimate=pl.CostEstimate(flops=0, transcendentals=0, bytes_accessed=0),
        compiler_params=pltpu.CompilerParams(vmem_limit_bytes=48 * 1024 * 1024),
    )(*scalars, *[a for a, _ in inputs])


def shape_of(*dims, kind=bf16):
    return jax.ShapeDtypeStruct(dims, kind)


def products_away(at, left, right):
    rows, width = left[0].shape
    sent = shape_of(2, width // 4, right[0].shape[2])
    return call(
        partial(away_kernel, count=len(left)),
        [(l, True) for l in left] + [(r, False) for r in right],
        [(sent, False), (sent, False), (shape_of(width, rows * len(left)), True)],
        scalars=(at.position(),),
    )


def products_here(at, turned, right, from_y, from_x):
    part = shape_of(2, from_y.shape[1] // 2, from_y.shape[2])
    return call(
        here_kernel,
        [(from_y, False), (from_x, False), (turned, True)] + [(r, False) for r in right],
        [(part, False)] * 4,
        scalars=(at.position(),),
    )


def join_halves(at, *parts):
    return call(
        join_kernel,
        [(part, False) for part in parts],
        [(shape_of(*parts[0].shape), False)] * 2,
        scalars=(at.position(),),
    )


PLAN = {
    "A0": ("pD", "1D"),
    "A1": ("pU",),
    "A2": ("2D", "1U"),
    "A3": (),
    "A4": ("pA",),
    "A5": (),
    "A6": ("2U", "1A", "zD"),
    "A7": (),
    "B0": ("pd", "2A", "1d", "zU", "fD"),
    "B1": ("pu",),
    "B2": (),
    "B3": (),
    "B4": ("2d", "1u", "zA", "fU"),
    "C0": (),
    "C1": ("eD", "pa", "fA", "2u", "1a", "zd", "eU"),
    "C2": (),
    "C3": (),
    "C4": ("2a", "zu", "fd"),
    "C5": ("za",),
    "C6": (),
    "C7": ("fu", "ed", "fa", "eA", "ea", "eu"),
}


class Sums:
    def __init__(self, at):
        self.at = at
        self.state = {}
        self.done = {}

    def offer(self, name, left, right):
        self.state[name] = (None, (list(left), list(right)))

    def run(self, place, main):
        for step in PLAN[place]:
            kind, name = step
            if name not in self.state:
                continue
            kept, pending = self.state.pop(name)
            pending, main = lax.optimization_barrier((pending, main))
            if kind == "w":
                self.state[name] = (kept, pending)
                continue
            if self.at.ns != 2:
                self.done[name] = self.generic(*pending)
                continue
            kept, messages = getattr(self, "step_" + kind)(kept, pending)
            values, main = lax.optimization_barrier(([value for _, value in messages], main))
            if kind == "e":
                self.done[name] = values
            else:
                sent = [value if how is None else how(value) for (how, _), value in zip(messages, values)]
                self.state[name] = (kept, sent)
        return main

    def generic(self, left, right):
        at = self.at
        summed = lax.psum_scatter(
            product(left, right), "shard", scatter_dimension=1, tiled=True
        )
        half = summed.shape[1] // 2
        halves = [summed[:, :half], summed[:, half:]]
        got = at.core(jnp.where(at.k == 0, halves[1], halves[0]))
        kept = jnp.where(at.k == 0, halves[0], halves[1])
        mine = scatter_z(jnp.concatenate(at.by_k(kept, got), axis=0))
        mine = (mine.astype(f32) + at.swap_x(mine).astype(f32)).astype(bf16)
        return jnp.concatenate(at.by_k(mine, at.core(mine)), axis=0)

    def step_p(self, _, pending):
        left, right = pending
        to_y, to_x, turned = products_away(self.at, left, right)
        return (right, turned), [(None, to_y), (None, to_x)]

    def step_1(self, kept, pending):
        to_y, to_x = pending
        return kept, [(self.at.swap_y, to_y), (self.at.swap_x, to_x)]

    def step_2(self, kept, pending):
        right, turned = kept
        over_y, over_x, to_x, to_y = products_here(self.at, turned, right, *pending)
        return (over_y, over_x), [(self.at.swap_x, to_x), (self.at.swap_y, to_y)]

    def step_z(self, kept, pending):
        kept, given = join_halves(self.at, *kept, *pending)
        everything = jnp.concatenate(self.at.by_k(kept, self.at.core(given)), axis=0)
        return None, [(scatter_z, everything)]

    def step_f(self, _, pending):
        (mine,) = pending
        return mine, [(self.at.swap_x, mine)]

    def step_e(self, mine, pending):
        (far,) = pending
        mine = jnp.stack(self.at.by_x(mine, far))
        return None, [(None, mine), (None, self.at.core(mine))]


def rows_in_place(place_ref, mine, theirs, target, b):
    k = place_ref[2]
    rows = mine.shape[1]
    for ref, member in ((mine, k), (theirs, 1 - k)):
        for x in range(2):
            start = pl.multiple_of((2 * x + member) * rows, 8)
            target[b, pl.ds(start, rows), :] = ref[x].astype(f32)


def rows_kernel(place_ref, *refs):
    for b in range(2):
        rows_in_place(place_ref, refs[2 * b], refs[2 * b + 1], refs[4], b)


def turned_kernel(place_ref, *refs):
    qkv_ref, out_ref, target = refs[4:]
    cols = out_ref.shape[1]
    for b in range(2):
        rows_in_place(place_ref, refs[2 * b], refs[2 * b + 1], target, b)
        values = target[b].T
        for number in range(3):
            qkv_ref[b, number] = values[number * cols : (number + 1) * cols]
        out_ref[b] = values[3 * cols :]


def simple_call(kernel, inputs, outputs, scratch=(), scalars=()):
    return pl.pallas_call(
        kernel,
        out_shape=tuple(outputs),
        in_specs=[pl.BlockSpec(memory_space=pltpu.SMEM)] * len(scalars)
        + [pl.BlockSpec(memory_space=pltpu.VMEM)] * len(inputs),
        out_specs=tuple(pl.BlockSpec(memory_space=pltpu.VMEM) for _ in outputs),
        scratch_shapes=list(scratch),
        cost_estimate=pl.CostEstimate(flops=0, transcendentals=0, bytes_accessed=0),
        compiler_params=pltpu.CompilerParams(vmem_limit_bytes=48 * 1024 * 1024),
    )(*scalars, *inputs)


def rows_grads(at, first, second):
    if at.ns != 2:
        return jnp.stack([first, second]).astype(f32)
    _, rows, cols = first[0].shape
    shape = shape_of(2, 4 * rows, cols, kind=f32)
    return simple_call(rows_kernel, [*first, *second], [shape], scalars=(at.position(),))[0]


def attention_grads(at, first, second, head_width):
    if at.ns != 2:
        both = jnp.swapaxes(jnp.stack([first, second]).astype(f32), 1, 2)
        qkv = both[:, : 3 * head_width].reshape(2, 3, head_width, -1)
        return jnp.swapaxes(qkv, 2, 3), both[:, 3 * head_width :]
    _, rows, cols = first[0].shape
    qkv, out = simple_call(
        turned_kernel,
        [*first, *second],
        [
            shape_of(2, 3, head_width, 4 * rows, kind=f32),
            shape_of(2, head_width, 4 * rows, kind=f32),
        ],
        scratch=[pltpu.VMEM((2, 4 * rows, cols), f32)],
        scalars=(at.position(),),
    )
    return jnp.swapaxes(qkv, 2, 3), out


def prepare_kernel(qkv_ref, out_ref, target):
    for b in range(2):
        rows = [qkv_ref[b, number].T for number in range(3)] + [out_ref[b].T]
        target[b] = jnp.concatenate(rows, axis=1)


def attention_weights(w_qkv, w_out):
    _, _, rows, cols = w_qkv.shape
    return simple_call(
        prepare_kernel, [jnp.swapaxes(w_qkv, 2, 3), w_out], [shape_of(2, rows, 4 * cols)]
    )[0]


def heads_of(values, number, head):
    start = number * 4 * HEAD_DIM + head * HEAD_DIM
    return values[:, start : start + HEAD_DIM]


def probs_of(query, key, temporal):
    scores = lax.dot_general(
        query, key, (((1,), (1,)), ((), ())), preferred_element_type=f32
    ) * (1.0 / math.sqrt(HEAD_DIM))
    if temporal:
        rows = lax.broadcasted_iota(jnp.int32, scores.shape, 0) % temporal
        cols = lax.broadcasted_iota(jnp.int32, scores.shape, 1) % temporal
        scores = jnp.where(rows == cols, scores, -jnp.inf)
    weights = jnp.exp(scores - jnp.max(scores, axis=-1, keepdims=True))
    return weights / jnp.sum(weights, axis=-1, keepdims=True)


def attend_kernel(qkv_ref, out_ref, *, temporal):
    values = qkv_ref[0]
    results = [jnp.zeros((values.shape[0], 12 * HEAD_DIM), bf16)]
    for head in range(4):
        probs = probs_of(heads_of(values, 0, head), heads_of(values, 1, head), temporal)
        results.append(
            jnp.dot(
                probs.astype(bf16), heads_of(values, 2, head), preferred_element_type=f32
            ).astype(bf16)
        )
    out_ref[0] = jnp.concatenate(results, axis=1)


def attend_back_kernel(qkv_ref, grad_ref, out_ref, *, temporal):
    factor = 1.0 / math.sqrt(HEAD_DIM)
    values = qkv_ref[0]
    grads = grad_ref[0]
    queries, keys, vals = [], [], []
    for head in range(4):
        query, key, value = (heads_of(values, number, head) for number in range(3))
        grad = heads_of(grads, 3, head)
        probs = probs_of(query, key, temporal)
        vals.append(
            lax.dot_general(
                probs.astype(bf16), grad, (((0,), (0,)), ((), ())), preferred_element_type=f32
            ).astype(bf16)
        )
        grad_probs = lax.dot_general(
            grad, value, (((1,), (1,)), ((), ())), preferred_element_type=f32
        )
        inner = jnp.sum(grad_probs * probs, axis=-1, keepdims=True)
        grad_scores = (probs * (grad_probs - inner)).astype(bf16)
        queries.append(
            (jnp.dot(grad_scores, key, preferred_element_type=f32) * factor).astype(bf16)
        )
        keys.append(
            (
                lax.dot_general(
                    grad_scores, query, (((0,), (0,)), ((), ())), preferred_element_type=f32
                )
                * factor
            ).astype(bf16)
        )
    zeros = jnp.zeros((values.shape[0], 4 * HEAD_DIM), bf16)
    out_ref[0] = jnp.concatenate(queries + keys + vals + [zeros], axis=1)


def call_attention(kernel, arrays, rows, temporal):
    shape = arrays[0].shape
    spec = pl.BlockSpec((1, rows, shape[2]), lambda i, j: (i, j, 0))
    return pl.pallas_call(
        partial(kernel, temporal=temporal),
        out_shape=shape_of(*shape),
        grid=(shape[0], shape[1] // rows),
        in_specs=[spec] * len(arrays),
        out_specs=spec,
        cost_estimate=pl.CostEstimate(flops=0, transcendentals=0, bytes_accessed=0),
        compiler_params=pltpu.CompilerParams(vmem_limit_bytes=48 * 1024 * 1024),
    )(*arrays)


SLOPE = math.sqrt(2.0 / math.pi)


def gelu(u):
    return 0.5 * u * (1.0 + jnp.tanh(SLOPE * (u + 0.044715 * (u * u * u))))


def gelu_slope(u):
    t = jnp.tanh(SLOPE * (u + 0.044715 * (u * u * u)))
    inner = SLOPE * (1.0 + 3.0 * 0.044715 * (u * u))
    return 0.5 * (1.0 + t) + 0.5 * u * (1.0 - t * t) * inner


def times_of(own, other, weight):
    left = jnp.concatenate([own[...], other[...]], axis=0)
    return jnp.dot(left, weight[0], preferred_element_type=f32)


def qkv_kernel(own, other, weight, bias, out):
    out[0] = (times_of(own, other, weight) + bias[0]).astype(bf16)


def plain_kernel(own, other, weight, out):
    out[0] = times_of(own, other, weight).astype(bf16)


def up_kernel(own, other, weight, bias, up, activated):
    values = times_of(own, other, weight) + bias[0]
    up[0] = values
    activated[0] = gelu(values).astype(bf16)


def up_back_kernel(own, other, weight, up, out, sums):
    values = (gelu_slope(up[0]) * times_of(own, other, weight)).astype(bf16)
    out[0] = values
    sums[0] = jnp.sum(values.astype(f32), axis=0, keepdims=True)


def back_kernel(left, weight, own, other, total):
    term = jnp.dot(left[0], weight[0], preferred_element_type=f32)
    rows = own.shape[0]

    @pl.when(pl.program_id(0) == 0)
    def _():
        total[...] = term

    @pl.when(pl.program_id(0) == 1)
    def _():
        own[...] = total[:rows] + term[:rows]
        other[...] = (total[rows:] + term[rows:]).astype(bf16)


def times(kernel, pair, weight, extra=(), outputs=()):
    rows = 2 * pair[0].shape[0]
    cols = weight.shape[2]
    return call(
        kernel,
        [(pair[0], True), (pair[1], True), (weight, False)] + [(e, False) for e in extra],
        [(shape_of(2, rows if tall else 1, cols, kind=kind), False) for tall, kind in outputs],
    )


def times_back(at, left, weight):
    rows, width = left.shape[1] // 2, weight.shape[2]
    own, other = call(
        back_kernel,
        [(left, False), (weight, False)],
        [(shape_of(rows, width, kind=f32), True), (shape_of(rows, width), True)],
        scratch=[pltpu.VMEM((2 * rows, width), f32)],
    )
    return own, at.core(other)


def normalized(values):
    average = jnp.mean(values, axis=-1, keepdims=True)
    centered = values - average
    inverse = lax.rsqrt(jnp.mean(centered * centered, axis=-1, keepdims=True) + 1e-06)
    return centered * inverse, inverse


def norm_back(grad, normal, inverse, factor):
    dn = grad * (1.0 + factor)
    return (
        dn
        - jnp.mean(dn, axis=-1, keepdims=True)
        - normal * jnp.mean(dn * normal, axis=-1, keepdims=True)
    ) * inverse


def token_sum(values):
    return jnp.sum(values, axis=0, keepdims=True)


def mod_of(mod, number):
    return mod[number : number + 1, :]


def enter_kernel(inputs, mod, hidden):
    normal, _ = normalized(inputs[...].astype(f32))
    hidden[...] = (normal * (1.0 + mod_of(mod, 1)) + mod_of(mod, 0)).astype(bf16)


def middle_kernel(own, got, inputs, mod, bias, attn, after, hidden):
    attn_out = own[...] + got[...].astype(f32) + bias[...]
    attn[...] = attn_out
    values = inputs[...].astype(f32) + mod_of(mod, 2) * attn_out
    after[...] = values
    normal, _ = normalized(values)
    hidden[...] = (normal * (1.0 + mod_of(mod, 4)) + mod_of(mod, 3)).astype(bf16)


def leave_kernel(own, got, after, mod, bias, mlp, result):
    mlp_out = own[...] + got[...].astype(f32) + bias[...]
    mlp[...] = mlp_out
    result[...] = (after[...] + mod_of(mod, 5) * mlp_out).astype(bf16)


def enter_back_kernel(grad_y, mod, grad_mlp, sums):
    values = (mod_of(mod, 5) * grad_y[...].astype(f32)).astype(bf16)
    grad_mlp[...] = values
    sums[...] = token_sum(values.astype(f32))


def gate_kernel(grad_y, mlp, sums):
    sums[...] = token_sum(grad_y[...].astype(f32) * mlp[...])


def gate_sum(grad_y, mlp):
    return simple_call(gate_kernel, [grad_y, mlp], [shape_of(1, mlp.shape[1], kind=f32)])[0][0]


def middle_back_kernel(own, got, after, grad_y, attn, mod, grad_after, grad_attn, sums):
    grad = own[...] + got[...].astype(f32)
    normal, inverse = normalized(after[...])
    sums[0:1] = token_sum(grad)
    sums[1:2] = token_sum(grad * normal)
    total = grad_y[...].astype(f32) + norm_back(grad, normal, inverse, mod_of(mod, 4))
    grad_after[...] = total
    values = (mod_of(mod, 2) * total).astype(bf16)
    grad_attn[...] = values
    sums[2:3] = token_sum(total * attn[...])
    sums[3:4] = token_sum(values.astype(f32))


def leave_back_kernel(own, got, inputs, grad_after, mod, grad_inputs, sums):
    grad = own[...] + got[...].astype(f32)
    normal, inverse = normalized(inputs[...].astype(f32))
    sums[0:1] = token_sum(grad)
    sums[1:2] = token_sum(grad * normal)
    grad_inputs[...] = (
        grad_after[...] + norm_back(grad, normal, inverse, mod_of(mod, 1))
    ).astype(bf16)


def forward_block(
    at, inputs, mod, weights, first, bias_qkv, bias_up, b_out, b_down, temporal, steps
):
    rows, width = inputs.shape
    for _ in range(steps[0]):
        inputs = weights.step(inputs)
    wide = shape_of(rows, width, kind=f32)
    low = shape_of(rows, width)
    (hidden,) = simple_call(enter_kernel, [inputs, mod], [low])
    hidden = (hidden, at.core(hidden))
    for _ in range(steps[1]):
        hidden = weights.step(hidden)
    w_attn, w_attn_t = weights.whole[first]
    (qkv,) = times(qkv_kernel, hidden, w_attn, [bias_qkv], [(True, bf16)])
    attended = call_attention(attend_kernel, [qkv], rows, temporal)
    own, got = times_back(at, attended, w_attn_t)
    attn, after, hidden_two = simple_call(
        middle_kernel, [own, got, inputs, mod, b_out], [wide, wide, low]
    )
    hidden_two = (hidden_two, at.core(hidden_two))
    for _ in range(steps[2]):
        hidden_two = weights.step(hidden_two)
    w_up = weights.whole[first + 1][0]
    up, activated = times(up_kernel, hidden_two, w_up, [bias_up], [(True, f32), (True, bf16)])
    for _ in range(steps[3]):
        activated = weights.step(activated)

    def leave():
        own, got = times_back(at, activated, weights.whole[first + 2][1])
        return simple_call(leave_kernel, [own, got, after, mod, b_down], [wide, low])

    return leave, (inputs, hidden, qkv, attended, attn, after, hidden_two, up, activated)


def backward_block(at, grad_y, kept, mod, weights, first, temporal, sums, names, place):
    inputs, hidden, qkv, attended, attn, after, hidden_two, up, activated = kept
    rows, width = inputs.shape
    wide = shape_of(rows, width, kind=f32)
    low = shape_of(rows, width)
    grad_mlp, sums_m = simple_call(
        enter_back_kernel, [grad_y, mod], [low, shape_of(1, width, kind=f32)]
    )
    grad_mlp = (grad_mlp, at.core(grad_mlp))
    sums.offer(names[0], grad_mlp, [activated])
    grad_mlp = weights.step(sums.run(place + "0", grad_mlp))
    (w_attn, w_attn_t), (_, w_up_t), (w_down, _) = weights.whole[first : first + 3]
    grad_up, grad_b_up = times(
        up_back_kernel, grad_mlp, w_down, [up], [(True, bf16), (False, f32)]
    )
    sums.offer(names[1], hidden_two, [grad_up])
    grad_up = sums.run(place + "1", grad_up)
    own, got = times_back(at, grad_up, w_up_t)
    grad_after, grad_attn, sums_a = simple_call(
        middle_back_kernel,
        [own, got, after, grad_y, attn, mod],
        [wide, low, shape_of(4, width, kind=f32)],
    )
    grad_attn = (grad_attn, at.core(grad_attn))
    grad_attn = sums.run(place + "2", grad_attn)
    (grad_attended,) = times(plain_kernel, grad_attn, w_attn, [], [(True, bf16)])
    grad_attended = sums.run(place + "3", grad_attended)
    grad_qkv = call_attention(attend_back_kernel, [qkv, grad_attended], rows, temporal)
    sums.offer(names[2], hidden + grad_attn, [grad_qkv, attended])
    own, got = times_back(at, grad_qkv, w_attn_t)
    own = sums.run(place + "4", own)
    grad_inputs, sums_i = simple_call(
        leave_back_kernel,
        [own, got, inputs, grad_after, mod],
        [low, shape_of(2, width, kind=f32)],
    )
    grad_mod = jnp.concatenate([sums_i[0], sums_i[1], sums_a[2], sums_a[0], sums_a[1]])
    grad_b_qkv = jnp.sum(grad_qkv, axis=1, dtype=f32)
    cols = grad_b_qkv.shape[1] // 4
    grad_bias = jnp.concatenate(
        [grad_b_qkv[:, :cols], grad_b_qkv[:, 2 * cols : 3 * cols], grad_b_up[:, 0]], axis=1
    )
    return grad_inputs, grad_bias, sums_a[3], sums_m[0], grad_mod


def body(
    video, cond, w_ada, b_ada, w_qkv, b_qv, w_out, b_out, w_up, b_up, w_down, b_down, cotangent
):
    at = Place()
    width = video.shape[-1]
    own_width = w_up.shape[1]
    head_width = w_qkv.shape[3]
    silu_value, silu_back = jax.vjp(jax.nn.silu, cond.astype(f32))
    cond_act = silu_value.astype(bf16)
    if at.ns == 2:
        other = at.swap_y(cond_act)
        cond_all = jnp.concatenate(
            [jnp.where(at.s == 0, cond_act, other), jnp.where(at.s == 0, other, cond_act)], axis=0
        )
    else:
        cond_all = lax.all_gather(cond_act, "shard", axis=0, tiled=True)
    cond_rows = lax.dynamic_slice_in_dim(cond_all, at.s * own_width, own_width, axis=1)
    mod_part = jnp.einsum("cd,bdn->cbn", cond_rows, w_ada, preferred_element_type=f32)
    if at.ns == 2:
        kept = lax.dynamic_index_in_dim(mod_part, at.s, 0, False)
        mod_part = kept + at.swap_y(lax.dynamic_index_in_dim(mod_part, 1 - at.s, 0, False))
    else:
        mod_part = lax.psum_scatter(mod_part, "shard", scatter_dimension=0, tiled=True)[0]
    ada_cols = w_ada.shape[2]
    small = jnp.concatenate(
        [mod_part + b_ada, b_qv.reshape(2, -1).astype(f32), b_up.astype(f32)], axis=1
    )

    small = at.gather_small(small)
    arrays = (attention_weights(w_qkv, w_out), w_up, jnp.swapaxes(w_down, 1, 2))
    frames = lax.all_to_all(video, "tp", split_axis=1, concat_axis=2, tiled=True)
    rows = frames.size // width
    weights = Weights(at, arrays)
    small, frames = weights.step((small, frames))
    mods = jnp.moveaxis(small[:, :, :ada_cols], 0, 1).reshape(2, 6, width)
    biases = small[:, :, ada_cols:]
    biases = jnp.stack(
        [
            lax.dynamic_index_in_dim(biases, 2 * at.k, 0, False),
            lax.dynamic_index_in_dim(biases, 2 * at.k + 1, 0, False),
        ],
        axis=1,
    )
    zeros = jnp.zeros((2, 2, head_width), f32)
    bias_qkv = jnp.concatenate(
        [biases[:, :, :head_width], zeros, biases[:, :, head_width : 2 * head_width], zeros], axis=2
    )[:, :, None]
    bias_up = biases[:, :, None, 2 * head_width :]
    b_out_row, b_down_row = (v.astype(f32)[:, None] for v in (b_out, b_down))

    frames = weights.step(frames)
    inputs = frames.reshape(rows, width)
    leave, kept_one = forward_block(
        at,
        inputs,
        mods[0],
        weights,
        0,
        bias_qkv[0],
        bias_up[0],
        b_out_row[0],
        b_down_row[0],
        0,
        (0, 1, 1, 1),
    )
    mlp_one, middle = leave()
    moved = lax.all_to_all(
        middle.reshape(frames.shape), "tp", split_axis=2, concat_axis=1, tiled=True
    )
    middle = weights.step(middle)
    moved, middle = lax.optimization_barrier((moved, middle))
    moved = lax.all_to_all(moved, "ctx", split_axis=3, concat_axis=1, tiled=True)
    grid = moved.shape
    patches = grid[2] * grid[3]
    leave, kept_two = forward_block(
        at,
        moved.reshape(rows, width),
        mods[1],
        weights,
        3,
        bias_qkv[1],
        bias_up[1],
        b_out_row[1],
        b_down_row[1],
        patches,
        (1, 0, 0, 0),
    )
    sums = Sums(at)
    grad_y = cotangent.reshape(rows, width)
    grad_moved, *small_two = backward_block(
        at, grad_y, kept_two, mods[1], weights, 3, patches, sums, "DUA", "A"
    )
    mlp_two, result = leave()
    gate_two = gate_sum(grad_y, mlp_two)
    grad_moved = sums.run("A5", grad_moved)
    grad_middle = lax.all_to_all(
        grad_moved.reshape(grid), "ctx", split_axis=1, concat_axis=3, tiled=True
    )
    grad_middle = sums.run("A6", grad_middle)
    grad_middle = lax.all_to_all(grad_middle, "tp", split_axis=1, concat_axis=2, tiled=True)
    grad_middle = sums.run("A7", grad_middle)
    grad_y = grad_middle.reshape(rows, width)
    grad_frames, *small_one = backward_block(
        at, grad_y, kept_one, mods[0], weights, 0, 0, sums, "dua", "B"
    )
    gates = (gate_sum(grad_y, mlp_one), gate_two)
    grad_video = lax.all_to_all(
        grad_frames.reshape(frames.shape), "tp", split_axis=2, concat_axis=1, tiled=True
    ).astype(f32)

    grad_bias, grad_b_out, grad_b_down, grad_mod = (
        jnp.stack([one, two]) for one, two in zip(small_one, small_two)
    )
    grad_mod = jnp.concatenate([grad_mod, jnp.stack(gates)], axis=1)
    blocks = jnp.arange(at.nt)[:, None, None]
    grad_bias = jnp.where(blocks == 2 * at.k, grad_bias[:, 0], 0.0) + jnp.where(
        blocks == 2 * at.k + 1, grad_bias[:, 1], 0.0
    )
    small = jnp.concatenate(
        [grad_bias.reshape(-1), grad_b_out.reshape(-1), grad_b_down.reshape(-1)]
    )
    small, grad_mods = at.sum_all(
        small,
        grad_mod.reshape(-1),
        sums.run,
    )
    size = grad_bias.size
    grad_bias = lax.dynamic_index_in_dim(small[:size].reshape(grad_bias.shape), at.t, 0, False)
    grad_b_out, grad_b_down = small[size:].reshape(2, 2, width)
    grad_mods = jnp.moveaxis(grad_mods.reshape(at.ns, 2, 6 * width), 0, 1)
    grad_mods = lax.dynamic_slice_in_dim(grad_mods, at.t * ada_cols, ada_cols, axis=2)
    cond_rows = cond_rows.astype(f32)
    grad_w_ada = sum(
        cond_rows[i][None, :, None] * grad_mods[:, i][:, None, :] for i in range(at.ns)
    )
    grad_b_ada = jnp.sum(grad_mods, axis=1)
    grad_act = jnp.einsum(
        "bcn,bdn->cd", grad_mods, w_ada.astype(f32), precision=highest, preferred_element_type=f32
    )
    if at.ns == 2:
        grad_act = at.sum_group(at.sum_group(grad_act, "tp", 1), "tp", 2)
        grad_act = sums.run("C5", grad_act)
        ours = lax.dynamic_slice_in_dim(grad_act, at.s, 1, axis=0)
        theirs = at.swap_y(lax.dynamic_slice_in_dim(grad_act, 1 - at.s, 1, axis=0))
        grad_act = jnp.concatenate(
            [jnp.where(at.s == 0, ours, theirs), jnp.where(at.s == 0, theirs, ours)], axis=1
        )
    else:
        grad_act = lax.psum_scatter(
            lax.dynamic_update_slice_in_dim(
                jnp.zeros((at.ns, width), f32), grad_act, at.s * own_width, axis=1
            ),
            "shard",
            scatter_dimension=0,
            tiled=True,
        )
        grad_act = lax.psum(grad_act, "tp")
    grad_act, grad_video = sums.run("C6", (grad_act, grad_video))
    sums.run("C7", ())
    sums = sums.done
    grad_cond = silu_back(grad_act)[0]

    grad_w_qkv, grad_w_out = attention_grads(at, sums["a"], sums["A"], head_width)
    return (
        result.reshape(grid),
        grad_video,
        grad_cond,
        grad_w_ada,
        grad_b_ada,
        grad_w_qkv,
        grad_bias[:, : 2 * head_width].reshape(2, 2, head_width),
        grad_w_out,
        grad_b_out,
        rows_grads(at, sums["u"], sums["U"]),
        grad_bias[:, 2 * head_width :],
        jnp.swapaxes(rows_grads(at, sums["d"], sums["D"]), 1, 2),
        grad_b_down,
    )


def solution(mesh):
    in_specs = (
        P("shard", "ctx", "tp", None, None),
        P("shard", None),
        P(None, "shard", "tp"),
        P(None, "tp"),
        P(None, None, "shard", "tp"),
        P(None, None, "tp"),
        P(None, "tp", "shard"),
        P(),
        P(None, "shard", "tp"),
        P(None, "tp"),
        P(None, "tp", "shard"),
        P(),
        P("shard", None, "tp", "ctx", None),
    )
    out_specs = (
        P("shard", None, "tp", "ctx", None),
        P("shard", "ctx", "tp", None, None),
        P("shard", None),
        P(None, "shard", "tp"),
        P(None, "tp"),
        P(None, None, "shard", "tp"),
        P(None, None, "tp"),
        P(None, "tp", "shard"),
        P(),
        P(None, "shard", "tp"),
        P(None, "tp"),
        P(None, "tp", "shard"),
        P(),
    )
    return jax.shard_map(body, mesh=mesh, in_specs=in_specs, out_specs=out_specs, check_vma=False)
```

```python
from functools import partial
import math

import jax
import jax.numpy as jnp
from jax import lax
from jax.experimental import pallas as pl
from jax.experimental.pallas import tpu as pltpu
from jax.sharding import PartitionSpec as P

HEAD_DIM = 72
bf16 = jnp.bfloat16
f32 = jnp.float32
highest = lax.Precision.HIGHEST


class Place:
    def __init__(self):
        self.ns = lax.axis_size("shard")
        self.nc = lax.axis_size("ctx")
        self.nt = lax.axis_size("tp")
        self.s = lax.axis_index("shard")
        self.c = lax.axis_index("ctx")
        self.t = lax.axis_index("tp")
        self.x = self.c // 2
        self.k = self.c % 2
        self.d = jnp.where(self.k == 0, self.t, self.nt - 1 - self.t)

    def core(self, v):
        return lax.ppermute(v, "ctx", [(c, c ^ 1) for c in range(self.nc)])

    def swap_x(self, v):
        return lax.ppermute(v, "ctx", [(c, c ^ 2) for c in range(self.nc)])

    def swap_y(self, v):
        return lax.ppermute(v, "shard", [(i, i ^ 1) for i in range(self.ns)])

    def along_z(self, v, pairs):
        def at(c, d):
            return c * self.nt + (d if c % 2 == 0 else self.nt - 1 - d)

        return lax.ppermute(
            v, ("ctx", "tp"), [(at(c, i), at(c, j)) for c in range(self.nc) for i, j in pairs]
        )

    def gather_small(self, v):
        got = [v] + [
            lax.ppermute(v, "tp", [(i, i ^ step) for i in range(self.nt)])
            for step in range(1, self.nt)
        ]
        return jnp.stack([pick(self.t ^ i, got) for i in range(self.nt)])

    def sum_group(self, v, axis, step):
        size = self.nc if axis == "ctx" else self.nt
        return v + lax.ppermute(v, axis, [(i, i ^ step) for i in range(size)])

    def sum_all(self, v, per_clip, held, run):
        size = v.size
        v = jnp.concatenate([v, per_clip]).reshape(1, -1)
        v = run("C0", self.sum_group(v, "ctx", 1))
        v, held = run("C1", (self.sum_group(v, "ctx", 2), held))
        v = run("C2", self.sum_group(v, "tp", 1))
        v = run("C3", self.sum_group(v, "tp", 2))
        if self.ns != 2:
            total = lax.psum(v[0, :size], "shard")
            return total, lax.all_gather(v[:, size:], "shard", axis=0, tiled=True), held
        v, w = run("C4", (v, self.swap_y(v)))
        rows = [jnp.where(self.s == 0, v, w), jnp.where(self.s == 0, w, v)]
        return (v + w)[0, :size], jnp.concatenate(rows, axis=0)[:, size:], held

    def position(self):
        return jnp.stack([self.s, self.x, self.k]).astype(jnp.int32)

    def by_x(self, near, far):
        return [jnp.where(self.x == 0, near, far), jnp.where(self.x == 0, far, near)]

    def by_k(self, near, far):
        return [jnp.where(self.k == 0, near, far), jnp.where(self.k == 0, far, near)]


def pick(index, options):
    out = options[-1]
    for number in range(len(options) - 2, -1, -1):
        out = jnp.where(index == number, options[number], out)
    return out


def tie(values, *others):
    return lax.optimization_barrier((values, others))[0]


class Chunk:
    def __init__(self, first, common, part):
        self.first = first
        self.common = common
        self.part = part
        self.rows = common + 2 * part

    def sent(self, at, both, b):
        half, part = self.common // 2, self.part // 2
        starts = (self.first + at.k * half, self.first + self.common + at.x * self.part + at.k * part)
        cols = both.shape[2]
        return jnp.concatenate(
            [
                lax.dynamic_slice(both, (b, start, 0), (1, size, cols))[0]
                for start, size in zip(starts, (half, part))
                if size
            ],
            axis=0,
        )

    def core_step(self, at, blocks):
        got = at.core(lax.dynamic_slice_in_dim(blocks, 2 - 2 * at.k, 2, axis=0))
        mine = lax.dynamic_slice_in_dim(blocks, 2 * at.k, 2, axis=0)
        half = self.common // 2
        common = jnp.where(at.x == at.k, mine[:, :half], got[:, :half])
        if not self.part:
            return (mine, got), common
        part = jnp.concatenate([mine[:, half:], got[:, half:]], axis=1)
        return (mine, got), jnp.concatenate([common, part], axis=1), part


def assemble_kernel(place_ref, *refs, chunk):
    out_ref, turned_ref = refs[-2:]
    s, x, k = place_ref[0], place_ref[1], place_ref[2]
    width = out_ref.shape[1] // 2

    def copy(source, start, size, offset):
        if size:
            out_ref[0, pl.ds(pl.multiple_of(offset, 16), size), :] = source[
                0, start : start + size, :
            ]

    mine, got, near, far = refs[:4]
    side = refs[4] if chunk.part else None
    half, part = chunk.common // 2, chunk.part // 2
    own, other = s * width, (1 - s) * width

    def parts(source, start, base, plane):
        offset = base + chunk.common + plane * chunk.part
        copy(source, start, part, offset + k * part)
        copy(source, start + part, part, offset + (1 - k) * part)

    copy(mine, 0, half, own + k * half)
    copy(got, 0, half, own + (1 - k) * half)
    copy(mine, half, part, own + chunk.common + x * chunk.part + k * part)
    copy(got, half, part, own + chunk.common + x * chunk.part + (1 - k) * part)
    parts(side, 0, own, 1 - x)
    copy(near, 0, half, other + x * half)
    parts(near, half, other, x)
    copy(far, 0, half, other + (1 - x) * half)
    parts(far, half, other, 1 - x)
    turned_ref[0] = out_ref[0].T


def assemble(at, chunk, arrays):
    cols = arrays[0].shape[2]
    rows = 2 * chunk.rows
    return call(
        partial(assemble_kernel, chunk=chunk),
        [(a, False) for a in arrays],
        [(shape_of(2, rows, cols), False), (shape_of(2, cols, rows), False)],
        scalars=(at.position(),),
    )


class Weights:
    def __init__(self, at, arrays):
        self.at = at
        self.whole = []
        self.count = 2 * len(arrays)
        self.number = 0
        jobs = [(b, array) for b in range(2) for array in arrays]
        if at.ns != 2:
            for b, array in jobs:
                both = lax.all_gather(array[b], "tp", axis=0)
                both = lax.dynamic_slice_in_dim(both, 2 * at.k, 2, axis=0)
                both = lax.all_gather(both, "shard", axis=1, tiled=True)
                self.whole.append((both, jnp.swapaxes(both, 1, 2)))
            return
        rows = arrays[0].shape[1]
        self.plans = [
            Chunk(0, rows - 2 * part, part)
            for part in (rows // 36 * units for units in (14, 10, 8, 8, 6, 0))
        ]
        self.blocks = []
        sent = ()
        for plan, (b, array) in zip(self.plans, jobs):
            sent = plan.sent(at, tie(array, sent), b)
            self.blocks.append(lax.all_gather(sent, "tp", axis=0))
        self.held, self.near, self.far, self.side = {}, {}, {}, {}

    def step(self, main):
        if self.at.ns != 2 or self.number == self.count + 2:
            return main
        at, number = self.at, self.number
        self.number += 1
        block = self.blocks[number] if number < self.count else ()
        block, near, far, side, main = lax.optimization_barrier(
            (
                block,
                self.near.get(number - 1),
                self.far.get(number - 2),
                self.side.get(number - 1),
                main,
            )
        )
        if 0 < number <= self.count:
            self.near[number - 1], self.side[number - 1] = near, side
            self.far[number - 1] = at.swap_x(near)
        if number < self.count:
            self.held[number], *messages = self.plans[number].core_step(at, block)
            messages, main = lax.optimization_barrier((messages, main))
            self.near[number] = at.swap_y(messages[0])
            self.side[number] = at.swap_x(messages[-1]) if self.plans[number].part else ()
        if number > 1:
            m = number - 2
            sides = [self.side[m]] if self.plans[m].part else []
            arrays = [*self.held[m], self.near[m], far, *sides]
            self.whole.append(assemble(at, self.plans[m], arrays))
        return main


def scatter_z(everything):
    return lax.psum_scatter(everything, "tp", scatter_dimension=0, tiled=True)[0]


def product(left, right):
    left = jnp.concatenate(left, axis=0)
    right = jnp.concatenate(right, axis=1)
    return jnp.einsum("rd,prn->pdn", left, right, preferred_element_type=f32).astype(bf16)


def term_of(turned, right, starts, rows):
    left = [turned[pl.ds(pl.multiple_of(start, 16), rows), :] for start in starts]
    left = jnp.concatenate(left, axis=0)
    depth = right[0].shape[1]
    return sum(
        jnp.dot(left[:, i * depth : (i + 1) * depth], r[0], preferred_element_type=f32)
        for i, r in enumerate(right)
    )


def starts_of(place_ref, width, pairs, half):
    s, x = place_ref[0], place_ref[1]
    return [
        (4 * jnp.abs(s - ds) + 2 * jnp.abs(x - dx) + half) * (width // 8) for ds, dx in pairs
    ]


def away_kernel(place_ref, *refs, count):
    left, right = refs[:count], refs[count:-3]
    to_y, to_x, turned = refs[-3:]
    rows = left[0].shape[0]
    width = turned.shape[0]

    @pl.when(pl.program_id(0) == 0)
    def _():
        for i, source in enumerate(left):
            turned[:, i * rows : (i + 1) * rows] = source[...].T

    first = starts_of(place_ref, width, ((1, 0), (1, 1)), 0)
    second = starts_of(place_ref, width, ((0, 1), (1, 1)), 1)
    to_y[0] = term_of(turned, right, first, width // 8).astype(bf16)
    to_x[0] = term_of(turned, right, second, width // 8).astype(bf16)


def here_kernel(place_ref, from_y, from_x, turned, *refs):
    right = refs[:-4]
    over_y, over_x, to_x, to_y = refs[-4:]
    width = turned.shape[0]
    rows = width // 8
    first = starts_of(place_ref, width, ((0, 0), (0, 1)), 0)
    second = starts_of(place_ref, width, ((0, 0), (1, 0)), 1)
    one = term_of(turned, right, first, rows) + from_y[0].astype(f32)
    over_y[0] = one[:rows].astype(bf16)
    to_x[0] = one[rows:].astype(bf16)
    two = term_of(turned, right, second, rows) + from_x[0].astype(f32)
    over_x[0] = two[:rows].astype(bf16)
    to_y[0] = two[rows:].astype(bf16)


def join_kernel(place_ref, over_y, over_x, from_x, from_y, kept, given):
    k = place_ref[2]
    for out, flag in ((kept, k == 0), (given, k == 1)):

        @pl.when(flag)
        def _():
            out[0] = (over_y[0].astype(f32) + from_x[0].astype(f32)).astype(bf16)

        @pl.when(jnp.logical_not(flag))
        def _():
            out[0] = (over_x[0].astype(f32) + from_y[0].astype(f32)).astype(bf16)


def per_block(array):
    return pl.BlockSpec((1,) + array.shape[1:], lambda i: (i,) + (0,) * (len(array.shape) - 1))


def entire(array):
    return pl.BlockSpec(array.shape, lambda i: (0,) * len(array.shape))


def call(kernel, inputs, outputs, scratch=(), scalars=()):
    return pl.pallas_call(
        kernel,
        out_shape=tuple(a for a, _ in outputs),
        grid=(2,),
        in_specs=[pl.BlockSpec(memory_space=pltpu.SMEM)] * len(scalars)
        + [entire(a) if whole else per_block(a) for a, whole in inputs],
        out_specs=tuple(entire(a) if whole else per_block(a) for a, whole in outputs),
        scratch_shapes=list(scratch),
        cost_estimate=pl.CostEstimate(flops=0, transcendentals=0, bytes_accessed=0),
        compiler_params=pltpu.CompilerParams(vmem_limit_bytes=48 * 1024 * 1024),
    )(*scalars, *[a for a, _ in inputs])


def shape_of(*dims, kind=bf16):
    return jax.ShapeDtypeStruct(dims, kind)


def products_away(at, left, right):
    rows, width = left[0].shape
    sent = shape_of(2, width // 4, right[0].shape[2])
    return call(
        partial(away_kernel, count=len(left)),
        [(l, True) for l in left] + [(r, False) for r in right],
        [(sent, False), (sent, False), (shape_of(width, rows * len(left)), True)],
        scalars=(at.position(),),
    )


def products_here(at, turned, right, from_y, from_x):
    part = shape_of(2, from_y.shape[1] // 2, from_y.shape[2])
    return call(
        here_kernel,
        [(from_y, False), (from_x, False), (turned, True)] + [(r, False) for r in right],
        [(part, False)] * 4,
        scalars=(at.position(),),
    )


def join_halves(at, *parts):
    return call(
        join_kernel,
        [(part, False) for part in parts],
        [(shape_of(*parts[0].shape), False)] * 2,
        scalars=(at.position(),),
    )


PLAN = {
    "A0": ("pD", "1D"),
    "A1": ("pU",),
    "A2": ("2D", "1U"),
    "A3": (),
    "A4": ("pA",),
    "A5": (),
    "A6": ("2U", "1A", "zD"),
    "A7": (),
    "B0": ("pd", "2A", "1d", "zU", "fD"),
    "B1": ("pu",),
    "B2": (),
    "B3": (),
    "B4": ("2d", "1u", "zA", "fU"),
    "C0": (),
    "C1": ("eD", "pa", "fA", "2u", "1a", "zd", "eU"),
    "C2": (),
    "C3": (),
    "C4": ("2a", "zu", "fd"),
    "C5": ("za",),
    "C6": (),
    "C7": ("fu", "ed", "fa", "eA", "ea", "eu"),
}


class Sums:
    def __init__(self, at):
        self.at = at
        self.state = {}
        self.done = {}

    def offer(self, name, left, right):
        self.state[name] = (None, (list(left), list(right)))

    def run(self, place, main):
        for step in PLAN[place]:
            kind, name = step
            if name not in self.state:
                continue
            kept, pending = self.state.pop(name)
            pending, main = lax.optimization_barrier((pending, main))
            if kind == "w":
                self.state[name] = (kept, pending)
                continue
            if self.at.ns != 2:
                self.done[name] = self.generic(*pending)
                continue
            kept, messages = getattr(self, "step_" + kind)(kept, pending)
            values, main = lax.optimization_barrier(([value for _, value in messages], main))
            if kind == "e":
                self.done[name] = values
            else:
                sent = [value if how is None else how(value) for (how, _), value in zip(messages, values)]
                self.state[name] = (kept, sent)
        return main

    def generic(self, left, right):
        at = self.at
        summed = lax.psum_scatter(
            product(left, right), "shard", scatter_dimension=1, tiled=True
        )
        half = summed.shape[1] // 2
        halves = [summed[:, :half], summed[:, half:]]
        got = at.core(jnp.where(at.k == 0, halves[1], halves[0]))
        kept = jnp.where(at.k == 0, halves[0], halves[1])
        mine = scatter_z(jnp.concatenate(at.by_k(kept, got), axis=0))
        mine = (mine.astype(f32) + at.swap_x(mine).astype(f32)).astype(bf16)
        return jnp.concatenate(at.by_k(mine, at.core(mine)), axis=0)

    def step_p(self, _, pending):
        left, right = pending
        to_y, to_x, turned = products_away(self.at, left, right)
        return (right, turned), [(None, to_y), (None, to_x)]

    def step_1(self, kept, pending):
        to_y, to_x = pending
        return kept, [(self.at.swap_y, to_y), (self.at.swap_x, to_x)]

    def step_2(self, kept, pending):
        right, turned = kept
        over_y, over_x, to_x, to_y = products_here(self.at, turned, right, *pending)
        return (over_y, over_x), [(self.at.swap_x, to_x), (self.at.swap_y, to_y)]

    def step_z(self, kept, pending):
        kept, given = join_halves(self.at, *kept, *pending)
        everything = jnp.concatenate(self.at.by_k(kept, self.at.core(given)), axis=0)
        return None, [(scatter_z, everything)]

    def step_f(self, _, pending):
        (mine,) = pending
        return mine, [(self.at.swap_x, mine)]

    def step_e(self, mine, pending):
        (far,) = pending
        mine = jnp.stack(self.at.by_x(mine, far))
        return None, [(None, mine), (None, self.at.core(mine))]


def rows_in_place(place_ref, mine, theirs, target, b):
    k = place_ref[2]
    rows = mine.shape[1]
    for ref, member in ((mine, k), (theirs, 1 - k)):
        for x in range(2):
            start = pl.multiple_of((2 * x + member) * rows, 8)
            target[b, pl.ds(start, rows), :] = ref[x].astype(f32)


def rows_kernel(place_ref, *refs):
    for b in range(2):
        rows_in_place(place_ref, refs[2 * b], refs[2 * b + 1], refs[4], b)


def turned_kernel(place_ref, *refs):
    qkv_ref, out_ref, target = refs[4:]
    cols = out_ref.shape[1]
    for b in range(2):
        rows_in_place(place_ref, refs[2 * b], refs[2 * b + 1], target, b)
        values = target[b].T
        for number in range(3):
            qkv_ref[b, number] = values[number * cols : (number + 1) * cols]
        out_ref[b] = values[3 * cols :]


def simple_call(kernel, inputs, outputs, scratch=(), scalars=()):
    return pl.pallas_call(
        kernel,
        out_shape=tuple(outputs),
        in_specs=[pl.BlockSpec(memory_space=pltpu.SMEM)] * len(scalars)
        + [pl.BlockSpec(memory_space=pltpu.VMEM)] * len(inputs),
        out_specs=tuple(pl.BlockSpec(memory_space=pltpu.VMEM) for _ in outputs),
        scratch_shapes=list(scratch),
        cost_estimate=pl.CostEstimate(flops=0, transcendentals=0, bytes_accessed=0),
        compiler_params=pltpu.CompilerParams(vmem_limit_bytes=48 * 1024 * 1024),
    )(*scalars, *inputs)


def rows_grads(at, first, second):
    if at.ns != 2:
        return jnp.stack([first, second]).astype(f32)
    _, rows, cols = first[0].shape
    shape = shape_of(2, 4 * rows, cols, kind=f32)
    return simple_call(rows_kernel, [*first, *second], [shape], scalars=(at.position(),))[0]


def attention_grads(at, first, second, head_width):
    if at.ns != 2:
        both = jnp.swapaxes(jnp.stack([first, second]).astype(f32), 1, 2)
        qkv = both[:, : 3 * head_width].reshape(2, 3, head_width, -1)
        return jnp.swapaxes(qkv, 2, 3), both[:, 3 * head_width :]
    _, rows, cols = first[0].shape
    qkv, out = simple_call(
        turned_kernel,
        [*first, *second],
        [
            shape_of(2, 3, head_width, 4 * rows, kind=f32),
            shape_of(2, head_width, 4 * rows, kind=f32),
        ],
        scratch=[pltpu.VMEM((2, 4 * rows, cols), f32)],
        scalars=(at.position(),),
    )
    return jnp.swapaxes(qkv, 2, 3), out


def prepare_kernel(qkv_ref, out_ref, target):
    for b in range(2):
        rows = [qkv_ref[b, number].T for number in range(3)] + [out_ref[b].T]
        target[b] = jnp.concatenate(rows, axis=1)


def attention_weights(w_qkv, w_out):
    _, _, rows, cols = w_qkv.shape
    return simple_call(
        prepare_kernel, [jnp.swapaxes(w_qkv, 2, 3), w_out], [shape_of(2, rows, 4 * cols)]
    )[0]


def heads_of(values, number, head):
    start = number * 4 * HEAD_DIM + head * HEAD_DIM
    return values[:, start : start + HEAD_DIM]


def probs_of(query, key, temporal):
    scores = lax.dot_general(
        query, key, (((1,), (1,)), ((), ())), preferred_element_type=f32
    ) * (1.0 / math.sqrt(HEAD_DIM))
    if temporal:
        rows = lax.broadcasted_iota(jnp.int32, scores.shape, 0) % temporal
        cols = lax.broadcasted_iota(jnp.int32, scores.shape, 1) % temporal
        scores = jnp.where(rows == cols, scores, -jnp.inf)
    weights = jnp.exp(scores - jnp.max(scores, axis=-1, keepdims=True))
    return weights / jnp.sum(weights, axis=-1, keepdims=True)


def attend_kernel(qkv_ref, out_ref, *, temporal):
    values = qkv_ref[0]
    results = [jnp.zeros((values.shape[0], 12 * HEAD_DIM), bf16)]
    for head in range(4):
        probs = probs_of(heads_of(values, 0, head), heads_of(values, 1, head), temporal)
        results.append(
            jnp.dot(
                probs.astype(bf16), heads_of(values, 2, head), preferred_element_type=f32
            ).astype(bf16)
        )
    out_ref[0] = jnp.concatenate(results, axis=1)


def attend_back_kernel(qkv_ref, grad_ref, out_ref, *, temporal):
    factor = 1.0 / math.sqrt(HEAD_DIM)
    values = qkv_ref[0]
    grads = grad_ref[0]
    queries, keys, vals = [], [], []
    for head in range(4):
        query, key, value = (heads_of(values, number, head) for number in range(3))
        grad = heads_of(grads, 3, head)
        probs = probs_of(query, key, temporal)
        vals.append(
            lax.dot_general(
                probs.astype(bf16), grad, (((0,), (0,)), ((), ())), preferred_element_type=f32
            ).astype(bf16)
        )
        grad_probs = lax.dot_general(
            grad, value, (((1,), (1,)), ((), ())), preferred_element_type=f32
        )
        inner = jnp.sum(grad_probs * probs, axis=-1, keepdims=True)
        grad_scores = (probs * (grad_probs - inner)).astype(bf16)
        queries.append(
            (jnp.dot(grad_scores, key, preferred_element_type=f32) * factor).astype(bf16)
        )
        keys.append(
            (
                lax.dot_general(
                    grad_scores, query, (((0,), (0,)), ((), ())), preferred_element_type=f32
                )
                * factor
            ).astype(bf16)
        )
    zeros = jnp.zeros((values.shape[0], 4 * HEAD_DIM), bf16)
    out_ref[0] = jnp.concatenate(queries + keys + vals + [zeros], axis=1)


def call_attention(kernel, arrays, rows, temporal):
    shape = arrays[0].shape
    spec = pl.BlockSpec((1, rows, shape[2]), lambda i, j: (i, j, 0))
    return pl.pallas_call(
        partial(kernel, temporal=temporal),
        out_shape=shape_of(*shape),
        grid=(shape[0], shape[1] // rows),
        in_specs=[spec] * len(arrays),
        out_specs=spec,
        cost_estimate=pl.CostEstimate(flops=0, transcendentals=0, bytes_accessed=0),
        compiler_params=pltpu.CompilerParams(vmem_limit_bytes=48 * 1024 * 1024),
    )(*arrays)


SLOPE = math.sqrt(2.0 / math.pi)


def gelu(u):
    return 0.5 * u * (1.0 + jnp.tanh(SLOPE * (u + 0.044715 * (u * u * u))))


def gelu_slope(u):
    t = jnp.tanh(SLOPE * (u + 0.044715 * (u * u * u)))
    inner = SLOPE * (1.0 + 3.0 * 0.044715 * (u * u))
    return 0.5 * (1.0 + t) + 0.5 * u * (1.0 - t * t) * inner


def times_of(own, other, weight):
    left = jnp.concatenate([own[...], other[...]], axis=0)
    return jnp.dot(left, weight[0], preferred_element_type=f32)


def qkv_kernel(own, other, weight, bias, out):
    out[0] = (times_of(own, other, weight) + bias[0]).astype(bf16)


def plain_kernel(own, other, weight, out):
    out[0] = times_of(own, other, weight).astype(bf16)


def up_kernel(own, other, weight, bias, up, activated):
    values = times_of(own, other, weight) + bias[0]
    up[0] = values
    activated[0] = gelu(values).astype(bf16)


def up_back_kernel(own, other, weight, up, out, sums):
    values = (gelu_slope(up[0]) * times_of(own, other, weight)).astype(bf16)
    out[0] = values
    sums[0] = jnp.sum(values.astype(f32), axis=0, keepdims=True)


def back_kernel(left, weight, own, other, total):
    term = jnp.dot(left[0], weight[0], preferred_element_type=f32)
    rows = own.shape[0]

    @pl.when(pl.program_id(0) == 0)
    def _():
        total[...] = term

    @pl.when(pl.program_id(0) == 1)
    def _():
        own[...] = total[:rows] + term[:rows]
        other[...] = (total[rows:] + term[rows:]).astype(bf16)


def times(kernel, pair, weight, extra=(), outputs=()):
    rows = 2 * pair[0].shape[0]
    cols = weight.shape[2]
    return call(
        kernel,
        [(pair[0], True), (pair[1], True), (weight, False)] + [(e, False) for e in extra],
        [(shape_of(2, rows if tall else 1, cols, kind=kind), False) for tall, kind in outputs],
    )


def times_back(at, left, weight):
    rows, width = left.shape[1] // 2, weight.shape[2]
    own, other = call(
        back_kernel,
        [(left, False), (weight, False)],
        [(shape_of(rows, width, kind=f32), True), (shape_of(rows, width), True)],
        scratch=[pltpu.VMEM((2 * rows, width), f32)],
    )
    return own, at.core(other)


def normalized(values):
    average = jnp.mean(values, axis=-1, keepdims=True)
    centered = values - average
    inverse = lax.rsqrt(jnp.mean(centered * centered, axis=-1, keepdims=True) + 1e-06)
    return centered * inverse, inverse


def norm_back(grad, normal, inverse, factor):
    dn = grad * (1.0 + factor)
    return (
        dn
        - jnp.mean(dn, axis=-1, keepdims=True)
        - normal * jnp.mean(dn * normal, axis=-1, keepdims=True)
    ) * inverse


def token_sum(values):
    return jnp.sum(values, axis=0, keepdims=True)


def mod_of(mod, number):
    return mod[number : number + 1, :]


def enter_kernel(inputs, mod, hidden):
    normal, _ = normalized(inputs[...].astype(f32))
    hidden[...] = (normal * (1.0 + mod_of(mod, 1)) + mod_of(mod, 0)).astype(bf16)


def middle_kernel(own, got, inputs, mod, bias, attn, after, hidden):
    attn_out = own[...] + got[...].astype(f32) + bias[...]
    attn[...] = attn_out
    values = inputs[...].astype(f32) + mod_of(mod, 2) * attn_out
    after[...] = values
    normal, _ = normalized(values)
    hidden[...] = (normal * (1.0 + mod_of(mod, 4)) + mod_of(mod, 3)).astype(bf16)


def leave_kernel(own, got, after, mod, bias, mlp, result):
    mlp_out = own[...] + got[...].astype(f32) + bias[...]
    mlp[...] = mlp_out
    result[...] = (after[...] + mod_of(mod, 5) * mlp_out).astype(bf16)


def enter_back_kernel(grad_y, mod, grad_mlp, sums):
    values = (mod_of(mod, 5) * grad_y[...].astype(f32)).astype(bf16)
    grad_mlp[...] = values
    sums[...] = token_sum(values.astype(f32))


def gate_kernel(grad_y, mlp, sums):
    sums[...] = token_sum(grad_y[...].astype(f32) * mlp[...])


def gate_sum(grad_y, mlp):
    return simple_call(gate_kernel, [grad_y, mlp], [shape_of(1, mlp.shape[1], kind=f32)])[0][0]


def middle_back_kernel(own, got, after, grad_y, attn, mod, grad_after, grad_attn, sums):
    grad = own[...] + got[...].astype(f32)
    normal, inverse = normalized(after[...])
    sums[0:1] = token_sum(grad)
    sums[1:2] = token_sum(grad * normal)
    total = grad_y[...].astype(f32) + norm_back(grad, normal, inverse, mod_of(mod, 4))
    grad_after[...] = total
    values = (mod_of(mod, 2) * total).astype(bf16)
    grad_attn[...] = values
    sums[2:3] = token_sum(total * attn[...])
    sums[3:4] = token_sum(values.astype(f32))


def leave_back_kernel(own, got, inputs, grad_after, mod, grad_inputs, sums):
    grad = own[...] + got[...].astype(f32)
    normal, inverse = normalized(inputs[...].astype(f32))
    sums[0:1] = token_sum(grad)
    sums[1:2] = token_sum(grad * normal)
    grad_inputs[...] = (
        grad_after[...] + norm_back(grad, normal, inverse, mod_of(mod, 1))
    ).astype(bf16)


def forward_block(
    at, inputs, mod, weights, first, bias_qkv, bias_up, b_out, b_down, temporal, steps
):
    rows, width = inputs.shape
    for _ in range(steps[0]):
        inputs = weights.step(inputs)
    wide = shape_of(rows, width, kind=f32)
    low = shape_of(rows, width)
    (hidden,) = simple_call(enter_kernel, [inputs, mod], [low])
    hidden = (hidden, at.core(hidden))
    for _ in range(steps[1]):
        hidden = weights.step(hidden)
    w_attn, w_attn_t = weights.whole[first]
    (qkv,) = times(qkv_kernel, hidden, w_attn, [bias_qkv], [(True, bf16)])
    attended = call_attention(attend_kernel, [qkv], rows, temporal)
    own, got = times_back(at, attended, w_attn_t)
    attn, after, hidden_two = simple_call(
        middle_kernel, [own, got, inputs, mod, b_out], [wide, wide, low]
    )
    hidden_two = (hidden_two, at.core(hidden_two))
    for _ in range(steps[2]):
        hidden_two = weights.step(hidden_two)
    w_up = weights.whole[first + 1][0]
    up, activated = times(up_kernel, hidden_two, w_up, [bias_up], [(True, f32), (True, bf16)])
    for _ in range(steps[3]):
        activated = weights.step(activated)

    def leave():
        own, got = times_back(at, activated, weights.whole[first + 2][1])
        return simple_call(leave_kernel, [own, got, after, mod, b_down], [wide, low])

    return leave, (inputs, hidden, qkv, attended, attn, after, hidden_two, up, activated)


def backward_block(at, grad_y, kept, mod, weights, first, temporal, sums, names, place):
    inputs, hidden, qkv, attended, attn, after, hidden_two, up, activated = kept
    rows, width = inputs.shape
    wide = shape_of(rows, width, kind=f32)
    low = shape_of(rows, width)
    grad_mlp, sums_m = simple_call(
        enter_back_kernel, [grad_y, mod], [low, shape_of(1, width, kind=f32)]
    )
    grad_mlp = (grad_mlp, at.core(grad_mlp))
    sums.offer(names[0], grad_mlp, [activated])
    grad_mlp = weights.step(sums.run(place + "0", grad_mlp))
    (w_attn, w_attn_t), (_, w_up_t), (w_down, _) = weights.whole[first : first + 3]
    grad_up, grad_b_up = times(
        up_back_kernel, grad_mlp, w_down, [up], [(True, bf16), (False, f32)]
    )
    sums.offer(names[1], hidden_two, [grad_up])
    grad_up = sums.run(place + "1", grad_up)
    own, got = times_back(at, grad_up, w_up_t)
    grad_after, grad_attn, sums_a = simple_call(
        middle_back_kernel,
        [own, got, after, grad_y, attn, mod],
        [wide, low, shape_of(4, width, kind=f32)],
    )
    grad_attn = (grad_attn, at.core(grad_attn))
    grad_attn = sums.run(place + "2", grad_attn)
    (grad_attended,) = times(plain_kernel, grad_attn, w_attn, [], [(True, bf16)])
    grad_attended = sums.run(place + "3", grad_attended)
    grad_qkv = call_attention(attend_back_kernel, [qkv, grad_attended], rows, temporal)
    sums.offer(names[2], hidden + grad_attn, [grad_qkv, attended])
    own, got = times_back(at, grad_qkv, w_attn_t)
    own = sums.run(place + "4", own)
    grad_inputs, sums_i = simple_call(
        leave_back_kernel,
        [own, got, inputs, grad_after, mod],
        [low, shape_of(2, width, kind=f32)],
    )
    grad_mod = jnp.concatenate([sums_i[0], sums_i[1], sums_a[2], sums_a[0], sums_a[1]])
    grad_b_qkv = jnp.sum(grad_qkv, axis=1, dtype=f32)
    cols = grad_b_qkv.shape[1] // 4
    grad_bias = jnp.concatenate(
        [grad_b_qkv[:, :cols], grad_b_qkv[:, 2 * cols : 3 * cols], grad_b_up[:, 0]], axis=1
    )
    return grad_inputs, grad_bias, sums_a[3], sums_m[0], grad_mod


def body(
    video, cond, w_ada, b_ada, w_qkv, b_qv, w_out, b_out, w_up, b_up, w_down, b_down, cotangent
):
    at = Place()
    width = video.shape[-1]
    own_width = w_up.shape[1]
    head_width = w_qkv.shape[3]
    silu_value, silu_back = jax.vjp(jax.nn.silu, cond.astype(f32))
    cond_act = silu_value.astype(bf16)
    if at.ns == 2:
        other = at.swap_y(cond_act)
        cond_all = jnp.concatenate(
            [jnp.where(at.s == 0, cond_act, other), jnp.where(at.s == 0, other, cond_act)], axis=0
        )
    else:
        cond_all = lax.all_gather(cond_act, "shard", axis=0, tiled=True)
    cond_rows = lax.dynamic_slice_in_dim(cond_all, at.s * own_width, own_width, axis=1)
    mod_part = jnp.einsum("cd,bdn->cbn", cond_rows, w_ada, preferred_element_type=f32)
    if at.ns == 2:
        kept = lax.dynamic_index_in_dim(mod_part, at.s, 0, False)
        mod_part = kept + at.swap_y(lax.dynamic_index_in_dim(mod_part, 1 - at.s, 0, False))
    else:
        mod_part = lax.psum_scatter(mod_part, "shard", scatter_dimension=0, tiled=True)[0]
    ada_cols = w_ada.shape[2]
    small = jnp.concatenate(
        [mod_part + b_ada, b_qv.reshape(2, -1).astype(f32), b_up.astype(f32)], axis=1
    )

    small = at.gather_small(small)
    arrays = (attention_weights(w_qkv, w_out), w_up, jnp.swapaxes(w_down, 1, 2))
    frames = lax.all_to_all(video, "tp", split_axis=1, concat_axis=2, tiled=True)
    rows = frames.size // width
    weights = Weights(at, arrays)
    small, frames = weights.step((small, frames))
    mods = jnp.moveaxis(small[:, :, :ada_cols], 0, 1).reshape(2, 6, width)
    biases = small[:, :, ada_cols:]
    biases = jnp.stack(
        [
            lax.dynamic_index_in_dim(biases, 2 * at.k, 0, False),
            lax.dynamic_index_in_dim(biases, 2 * at.k + 1, 0, False),
        ],
        axis=1,
    )
    zeros = jnp.zeros((2, 2, head_width), f32)
    bias_qkv = jnp.concatenate(
        [biases[:, :, :head_width], zeros, biases[:, :, head_width : 2 * head_width], zeros], axis=2
    )[:, :, None]
    bias_up = biases[:, :, None, 2 * head_width :]
    b_out_row, b_down_row = (v.astype(f32)[:, None] for v in (b_out, b_down))

    frames = weights.step(frames)
    inputs = frames.reshape(rows, width)
    leave, kept_one = forward_block(
        at,
        inputs,
        mods[0],
        weights,
        0,
        bias_qkv[0],
        bias_up[0],
        b_out_row[0],
        b_down_row[0],
        0,
        (0, 1, 1, 1),
    )
    mlp_one, middle = leave()
    moved = lax.all_to_all(
        middle.reshape(frames.shape), "tp", split_axis=2, concat_axis=1, tiled=True
    )
    middle = weights.step(middle)
    moved, middle = lax.optimization_barrier((moved, middle))
    moved = lax.all_to_all(moved, "ctx", split_axis=3, concat_axis=1, tiled=True)
    grid = moved.shape
    patches = grid[2] * grid[3]
    leave, kept_two = forward_block(
        at,
        moved.reshape(rows, width),
        mods[1],
        weights,
        3,
        bias_qkv[1],
        bias_up[1],
        b_out_row[1],
        b_down_row[1],
        patches,
        (1, 0, 0, 0),
    )
    sums = Sums(at)
    grad_y = cotangent.reshape(rows, width)
    grad_moved, *small_two = backward_block(
        at, grad_y, kept_two, mods[1], weights, 3, patches, sums, "DUA", "A"
    )
    mlp_two, result = leave()
    gate_two = gate_sum(grad_y, mlp_two)
    grad_moved = sums.run("A5", grad_moved)
    grad_middle = lax.all_to_all(
        grad_moved.reshape(grid), "ctx", split_axis=1, concat_axis=3, tiled=True
    )
    grad_middle = sums.run("A6", grad_middle)
    grad_middle = lax.all_to_all(grad_middle, "tp", split_axis=1, concat_axis=2, tiled=True)
    grad_middle = sums.run("A7", grad_middle)
    grad_y = grad_middle.reshape(rows, width)
    grad_frames, *small_one = backward_block(
        at, grad_y, kept_one, mods[0], weights, 0, 0, sums, "dua", "B"
    )
    gates = (gate_sum(grad_y, mlp_one), gate_two)
    grad_video = lax.all_to_all(
        grad_frames.reshape(frames.shape), "tp", split_axis=2, concat_axis=1, tiled=True
    )

    grad_bias, grad_b_out, grad_b_down, grad_mod = (
        jnp.stack([one, two]) for one, two in zip(small_one, small_two)
    )
    grad_mod = jnp.concatenate([grad_mod, jnp.stack(gates)], axis=1)
    blocks = jnp.arange(at.nt)[:, None, None]
    grad_bias = jnp.where(blocks == 2 * at.k, grad_bias[:, 0], 0.0) + jnp.where(
        blocks == 2 * at.k + 1, grad_bias[:, 1], 0.0
    )
    small = jnp.concatenate(
        [grad_bias.reshape(-1), grad_b_out.reshape(-1), grad_b_down.reshape(-1)]
    )
    small, grad_mods, grad_video = at.sum_all(
        small,
        grad_mod.reshape(-1),
        grad_video,
        sums.run,
    )
    size = grad_bias.size
    grad_bias = lax.dynamic_index_in_dim(small[:size].reshape(grad_bias.shape), at.t, 0, False)
    grad_b_out, grad_b_down = small[size:].reshape(2, 2, width)
    grad_mods = jnp.moveaxis(grad_mods.reshape(at.ns, 2, 6 * width), 0, 1)
    grad_mods = lax.dynamic_slice_in_dim(grad_mods, at.t * ada_cols, ada_cols, axis=2)
    cond_rows = cond_rows.astype(f32)
    grad_w_ada = sum(
        cond_rows[i][None, :, None] * grad_mods[:, i][:, None, :] for i in range(at.ns)
    )
    grad_b_ada = jnp.sum(grad_mods, axis=1)
    grad_act = jnp.einsum(
        "bcn,bdn->cd", grad_mods, w_ada.astype(f32), precision=highest, preferred_element_type=f32
    )
    if at.ns == 2:
        grad_act = at.sum_group(at.sum_group(grad_act, "tp", 1), "tp", 2)
        grad_act = sums.run("C5", grad_act)
        ours = lax.dynamic_slice_in_dim(grad_act, at.s, 1, axis=0)
        theirs = at.swap_y(lax.dynamic_slice_in_dim(grad_act, 1 - at.s, 1, axis=0))
        grad_act = jnp.concatenate(
            [jnp.where(at.s == 0, ours, theirs), jnp.where(at.s == 0, theirs, ours)], axis=1
        )
    else:
        grad_act = lax.psum_scatter(
            lax.dynamic_update_slice_in_dim(
                jnp.zeros((at.ns, width), f32), grad_act, at.s * own_width, axis=1
            ),
            "shard",
            scatter_dimension=0,
            tiled=True,
        )
        grad_act = lax.psum(grad_act, "tp")
    grad_act = sums.run("C6", grad_act)
    sums.run("C7", ())
    sums = sums.done
    grad_cond = silu_back(grad_act)[0]

    grad_w_qkv, grad_w_out = attention_grads(at, sums["a"], sums["A"], head_width)
    return (
        result.reshape(grid),
        grad_video.astype(f32),
        grad_cond,
        grad_w_ada,
        grad_b_ada,
        grad_w_qkv,
        grad_bias[:, : 2 * head_width].reshape(2, 2, head_width),
        grad_w_out,
        grad_b_out,
        rows_grads(at, sums["u"], sums["U"]),
        grad_bias[:, 2 * head_width :],
        jnp.swapaxes(rows_grads(at, sums["d"], sums["D"]), 1, 2),
        grad_b_down,
    )


def solution(mesh):
    in_specs = (
        P("shard", "ctx", "tp", None, None),
        P("shard", None),
        P(None, "shard", "tp"),
        P(None, "tp"),
        P(None, None, "shard", "tp"),
        P(None, None, "tp"),
        P(None, "tp", "shard"),
        P(),
        P(None, "shard", "tp"),
        P(None, "tp"),
        P(None, "tp", "shard"),
        P(),
        P("shard", None, "tp", "ctx", None),
    )
    out_specs = (
        P("shard", None, "tp", "ctx", None),
        P("shard", "ctx", "tp", None, None),
        P("shard", None),
        P(None, "shard", "tp"),
        P(None, "tp"),
        P(None, None, "shard", "tp"),
        P(None, None, "tp"),
        P(None, "tp", "shard"),
        P(),
        P(None, "shard", "tp"),
        P(None, "tp"),
        P(None, "tp", "shard"),
        P(),
    )
    return jax.shard_map(body, mesh=mesh, in_specs=in_specs, out_specs=out_specs, check_vma=False)
```

```python
from functools import partial
import math

import jax
import jax.numpy as jnp
from jax import lax
from jax.experimental import pallas as pl
from jax.experimental.pallas import tpu as pltpu
from jax.sharding import PartitionSpec as P

HEAD_DIM = 72
bf16 = jnp.bfloat16
f32 = jnp.float32
highest = lax.Precision.HIGHEST


class Place:
    def __init__(self):
        self.ns = lax.axis_size("shard")
        self.nc = lax.axis_size("ctx")
        self.nt = lax.axis_size("tp")
        self.s = lax.axis_index("shard")
        self.c = lax.axis_index("ctx")
        self.t = lax.axis_index("tp")
        self.x = self.c // 2
        self.k = self.c % 2
        self.d = jnp.where(self.k == 0, self.t, self.nt - 1 - self.t)

    def core(self, v):
        return lax.ppermute(v, "ctx", [(c, c ^ 1) for c in range(self.nc)])

    def swap_x(self, v):
        return lax.ppermute(v, "ctx", [(c, c ^ 2) for c in range(self.nc)])

    def swap_y(self, v):
        return lax.ppermute(v, "shard", [(i, i ^ 1) for i in range(self.ns)])

    def along_z(self, v, pairs):
        def at(c, d):
            return c * self.nt + (d if c % 2 == 0 else self.nt - 1 - d)

        return lax.ppermute(
            v, ("ctx", "tp"), [(at(c, i), at(c, j)) for c in range(self.nc) for i, j in pairs]
        )

    def gather_small(self, v):
        got = [v] + [
            lax.ppermute(v, "tp", [(i, i ^ step) for i in range(self.nt)])
            for step in range(1, self.nt)
        ]
        return jnp.stack([pick(self.t ^ i, got) for i in range(self.nt)])

    def sum_group(self, v, axis, step):
        size = self.nc if axis == "ctx" else self.nt
        return v + lax.ppermute(v, axis, [(i, i ^ step) for i in range(size)])

    def sum_all(self, v, per_clip, held, run):
        size = v.size
        v = jnp.concatenate([v, per_clip]).reshape(1, -1)
        v = run("C0", self.sum_group(v, "ctx", 1))
        v, held = run("C1", (self.sum_group(v, "ctx", 2), held))
        v = run("C2", self.sum_group(v, "tp", 1))
        v = run("C3", self.sum_group(v, "tp", 2))
        if self.ns != 2:
            total = lax.psum(v[0, :size], "shard")
            return total, lax.all_gather(v[:, size:], "shard", axis=0, tiled=True), held
        v, w = run("C4", (v, self.swap_y(v)))
        rows = [jnp.where(self.s == 0, v, w), jnp.where(self.s == 0, w, v)]
        return (v + w)[0, :size], jnp.concatenate(rows, axis=0)[:, size:], held

    def position(self):
        return jnp.stack([self.s, self.x, self.k]).astype(jnp.int32)

    def by_x(self, near, far):
        return [jnp.where(self.x == 0, near, far), jnp.where(self.x == 0, far, near)]

    def by_k(self, near, far):
        return [jnp.where(self.k == 0, near, far), jnp.where(self.k == 0, far, near)]


def pick(index, options):
    out = options[-1]
    for number in range(len(options) - 2, -1, -1):
        out = jnp.where(index == number, options[number], out)
    return out


def tie(values, *others):
    return lax.optimization_barrier((values, others))[0]


class Chunk:
    def __init__(self, first, common, part):
        self.first = first
        self.common = common
        self.part = part
        self.rows = common + 2 * part

    def sent(self, at, both, b):
        half, part = self.common // 2, self.part // 2
        starts = (self.first + at.k * half, self.first + self.common + at.x * self.part + at.k * part)
        cols = both.shape[2]
        return jnp.concatenate(
            [
                lax.dynamic_slice(both, (b, start, 0), (1, size, cols))[0]
                for start, size in zip(starts, (half, part))
                if size
            ],
            axis=0,
        )

    def core_step(self, at, blocks):
        got = at.core(lax.dynamic_slice_in_dim(blocks, 2 - 2 * at.k, 2, axis=0))
        mine = lax.dynamic_slice_in_dim(blocks, 2 * at.k, 2, axis=0)
        half = self.common // 2
        common = jnp.where(at.x == at.k, mine[:, :half], got[:, :half])
        if not self.part:
            return (mine, got), common
        part = jnp.concatenate([mine[:, half:], got[:, half:]], axis=1)
        return (mine, got), jnp.concatenate([common, part], axis=1), part


def assemble_kernel(place_ref, *refs, chunk):
    out_ref, turned_ref = refs[-2:]
    s, x, k = place_ref[0], place_ref[1], place_ref[2]
    width = out_ref.shape[1] // 2

    def copy(source, start, size, offset):
        if size:
            out_ref[0, pl.ds(pl.multiple_of(offset, 16), size), :] = source[
                0, start : start + size, :
            ]

    mine, got, near, far = refs[:4]
    side = refs[4] if chunk.part else None
    half, part = chunk.common // 2, chunk.part // 2
    own, other = s * width, (1 - s) * width

    def parts(source, start, base, plane):
        offset = base + chunk.common + plane * chunk.part
        copy(source, start, part, offset + k * part)
        copy(source, start + part, part, offset + (1 - k) * part)

    copy(mine, 0, half, own + k * half)
    copy(got, 0, half, own + (1 - k) * half)
    copy(mine, half, part, own + chunk.common + x * chunk.part + k * part)
    copy(got, half, part, own + chunk.common + x * chunk.part + (1 - k) * part)
    parts(side, 0, own, 1 - x)
    copy(near, 0, half, other + x * half)
    parts(near, half, other, x)
    copy(far, 0, half, other + (1 - x) * half)
    parts(far, half, other, 1 - x)
    turned_ref[0] = out_ref[0].T


def assemble(at, chunk, arrays):
    cols = arrays[0].shape[2]
    rows = 2 * chunk.rows
    return call(
        partial(assemble_kernel, chunk=chunk),
        [(a, False) for a in arrays],
        [(shape_of(2, rows, cols), False), (shape_of(2, cols, rows), False)],
        scalars=(at.position(),),
    )


class Weights:
    def __init__(self, at, arrays):
        self.at = at
        self.whole = []
        self.count = 2 * len(arrays)
        self.number = 0
        jobs = [(b, array) for b in range(2) for array in arrays]
        if at.ns != 2:
            for b, array in jobs:
                both = lax.all_gather(array[b], "tp", axis=0)
                both = lax.dynamic_slice_in_dim(both, 2 * at.k, 2, axis=0)
                both = lax.all_gather(both, "shard", axis=1, tiled=True)
                self.whole.append((both, jnp.swapaxes(both, 1, 2)))
            return
        rows = arrays[0].shape[1]
        self.plans = [
            Chunk(0, rows - 2 * part, part)
            for part in (rows // 36 * units for units in (14, 12, 10, 8, 6, 0))
        ]
        self.blocks = []
        sent = ()
        for plan, (b, array) in zip(self.plans, jobs):
            sent = plan.sent(at, tie(array, sent), b)
            self.blocks.append(lax.all_gather(sent, "tp", axis=0))
        self.held, self.near, self.far, self.side = {}, {}, {}, {}

    def step(self, main):
        if self.at.ns != 2 or self.number == self.count + 2:
            return main
        at, number = self.at, self.number
        self.number += 1
        block = self.blocks[number] if number < self.count else ()
        block, near, far, side, main = lax.optimization_barrier(
            (
                block,
                self.near.get(number - 1),
                self.far.get(number - 2),
                self.side.get(number - 1),
                main,
            )
        )
        if 0 < number <= self.count:
            self.near[number - 1], self.side[number - 1] = near, side
            self.far[number - 1] = at.swap_x(near)
        if number < self.count:
            self.held[number], *messages = self.plans[number].core_step(at, block)
            messages, main = lax.optimization_barrier((messages, main))
            self.near[number] = at.swap_y(messages[0])
            self.side[number] = at.swap_x(messages[-1]) if self.plans[number].part else ()
        if number > 1:
            m = number - 2
            sides = [self.side[m]] if self.plans[m].part else []
            arrays = [*self.held[m], self.near[m], far, *sides]
            self.whole.append(assemble(at, self.plans[m], arrays))
        return main


def scatter_z(everything):
    return lax.psum_scatter(everything, "tp", scatter_dimension=0, tiled=True)[0]


def product(left, right):
    left = jnp.concatenate(left, axis=0)
    right = jnp.concatenate(right, axis=1)
    return jnp.einsum("rd,prn->pdn", left, right, preferred_element_type=f32).astype(bf16)


def term_of(turned, right, starts, rows):
    left = [turned[pl.ds(pl.multiple_of(start, 16), rows), :] for start in starts]
    left = jnp.concatenate(left, axis=0)
    depth = right[0].shape[1]
    return sum(
        jnp.dot(left[:, i * depth : (i + 1) * depth], r[0], preferred_element_type=f32)
        for i, r in enumerate(right)
    )


def starts_of(place_ref, width, pairs, half):
    s, x = place_ref[0], place_ref[1]
    return [
        (4 * jnp.abs(s - ds) + 2 * jnp.abs(x - dx) + half) * (width // 8) for ds, dx in pairs
    ]


def away_kernel(place_ref, *refs, count):
    left, right = refs[:count], refs[count:-3]
    to_y, to_x, turned = refs[-3:]
    rows = left[0].shape[0]
    width = turned.shape[0]

    @pl.when(pl.program_id(0) == 0)
    def _():
        for i, source in enumerate(left):
            turned[:, i * rows : (i + 1) * rows] = source[...].T

    first = starts_of(place_ref, width, ((1, 0), (1, 1)), 0)
    second = starts_of(place_ref, width, ((0, 1), (1, 1)), 1)
    to_y[0] = term_of(turned, right, first, width // 8).astype(bf16)
    to_x[0] = term_of(turned, right, second, width // 8).astype(bf16)


def here_kernel(place_ref, from_y, from_x, turned, *refs):
    right = refs[:-4]
    over_y, over_x, to_x, to_y = refs[-4:]
    width = turned.shape[0]
    rows = width // 8
    first = starts_of(place_ref, width, ((0, 0), (0, 1)), 0)
    second = starts_of(place_ref, width, ((0, 0), (1, 0)), 1)
    one = term_of(turned, right, first, rows) + from_y[0].astype(f32)
    over_y[0] = one[:rows].astype(bf16)
    to_x[0] = one[rows:].astype(bf16)
    two = term_of(turned, right, second, rows) + from_x[0].astype(f32)
    over_x[0] = two[:rows].astype(bf16)
    to_y[0] = two[rows:].astype(bf16)


def join_kernel(place_ref, over_y, over_x, from_x, from_y, kept, given):
    k = place_ref[2]
    for out, flag in ((kept, k == 0), (given, k == 1)):

        @pl.when(flag)
        def _():
            out[0] = (over_y[0].astype(f32) + from_x[0].astype(f32)).astype(bf16)

        @pl.when(jnp.logical_not(flag))
        def _():
            out[0] = (over_x[0].astype(f32) + from_y[0].astype(f32)).astype(bf16)


def per_block(array):
    return pl.BlockSpec((1,) + array.shape[1:], lambda i: (i,) + (0,) * (len(array.shape) - 1))


def entire(array):
    return pl.BlockSpec(array.shape, lambda i: (0,) * len(array.shape))


def call(kernel, inputs, outputs, scratch=(), scalars=()):
    return pl.pallas_call(
        kernel,
        out_shape=tuple(a for a, _ in outputs),
        grid=(2,),
        in_specs=[pl.BlockSpec(memory_space=pltpu.SMEM)] * len(scalars)
        + [entire(a) if whole else per_block(a) for a, whole in inputs],
        out_specs=tuple(entire(a) if whole else per_block(a) for a, whole in outputs),
        scratch_shapes=list(scratch),
        cost_estimate=pl.CostEstimate(flops=0, transcendentals=0, bytes_accessed=0),
        compiler_params=pltpu.CompilerParams(vmem_limit_bytes=48 * 1024 * 1024),
    )(*scalars, *[a for a, _ in inputs])


def shape_of(*dims, kind=bf16):
    return jax.ShapeDtypeStruct(dims, kind)


def products_away(at, left, right):
    rows, width = left[0].shape
    sent = shape_of(2, width // 4, right[0].shape[2])
    return call(
        partial(away_kernel, count=len(left)),
        [(l, True) for l in left] + [(r, False) for r in right],
        [(sent, False), (sent, False), (shape_of(width, rows * len(left)), True)],
        scalars=(at.position(),),
    )


def products_here(at, turned, right, from_y, from_x):
    part = shape_of(2, from_y.shape[1] // 2, from_y.shape[2])
    return call(
        here_kernel,
        [(from_y, False), (from_x, False), (turned, True)] + [(r, False) for r in right],
        [(part, False)] * 4,
        scalars=(at.position(),),
    )


def join_halves(at, *parts):
    return call(
        join_kernel,
        [(part, False) for part in parts],
        [(shape_of(*parts[0].shape), False)] * 2,
        scalars=(at.position(),),
    )


PLAN = {
    "A0": ("pD", "1D"),
    "A1": ("pU",),
    "A2": ("2D", "1U"),
    "A3": (),
    "A4": ("pA",),
    "A5": (),
    "A6": ("2U", "1A", "zD"),
    "A7": (),
    "B0": ("pd", "2A", "1d", "zU", "fD"),
    "B1": ("pu",),
    "B2": (),
    "B3": (),
    "B4": ("2d", "1u", "zA", "fU"),
    "C0": (),
    "C1": ("eD", "pa", "fA", "2u", "1a", "zd", "eU"),
    "C2": (),
    "C3": (),
    "C4": ("2a", "zu", "fd"),
    "C5": ("za",),
    "C6": (),
    "C7": ("fu", "ed", "fa", "eA", "ea", "eu"),
}


class Sums:
    def __init__(self, at):
        self.at = at
        self.state = {}
        self.done = {}

    def offer(self, name, left, right):
        self.state[name] = (None, (list(left), list(right)))

    def run(self, place, main):
        for step in PLAN[place]:
            kind, name = step
            if name not in self.state:
                continue
            kept, pending = self.state.pop(name)
            pending, main = lax.optimization_barrier((pending, main))
            if kind == "w":
                self.state[name] = (kept, pending)
                continue
            if self.at.ns != 2:
                self.done[name] = self.generic(*pending)
                continue
            kept, messages = getattr(self, "step_" + kind)(kept, pending)
            values, main = lax.optimization_barrier(([value for _, value in messages], main))
            if kind == "e":
                self.done[name] = values
            else:
                sent = [value if how is None else how(value) for (how, _), value in zip(messages, values)]
                self.state[name] = (kept, sent)
        return main

    def generic(self, left, right):
        at = self.at
        summed = lax.psum_scatter(
            product(left, right), "shard", scatter_dimension=1, tiled=True
        )
        half = summed.shape[1] // 2
        halves = [summed[:, :half], summed[:, half:]]
        got = at.core(jnp.where(at.k == 0, halves[1], halves[0]))
        kept = jnp.where(at.k == 0, halves[0], halves[1])
        mine = scatter_z(jnp.concatenate(at.by_k(kept, got), axis=0))
        mine = (mine.astype(f32) + at.swap_x(mine).astype(f32)).astype(bf16)
        return jnp.concatenate(at.by_k(mine, at.core(mine)), axis=0)

    def step_p(self, _, pending):
        left, right = pending
        to_y, to_x, turned = products_away(self.at, left, right)
        return (right, turned), [(None, to_y), (None, to_x)]

    def step_1(self, kept, pending):
        to_y, to_x = pending
        return kept, [(self.at.swap_y, to_y), (self.at.swap_x, to_x)]

    def step_2(self, kept, pending):
        right, turned = kept
        over_y, over_x, to_x, to_y = products_here(self.at, turned, right, *pending)
        return (over_y, over_x), [(self.at.swap_x, to_x), (self.at.swap_y, to_y)]

    def step_z(self, kept, pending):
        kept, given = join_halves(self.at, *kept, *pending)
        everything = jnp.concatenate(self.at.by_k(kept, self.at.core(given)), axis=0)
        return None, [(scatter_z, everything)]

    def step_f(self, _, pending):
        (mine,) = pending
        return mine, [(self.at.swap_x, mine)]

    def step_e(self, mine, pending):
        (far,) = pending
        mine = jnp.stack(self.at.by_x(mine, far))
        return None, [(None, mine), (None, self.at.core(mine))]


def rows_in_place(place_ref, mine, theirs, target, b):
    k = place_ref[2]
    rows = mine.shape[1]
    for ref, member in ((mine, k), (theirs, 1 - k)):
        for x in range(2):
            start = pl.multiple_of((2 * x + member) * rows, 8)
            target[b, pl.ds(start, rows), :] = ref[x].astype(f32)


def rows_kernel(place_ref, *refs):
    for b in range(2):
        rows_in_place(place_ref, refs[2 * b], refs[2 * b + 1], refs[4], b)


def turned_kernel(place_ref, *refs):
    qkv_ref, out_ref, target = refs[4:]
    cols = out_ref.shape[1]
    for b in range(2):
        rows_in_place(place_ref, refs[2 * b], refs[2 * b + 1], target, b)
        values = target[b].T
        for number in range(3):
            qkv_ref[b, number] = values[number * cols : (number + 1) * cols]
        out_ref[b] = values[3 * cols :]


def simple_call(kernel, inputs, outputs, scratch=(), scalars=()):
    return pl.pallas_call(
        kernel,
        out_shape=tuple(outputs),
        in_specs=[pl.BlockSpec(memory_space=pltpu.SMEM)] * len(scalars)
        + [pl.BlockSpec(memory_space=pltpu.VMEM)] * len(inputs),
        out_specs=tuple(pl.BlockSpec(memory_space=pltpu.VMEM) for _ in outputs),
        scratch_shapes=list(scratch),
        cost_estimate=pl.CostEstimate(flops=0, transcendentals=0, bytes_accessed=0),
        compiler_params=pltpu.CompilerParams(vmem_limit_bytes=48 * 1024 * 1024),
    )(*scalars, *inputs)


def rows_grads(at, first, second):
    if at.ns != 2:
        return jnp.stack([first, second]).astype(f32)
    _, rows, cols = first[0].shape
    shape = shape_of(2, 4 * rows, cols, kind=f32)
    return simple_call(rows_kernel, [*first, *second], [shape], scalars=(at.position(),))[0]


def attention_grads(at, first, second, head_width):
    if at.ns != 2:
        both = jnp.swapaxes(jnp.stack([first, second]).astype(f32), 1, 2)
        qkv = both[:, : 3 * head_width].reshape(2, 3, head_width, -1)
        return jnp.swapaxes(qkv, 2, 3), both[:, 3 * head_width :]
    _, rows, cols = first[0].shape
    qkv, out = simple_call(
        turned_kernel,
        [*first, *second],
        [
            shape_of(2, 3, head_width, 4 * rows, kind=f32),
            shape_of(2, head_width, 4 * rows, kind=f32),
        ],
        scratch=[pltpu.VMEM((2, 4 * rows, cols), f32)],
        scalars=(at.position(),),
    )
    return jnp.swapaxes(qkv, 2, 3), out


def prepare_kernel(qkv_ref, out_ref, target):
    for b in range(2):
        rows = [qkv_ref[b, number].T for number in range(3)] + [out_ref[b].T]
        target[b] = jnp.concatenate(rows, axis=1)


def attention_weights(w_qkv, w_out):
    _, _, rows, cols = w_qkv.shape
    return simple_call(
        prepare_kernel, [jnp.swapaxes(w_qkv, 2, 3), w_out], [shape_of(2, rows, 4 * cols)]
    )[0]


def heads_of(values, number, head):
    start = number * 4 * HEAD_DIM + head * HEAD_DIM
    return values[:, start : start + HEAD_DIM]


def probs_of(query, key, temporal):
    scores = lax.dot_general(
        query, key, (((1,), (1,)), ((), ())), preferred_element_type=f32
    ) * (1.0 / math.sqrt(HEAD_DIM))
    if temporal:
        rows = lax.broadcasted_iota(jnp.int32, scores.shape, 0) % temporal
        cols = lax.broadcasted_iota(jnp.int32, scores.shape, 1) % temporal
        scores = jnp.where(rows == cols, scores, -jnp.inf)
    weights = jnp.exp(scores - jnp.max(scores, axis=-1, keepdims=True))
    return weights / jnp.sum(weights, axis=-1, keepdims=True)


def attend_kernel(qkv_ref, out_ref, *, temporal):
    values = qkv_ref[0]
    results = [jnp.zeros((values.shape[0], 12 * HEAD_DIM), bf16)]
    for head in range(4):
        probs = probs_of(heads_of(values, 0, head), heads_of(values, 1, head), temporal)
        results.append(
            jnp.dot(
                probs.astype(bf16), heads_of(values, 2, head), preferred_element_type=f32
            ).astype(bf16)
        )
    out_ref[0] = jnp.concatenate(results, axis=1)


def attend_back_kernel(qkv_ref, grad_ref, out_ref, *, temporal):
    factor = 1.0 / math.sqrt(HEAD_DIM)
    values = qkv_ref[0]
    grads = grad_ref[0]
    queries, keys, vals = [], [], []
    for head in range(4):
        query, key, value = (heads_of(values, number, head) for number in range(3))
        grad = heads_of(grads, 3, head)
        probs = probs_of(query, key, temporal)
        vals.append(
            lax.dot_general(
                probs.astype(bf16), grad, (((0,), (0,)), ((), ())), preferred_element_type=f32
            ).astype(bf16)
        )
        grad_probs = lax.dot_general(
            grad, value, (((1,), (1,)), ((), ())), preferred_element_type=f32
        )
        inner = jnp.sum(grad_probs * probs, axis=-1, keepdims=True)
        grad_scores = (probs * (grad_probs - inner)).astype(bf16)
        queries.append(
            (jnp.dot(grad_scores, key, preferred_element_type=f32) * factor).astype(bf16)
        )
        keys.append(
            (
                lax.dot_general(
                    grad_scores, query, (((0,), (0,)), ((), ())), preferred_element_type=f32
                )
                * factor
            ).astype(bf16)
        )
    zeros = jnp.zeros((values.shape[0], 4 * HEAD_DIM), bf16)
    out_ref[0] = jnp.concatenate(queries + keys + vals + [zeros], axis=1)


def call_attention(kernel, arrays, rows, temporal):
    shape = arrays[0].shape
    spec = pl.BlockSpec((1, rows, shape[2]), lambda i, j: (i, j, 0))
    return pl.pallas_call(
        partial(kernel, temporal=temporal),
        out_shape=shape_of(*shape),
        grid=(shape[0], shape[1] // rows),
        in_specs=[spec] * len(arrays),
        out_specs=spec,
        cost_estimate=pl.CostEstimate(flops=0, transcendentals=0, bytes_accessed=0),
        compiler_params=pltpu.CompilerParams(vmem_limit_bytes=48 * 1024 * 1024),
    )(*arrays)


SLOPE = math.sqrt(2.0 / math.pi)


def gelu(u):
    return 0.5 * u * (1.0 + jnp.tanh(SLOPE * (u + 0.044715 * (u * u * u))))


def gelu_slope(u):
    t = jnp.tanh(SLOPE * (u + 0.044715 * (u * u * u)))
    inner = SLOPE * (1.0 + 3.0 * 0.044715 * (u * u))
    return 0.5 * (1.0 + t) + 0.5 * u * (1.0 - t * t) * inner


def times_of(own, other, weight):
    left = jnp.concatenate([own[...], other[...]], axis=0)
    return jnp.dot(left, weight[0], preferred_element_type=f32)


def qkv_kernel(own, other, weight, bias, out):
    out[0] = (times_of(own, other, weight) + bias[0]).astype(bf16)


def plain_kernel(own, other, weight, out):
    out[0] = times_of(own, other, weight).astype(bf16)


def up_kernel(own, other, weight, bias, up, activated):
    values = times_of(own, other, weight) + bias[0]
    up[0] = values
    activated[0] = gelu(values).astype(bf16)


def up_back_kernel(own, other, weight, up, out, sums):
    values = (gelu_slope(up[0]) * times_of(own, other, weight)).astype(bf16)
    out[0] = values
    sums[0] = jnp.sum(values.astype(f32), axis=0, keepdims=True)


def back_kernel(left, weight, own, other, total):
    term = jnp.dot(left[0], weight[0], preferred_element_type=f32)
    rows = own.shape[0]

    @pl.when(pl.program_id(0) == 0)
    def _():
        total[...] = term

    @pl.when(pl.program_id(0) == 1)
    def _():
        own[...] = total[:rows] + term[:rows]
        other[...] = (total[rows:] + term[rows:]).astype(bf16)


def times(kernel, pair, weight, extra=(), outputs=()):
    rows = 2 * pair[0].shape[0]
    cols = weight.shape[2]
    return call(
        kernel,
        [(pair[0], True), (pair[1], True), (weight, False)] + [(e, False) for e in extra],
        [(shape_of(2, rows if tall else 1, cols, kind=kind), False) for tall, kind in outputs],
    )


def times_back(at, left, weight):
    rows, width = left.shape[1] // 2, weight.shape[2]
    own, other = call(
        back_kernel,
        [(left, False), (weight, False)],
        [(shape_of(rows, width, kind=f32), True), (shape_of(rows, width), True)],
        scratch=[pltpu.VMEM((2 * rows, width), f32)],
    )
    return own, at.core(other)


def normalized(values):
    average = jnp.mean(values, axis=-1, keepdims=True)
    centered = values - average
    inverse = lax.rsqrt(jnp.mean(centered * centered, axis=-1, keepdims=True) + 1e-06)
    return centered * inverse, inverse


def norm_back(grad, normal, inverse, factor):
    dn = grad * (1.0 + factor)
    return (
        dn
        - jnp.mean(dn, axis=-1, keepdims=True)
        - normal * jnp.mean(dn * normal, axis=-1, keepdims=True)
    ) * inverse


def token_sum(values):
    return jnp.sum(values, axis=0, keepdims=True)


def mod_of(mod, number):
    return mod[number : number + 1, :]


def enter_kernel(inputs, mod, hidden):
    normal, _ = normalized(inputs[...].astype(f32))
    hidden[...] = (normal * (1.0 + mod_of(mod, 1)) + mod_of(mod, 0)).astype(bf16)


def middle_kernel(own, got, inputs, mod, bias, attn, after, hidden):
    attn_out = own[...] + got[...].astype(f32) + bias[...]
    attn[...] = attn_out
    values = inputs[...].astype(f32) + mod_of(mod, 2) * attn_out
    after[...] = values
    normal, _ = normalized(values)
    hidden[...] = (normal * (1.0 + mod_of(mod, 4)) + mod_of(mod, 3)).astype(bf16)


def leave_kernel(own, got, after, mod, bias, mlp, result):
    mlp_out = own[...] + got[...].astype(f32) + bias[...]
    mlp[...] = mlp_out
    result[...] = (after[...] + mod_of(mod, 5) * mlp_out).astype(bf16)


def enter_back_kernel(grad_y, mod, grad_mlp, sums):
    values = (mod_of(mod, 5) * grad_y[...].astype(f32)).astype(bf16)
    grad_mlp[...] = values
    sums[...] = token_sum(values.astype(f32))


def gate_kernel(grad_y, mlp, sums):
    sums[...] = token_sum(grad_y[...].astype(f32) * mlp[...])


def gate_sum(grad_y, mlp):
    return simple_call(gate_kernel, [grad_y, mlp], [shape_of(1, mlp.shape[1], kind=f32)])[0][0]


def middle_back_kernel(own, got, after, grad_y, attn, mod, grad_after, grad_attn, sums):
    grad = own[...] + got[...].astype(f32)
    normal, inverse = normalized(after[...])
    sums[0:1] = token_sum(grad)
    sums[1:2] = token_sum(grad * normal)
    total = grad_y[...].astype(f32) + norm_back(grad, normal, inverse, mod_of(mod, 4))
    grad_after[...] = total
    values = (mod_of(mod, 2) * total).astype(bf16)
    grad_attn[...] = values
    sums[2:3] = token_sum(total * attn[...])
    sums[3:4] = token_sum(values.astype(f32))


def leave_back_kernel(own, got, inputs, grad_after, mod, grad_inputs, sums):
    grad = own[...] + got[...].astype(f32)
    normal, inverse = normalized(inputs[...].astype(f32))
    sums[0:1] = token_sum(grad)
    sums[1:2] = token_sum(grad * normal)
    grad_inputs[...] = (
        grad_after[...] + norm_back(grad, normal, inverse, mod_of(mod, 1))
    ).astype(bf16)


def forward_block(
    at, inputs, mod, weights, first, bias_qkv, bias_up, b_out, b_down, temporal, steps
):
    rows, width = inputs.shape
    for _ in range(steps[0]):
        inputs = weights.step(inputs)
    wide = shape_of(rows, width, kind=f32)
    low = shape_of(rows, width)
    (hidden,) = simple_call(enter_kernel, [inputs, mod], [low])
    hidden = (hidden, at.core(hidden))
    for _ in range(steps[1]):
        hidden = weights.step(hidden)
    w_attn, w_attn_t = weights.whole[first]
    (qkv,) = times(qkv_kernel, hidden, w_attn, [bias_qkv], [(True, bf16)])
    attended = call_attention(attend_kernel, [qkv], rows, temporal)
    own, got = times_back(at, attended, w_attn_t)
    attn, after, hidden_two = simple_call(
        middle_kernel, [own, got, inputs, mod, b_out], [wide, wide, low]
    )
    hidden_two = (hidden_two, at.core(hidden_two))
    for _ in range(steps[2]):
        hidden_two = weights.step(hidden_two)
    w_up = weights.whole[first + 1][0]
    up, activated = times(up_kernel, hidden_two, w_up, [bias_up], [(True, f32), (True, bf16)])
    for _ in range(steps[3]):
        activated = weights.step(activated)

    def leave():
        own, got = times_back(at, activated, weights.whole[first + 2][1])
        return simple_call(leave_kernel, [own, got, after, mod, b_down], [wide, low])

    return leave, (inputs, hidden, qkv, attended, attn, after, hidden_two, up, activated)


def backward_block(at, grad_y, kept, mod, weights, first, temporal, sums, names, place):
    inputs, hidden, qkv, attended, attn, after, hidden_two, up, activated = kept
    rows, width = inputs.shape
    wide = shape_of(rows, width, kind=f32)
    low = shape_of(rows, width)
    grad_mlp, sums_m = simple_call(
        enter_back_kernel, [grad_y, mod], [low, shape_of(1, width, kind=f32)]
    )
    grad_mlp = (grad_mlp, at.core(grad_mlp))
    sums.offer(names[0], grad_mlp, [activated])
    grad_mlp = weights.step(sums.run(place + "0", grad_mlp))
    (w_attn, w_attn_t), (_, w_up_t), (w_down, _) = weights.whole[first : first + 3]
    grad_up, grad_b_up = times(
        up_back_kernel, grad_mlp, w_down, [up], [(True, bf16), (False, f32)]
    )
    sums.offer(names[1], hidden_two, [grad_up])
    grad_up = sums.run(place + "1", grad_up)
    own, got = times_back(at, grad_up, w_up_t)
    grad_after, grad_attn, sums_a = simple_call(
        middle_back_kernel,
        [own, got, after, grad_y, attn, mod],
        [wide, low, shape_of(4, width, kind=f32)],
    )
    grad_attn = (grad_attn, at.core(grad_attn))
    grad_attn = sums.run(place + "2", grad_attn)
    (grad_attended,) = times(plain_kernel, grad_attn, w_attn, [], [(True, bf16)])
    grad_attended = sums.run(place + "3", grad_attended)
    grad_qkv = call_attention(attend_back_kernel, [qkv, grad_attended], rows, temporal)
    sums.offer(names[2], hidden + grad_attn, [grad_qkv, attended])
    own, got = times_back(at, grad_qkv, w_attn_t)
    own = sums.run(place + "4", own)
    grad_inputs, sums_i = simple_call(
        leave_back_kernel,
        [own, got, inputs, grad_after, mod],
        [low, shape_of(2, width, kind=f32)],
    )
    grad_mod = jnp.concatenate([sums_i[0], sums_i[1], sums_a[2], sums_a[0], sums_a[1]])
    grad_b_qkv = jnp.sum(grad_qkv, axis=1, dtype=f32)
    cols = grad_b_qkv.shape[1] // 4
    grad_bias = jnp.concatenate(
        [grad_b_qkv[:, :cols], grad_b_qkv[:, 2 * cols : 3 * cols], grad_b_up[:, 0]], axis=1
    )
    return grad_inputs, grad_bias, sums_a[3], sums_m[0], grad_mod


def body(
    video, cond, w_ada, b_ada, w_qkv, b_qv, w_out, b_out, w_up, b_up, w_down, b_down, cotangent
):
    at = Place()
    width = video.shape[-1]
    own_width = w_up.shape[1]
    head_width = w_qkv.shape[3]
    silu_value, silu_back = jax.vjp(jax.nn.silu, cond.astype(f32))
    cond_act = silu_value.astype(bf16)
    if at.ns == 2:
        other = at.swap_y(cond_act)
        cond_all = jnp.concatenate(
            [jnp.where(at.s == 0, cond_act, other), jnp.where(at.s == 0, other, cond_act)], axis=0
        )
    else:
        cond_all = lax.all_gather(cond_act, "shard", axis=0, tiled=True)
    cond_rows = lax.dynamic_slice_in_dim(cond_all, at.s * own_width, own_width, axis=1)
    mod_part = jnp.einsum("cd,bdn->cbn", cond_rows, w_ada, preferred_element_type=f32)
    if at.ns == 2:
        kept = lax.dynamic_index_in_dim(mod_part, at.s, 0, False)
        mod_part = kept + at.swap_y(lax.dynamic_index_in_dim(mod_part, 1 - at.s, 0, False))
    else:
        mod_part = lax.psum_scatter(mod_part, "shard", scatter_dimension=0, tiled=True)[0]
    ada_cols = w_ada.shape[2]
    small = jnp.concatenate(
        [mod_part + b_ada, b_qv.reshape(2, -1).astype(f32), b_up.astype(f32)], axis=1
    )

    small = at.gather_small(small)
    arrays = (attention_weights(w_qkv, w_out), w_up, jnp.swapaxes(w_down, 1, 2))
    frames = lax.all_to_all(video, "tp", split_axis=1, concat_axis=2, tiled=True)
    rows = frames.size // width
    weights = Weights(at, arrays)
    small, frames = weights.step((small, frames))
    mods = jnp.moveaxis(small[:, :, :ada_cols], 0, 1).reshape(2, 6, width)
    biases = small[:, :, ada_cols:]
    biases = jnp.stack(
        [
            lax.dynamic_index_in_dim(biases, 2 * at.k, 0, False),
            lax.dynamic_index_in_dim(biases, 2 * at.k + 1, 0, False),
        ],
        axis=1,
    )
    zeros = jnp.zeros((2, 2, head_width), f32)
    bias_qkv = jnp.concatenate(
        [biases[:, :, :head_width], zeros, biases[:, :, head_width : 2 * head_width], zeros], axis=2
    )[:, :, None]
    bias_up = biases[:, :, None, 2 * head_width :]
    b_out_row, b_down_row = (v.astype(f32)[:, None] for v in (b_out, b_down))

    frames = weights.step(frames)
    inputs = frames.reshape(rows, width)
    leave, kept_one = forward_block(
        at,
        inputs,
        mods[0],
        weights,
        0,
        bias_qkv[0],
        bias_up[0],
        b_out_row[0],
        b_down_row[0],
        0,
        (0, 1, 1, 1),
    )
    mlp_one, middle = leave()
    moved = lax.all_to_all(
        middle.reshape(frames.shape), "tp", split_axis=2, concat_axis=1, tiled=True
    )
    middle = weights.step(middle)
    moved, middle = lax.optimization_barrier((moved, middle))
    moved = lax.all_to_all(moved, "ctx", split_axis=3, concat_axis=1, tiled=True)
    grid = moved.shape
    patches = grid[2] * grid[3]
    leave, kept_two = forward_block(
        at,
        moved.reshape(rows, width),
        mods[1],
        weights,
        3,
        bias_qkv[1],
        bias_up[1],
        b_out_row[1],
        b_down_row[1],
        patches,
        (1, 0, 0, 0),
    )
    sums = Sums(at)
    grad_y = cotangent.reshape(rows, width)
    grad_moved, *small_two = backward_block(
        at, grad_y, kept_two, mods[1], weights, 3, patches, sums, "DUA", "A"
    )
    mlp_two, result = leave()
    gate_two = gate_sum(grad_y, mlp_two)
    grad_moved = sums.run("A5", grad_moved)
    grad_middle = lax.all_to_all(
        grad_moved.reshape(grid), "ctx", split_axis=1, concat_axis=3, tiled=True
    )
    grad_middle = sums.run("A6", grad_middle)
    grad_middle = lax.all_to_all(grad_middle, "tp", split_axis=1, concat_axis=2, tiled=True)
    grad_middle = sums.run("A7", grad_middle)
    grad_y = grad_middle.reshape(rows, width)
    grad_frames, *small_one = backward_block(
        at, grad_y, kept_one, mods[0], weights, 0, 0, sums, "dua", "B"
    )
    gates = (gate_sum(grad_y, mlp_one), gate_two)
    grad_video = lax.all_to_all(
        grad_frames.reshape(frames.shape), "tp", split_axis=2, concat_axis=1, tiled=True
    )

    grad_bias, grad_b_out, grad_b_down, grad_mod = (
        jnp.stack([one, two]) for one, two in zip(small_one, small_two)
    )
    grad_mod = jnp.concatenate([grad_mod, jnp.stack(gates)], axis=1)
    blocks = jnp.arange(at.nt)[:, None, None]
    grad_bias = jnp.where(blocks == 2 * at.k, grad_bias[:, 0], 0.0) + jnp.where(
        blocks == 2 * at.k + 1, grad_bias[:, 1], 0.0
    )
    small = jnp.concatenate(
        [grad_bias.reshape(-1), grad_b_out.reshape(-1), grad_b_down.reshape(-1)]
    )
    small, grad_mods, grad_video = at.sum_all(
        small,
        grad_mod.reshape(-1),
        grad_video,
        sums.run,
    )
    size = grad_bias.size
    grad_bias = lax.dynamic_index_in_dim(small[:size].reshape(grad_bias.shape), at.t, 0, False)
    grad_b_out, grad_b_down = small[size:].reshape(2, 2, width)
    grad_mods = jnp.moveaxis(grad_mods.reshape(at.ns, 2, 6 * width), 0, 1)
    grad_mods = lax.dynamic_slice_in_dim(grad_mods, at.t * ada_cols, ada_cols, axis=2)
    cond_rows = cond_rows.astype(f32)
    grad_w_ada = sum(
        cond_rows[i][None, :, None] * grad_mods[:, i][:, None, :] for i in range(at.ns)
    )
    grad_b_ada = jnp.sum(grad_mods, axis=1)
    grad_act = jnp.einsum(
        "bcn,bdn->cd", grad_mods, w_ada.astype(f32), precision=highest, preferred_element_type=f32
    )
    if at.ns == 2:
        grad_act = at.sum_group(at.sum_group(grad_act, "tp", 1), "tp", 2)
        grad_act = sums.run("C5", grad_act)
        ours = lax.dynamic_slice_in_dim(grad_act, at.s, 1, axis=0)
        theirs = at.swap_y(lax.dynamic_slice_in_dim(grad_act, 1 - at.s, 1, axis=0))
        grad_act = jnp.concatenate(
            [jnp.where(at.s == 0, ours, theirs), jnp.where(at.s == 0, theirs, ours)], axis=1
        )
    else:
        grad_act = lax.psum_scatter(
            lax.dynamic_update_slice_in_dim(
                jnp.zeros((at.ns, width), f32), grad_act, at.s * own_width, axis=1
            ),
            "shard",
            scatter_dimension=0,
            tiled=True,
        )
        grad_act = lax.psum(grad_act, "tp")
    grad_act = sums.run("C6", grad_act)
    sums.run("C7", ())
    sums = sums.done
    grad_cond = silu_back(grad_act)[0]

    grad_w_qkv, grad_w_out = attention_grads(at, sums["a"], sums["A"], head_width)
    return (
        result.reshape(grid),
        grad_video.astype(f32),
        grad_cond,
        grad_w_ada,
        grad_b_ada,
        grad_w_qkv,
        grad_bias[:, : 2 * head_width].reshape(2, 2, head_width),
        grad_w_out,
        grad_b_out,
        rows_grads(at, sums["u"], sums["U"]),
        grad_bias[:, 2 * head_width :],
        jnp.swapaxes(rows_grads(at, sums["d"], sums["D"]), 1, 2),
        grad_b_down,
    )


def solution(mesh):
    in_specs = (
        P("shard", "ctx", "tp", None, None),
        P("shard", None),
        P(None, "shard", "tp"),
        P(None, "tp"),
        P(None, None, "shard", "tp"),
        P(None, None, "tp"),
        P(None, "tp", "shard"),
        P(),
        P(None, "shard", "tp"),
        P(None, "tp"),
        P(None, "tp", "shard"),
        P(),
        P("shard", None, "tp", "ctx", None),
    )
    out_specs = (
        P("shard", None, "tp", "ctx", None),
        P("shard", "ctx", "tp", None, None),
        P("shard", None),
        P(None, "shard", "tp"),
        P(None, "tp"),
        P(None, None, "shard", "tp"),
        P(None, None, "tp"),
        P(None, "tp", "shard"),
        P(),
        P(None, "shard", "tp"),
        P(None, "tp"),
        P(None, "tp", "shard"),
        P(),
    )
    return jax.shard_map(body, mesh=mesh, in_specs=in_specs, out_specs=out_specs, check_vma=False)
```
